32 devices in a mesh: grp: 2 (over x), row: 16 (over z, y, core).
Axes of the slice: x: 2, y: 2, z: 4, core: 2. Of those that a mesh axis runs over, the one named last changes fastest.
Arguments:
- positions: float32 [3, 12288], P(None, ('grp', 'row')), parts along dimension 1, may hold values from -6 to 6
- noise: float32 [3, 12288], P(None, ('grp', 'row')), parts along dimension 1, may hold values from -6 to 6
- atom_single: bfloat16 [12288, 128], P(('grp', 'row')), parts along dimension 0, may hold values from -6 to 6
- atom_token: int32 [12288], P(('grp', 'row')), parts along dimension 0, may hold values from 0 to 511, as said below
- atom_counts: int32 [32], P(('grp', 'row')), parts along dimension 0, may hold values from 192 to 384, as said below
- window_offsets: int32 [384], P(('grp', 'row')), parts along dimension 0, may hold values from -64 to -32
- atom_bias: float32 [4, 12288, 128], P(None, ('grp', 'row')), parts along dimension 1, may hold values from -4 to 302
- token_single: bfloat16 [1024, 768], P(('grp', 'row')), parts along dimension 0, may hold values from -6 to 6
- token_bias: float32 [16, 1024, 512], P(None, ('grp', 'row')), parts along dimension 1, may hold values from -9 to 302
- pair_mask: int32 [1024, 512], P(('grp', 'row')), parts along dimension 0, may hold values from 0 to 1, as said below
- w_coord: float32 [3, 128], replicated, may hold values from -3.5 to 3.5
- w_atom_qkv: bfloat16 [128, 384], replicated, may hold values from -0.5 to 0.5
- w_atom_out: bfloat16 [128, 128], replicated, may hold values from -0.5 to 0.5
- w_agg: bfloat16 [128, 768], replicated, may hold values from -0.5 to 0.5
- w_tok_qkv: bfloat16 [768, 2304], replicated, may hold values from -0.21875 to 0.21875
- w_tok_gate: bfloat16 [768, 768], replicated, may hold values from -0.21875 to 0.21875
- w_tok_out: bfloat16 [768, 768], replicated, may hold values from -0.21875 to 0.21875
- w_back: bfloat16 [768, 128], replicated, may hold values from -0.21875 to 0.21875
- w_pos: bfloat16 [3, 128], replicated, may hold values from -0.5 to 0.5
Outputs:
- denoised: float32 [3, 12288], P(None, ('grp', 'row')), parts along dimension 1
- token_out: bfloat16 [1024, 768], P(('grp', 'row')), parts along dimension 0
The draws below stay inside these ranges and needn't reach their ends.
There are 2 independent parts, one for each index of `grp`. The reference program is written for one: setup_inputs(seed, part) draws one part's arguments, and reference() takes and returns one part's arrays. A program takes and returns all parts, laid end to end along the dimension named above; an argument that names none is the same for every part. Nothing has to cross between parts.
Inputs may be any that keep to these rules, and one draw needn't show every extreme that they name: `atom_token`: slots i * 384 to (i + 1) * 384 - 1 name tokens from i * 32 - 32 // 4 to (i + 1) * 32 + 32 // 4; ids never fall along the slots. `atom_counts`: entry i is the number of live slots at the front of slots i * 384 onward; some entry equals 384. `pair_mask`: each token's own column, and the column of its index xor 1, are 1.
All inputs are finite; a program needn't handle non-finite values.
Results may differ from the reference program's by a relative error of at most 0.0075.
Values may be sent and summed in bfloat16 or wider, within the bound.
No kernel may reach another device: no remote copies, remote signals or barrier semaphores. Data moves between devices by JAX's collectives and lax.ppermute only.
A program may use at most 64 MiB of HBM per device.

```python
import jax
import jax.numpy as jnp
from jax import lax

CA = 128
AH = 4
CT = 768
TH = 16
QWIN = 32
KWIN = 128
TOKQ = 32
ACAP = 384
TOKENS = 512
ATOMS = 6144
WINS = 192
N_ROW = 16


def shared_counts(key):
    inner = jax.random.fold_in(key, 11)
    first_key, second_key = jax.random.split(inner)
    counts = jax.random.randint(first_key, (N_ROW,), ACAP // 2, ACAP + 1)
    fullest = jax.random.randint(second_key, (), 0, N_ROW)
    return jnp.where(jnp.arange(N_ROW) == fullest, ACAP, counts).astype(jnp.int32)


def draw_atom_counts(key, part):
    return shared_counts(key)


def draw_atom_token(key, part):
    counts = shared_counts(key)
    inner = jax.random.fold_in(key, 12)
    first_key, second_key, third_key = jax.random.split(inner, 3)
    margin = TOKQ // 4
    jitter = jax.random.randint(first_key, (N_ROW + 1,), -margin, margin + 1)
    bounds = jnp.arange(N_ROW + 1) * TOKQ + jitter
    bounds = bounds.at[0].set(0)
    bounds = bounds.at[N_ROW].set(TOKENS - 1)
    bounds = jnp.clip(bounds, 0, TOKENS - 1)
    lower = bounds[:-1]
    upper = bounds[1:]
    raw_ids = jax.random.randint(second_key, (N_ROW, ACAP), 0, 1 << 20)
    picked = lower[:, None] + raw_ids % (upper - lower + 1)[:, None]
    ordered = jnp.sort(picked, axis=1)
    slot_ids = jnp.arange(ACAP)
    chosen = jnp.minimum(slot_ids[None, :] * ACAP // counts[:, None], ACAP - 1)
    live_ids = jnp.take_along_axis(ordered, chosen, axis=1)
    hole_raw = jax.random.randint(third_key, (N_ROW,), 0, 1 << 20)
    hole = lower + 1 + hole_raw % jnp.maximum(upper - lower - 2, 1)
    live_ids = jnp.where(live_ids == hole[:, None], hole[:, None] + 1, live_ids)
    result = jnp.where(slot_ids[None, :] < counts[:, None], live_ids, upper[:, None])
    return result.reshape(-1).astype(jnp.int32)


def draw_atom_bias(key, part):
    inner = jax.random.fold_in(key, 21)
    first_key = jax.random.fold_in(inner, 0)
    return jnp.clip(jax.random.normal(first_key, (AH, ATOMS, KWIN)), -4.0, 4.0).astype(jnp.float32)


def draw_token_bias(key, part):
    inner = jax.random.fold_in(key, 22)
    first_key = jax.random.fold_in(inner, 0)
    return jnp.clip(3.0 * jax.random.normal(first_key, (TH, TOKENS, TOKENS)), -9.0, 9.0).astype(jnp.float32)


def draw_pair_mask(key, part):
    inner = jax.random.fold_in(key, 31)
    coins = jax.random.randint(inner, (TOKENS, TOKENS), 0, 4) != 0
    row_ids = jnp.arange(TOKENS)[:, None]
    col_ids = jnp.arange(TOKENS)[None, :]
    keep = coins | (col_ids == row_ids) | (col_ids == row_ids ^ 1)
    return keep.astype(jnp.int32)


def plant(array, own_key, smallest, largest):
    index_at = [jax.random.randint(jax.random.fold_in(own_key, axis), (), 0, length) for axis, length in enumerate(array.shape)]
    longest = array.shape.index(max(array.shape))
    beside = index_at[:longest] + [(index_at[longest] + 1) % array.shape[longest]] + index_at[longest + 1:]
    return array.at[tuple(index_at)].set(smallest).at[tuple(beside)].set(largest)


def steps_of(own_key, dims, cuts, least, top_value):
    def one(axis_at, shards_of):
        heights = jax.random.uniform(jax.random.fold_in(jax.random.fold_in(own_key, 6), axis_at), (shards_of,), jnp.float32, least / len(cuts), top_value / len(cuts))
        return jnp.repeat(jnp.exp(heights), dims[axis_at] // shards_of).reshape((-1,) + (1,) * (len(dims) - axis_at - 1))

    factor_of = one(*cuts[0])
    for cut in cuts[1:]:
        factor_of = factor_of * one(*cut)
    return factor_of


def bell_draw(rng, extent, deviation, reach, cuts=(), kind=jnp.bfloat16):
    loudness = steps_of(rng, extent, cuts, -0.22, 0.18) if cuts else 1.0
    values = jax.random.normal(rng, extent, jnp.float32) * deviation * loudness
    return jnp.minimum(jnp.maximum(values, -reach), reach).astype(kind)


def setup_inputs(seed: int = 0, part: int = 0) -> dict:
    seeds = jax.random.split(jax.random.key(seed), 20)
    part_splits = jax.random.split(jax.random.fold_in(seeds[19], part), 20)
    return {
        "positions": bell_draw(part_splits[0], (3, ATOMS), 1.0, 6.0, ((1, 16),), jnp.float32),
        "noise": bell_draw(part_splits[1], (3, ATOMS), 1.0, 6.0, ((1, 16),), jnp.float32),
        "atom_single": bell_draw(part_splits[2], (ATOMS, CA), 1.0, 6.0, ((0, 16),)),
        "atom_token": draw_atom_token(jax.random.fold_in(jax.random.fold_in(seeds[19], part), 71), part),
        "atom_counts": draw_atom_counts(jax.random.fold_in(jax.random.fold_in(seeds[19], part), 71), part),
        "window_offsets": plant(jax.random.randint(part_splits[5], (WINS,), -(KWIN // 2), 1 - QWIN), jax.random.fold_in(part_splits[5], 1), -(KWIN // 2), (1 - QWIN) - 1).astype(jnp.int32),
        "atom_bias": draw_atom_bias(jax.random.fold_in(jax.random.fold_in(seeds[19], part), 71), part),
        "token_single": bell_draw(part_splits[7], (TOKENS, CT), 1.0, 6.0, ((0, 16),)),
        "token_bias": draw_token_bias(jax.random.fold_in(jax.random.fold_in(seeds[19], part), 71), part),
        "pair_mask": draw_pair_mask(jax.random.fold_in(jax.random.fold_in(seeds[19], part), 71), part),
        "w_coord": bell_draw(seeds[10], (3, CA), 3 ** -0.5, 3.5, (), jnp.float32),
        "w_atom_qkv": bell_draw(seeds[11], (CA, 3 * CA), CA ** -0.5, 0.5),
        "w_atom_out": bell_draw(seeds[12], (CA, CA), CA ** -0.5, 0.5),
        "w_agg": bell_draw(seeds[13], (CA, CT), CA ** -0.5, 0.5),
        "w_tok_qkv": bell_draw(seeds[14], (CT, 3 * CT), CT ** -0.5, 0.21875),
        "w_tok_gate": bell_draw(seeds[15], (CT, CT), CT ** -0.5, 0.21875),
        "w_tok_out": bell_draw(seeds[16], (CT, CT), CT ** -0.5, 0.21875),
        "w_back": bell_draw(seeds[17], (CT, CA), CT ** -0.5, 0.21875),
        "w_pos": bell_draw(seeds[18], (3, CA), CA ** -0.5, 0.5),
    }


noise_level = 2.0
input_scale = 1.0 / 5.0 ** 0.5
skip_scale = 1.0 / 5.0
output_scale = 2.0 / 5.0 ** 0.5
masked_score = -1e+30

def normalize(values):
    values = values.astype(jnp.float32)
    center = values - lax.optimization_barrier(jnp.mean(values, axis=-1, keepdims=True))
    spread = lax.optimization_barrier(jnp.mean(center * center, axis=-1, keepdims=True))
    return center * lax.rsqrt(spread + 1e-05)

def reference(positions, noise, atom_single, atom_token, atom_counts, window_offsets, atom_bias, token_single, token_bias, pair_mask, w_coord, w_atom_qkv, w_atom_out, w_agg, w_tok_qkv, w_tok_gate, w_tok_out, w_back, w_pos):
    noisy_coords = positions + noise_level * noise
    atom_start = atom_single.astype(jnp.float32) + lax.dot_general(input_scale * noisy_coords, w_coord, (((0,), (0,)), ((), ())), precision=lax.Precision.HIGHEST, preferred_element_type=jnp.float32)
    slot_ids = jnp.arange(ACAP, dtype=jnp.int32)
    living = (slot_ids[None, :] < atom_counts[:, None]).reshape(-1)
    starts = (jnp.cumsum(atom_counts) - atom_counts).astype(jnp.int32)
    total_atoms = jnp.sum(atom_counts).astype(jnp.int32)
    sequence_index = jnp.where(living, (starts[:, None] + slot_ids[None, :]).reshape(-1), ATOMS).astype(jnp.int32)
    normed = normalize(atom_start).astype(jnp.bfloat16)
    projected = jnp.dot(normed, w_atom_qkv, preferred_element_type=jnp.float32).astype(jnp.bfloat16)
    queries = projected[:, :CA]
    key_vals = projected[:, CA:]
    compact = jnp.zeros((ATOMS, 2 * CA), jnp.bfloat16).at[sequence_index].set(key_vals, mode='drop')
    windows = ATOMS // QWIN
    per_window = ACAP // QWIN
    window_ids = jnp.arange(windows, dtype=jnp.int32)
    window_first = starts[window_ids // per_window] + QWIN * (window_ids % per_window)
    key_index = window_first[:, None] + window_offsets[:, None] + jnp.arange(KWIN, dtype=jnp.int32)[None, :]
    key_usable = (key_index >= 0) & (key_index < total_atoms)
    clipped = jnp.clip(key_index, 0, ATOMS - 1).astype(jnp.int32)
    window_kv = compact[clipped]
    head_width = CA // AH
    query_heads = queries.reshape(windows, QWIN, AH, head_width).astype(jnp.float32)
    key_heads = window_kv[..., :CA].reshape(windows, KWIN, AH, head_width).astype(jnp.float32)
    value_heads = window_kv[..., CA:].reshape(windows, KWIN, AH, head_width).astype(jnp.float32)
    scores = jnp.einsum('wqhd,wkhd->hwqk', query_heads, key_heads) / head_width ** 0.5 + atom_bias.reshape(AH, windows, QWIN, KWIN)
    scores = jnp.where(key_usable[None, :, None, :], scores, masked_score)
    weights = jax.nn.softmax(scores, axis=-1).astype(jnp.bfloat16)
    attended = jnp.einsum('hwqk,wkhd->wqhd', weights.astype(jnp.float32), value_heads).reshape(ATOMS, CA)
    atom_mid = atom_start + jnp.dot(attended.astype(jnp.bfloat16), w_atom_out, preferred_element_type=jnp.float32)
    spread_rows = jnp.maximum(jnp.dot(atom_mid.astype(jnp.bfloat16), w_agg, preferred_element_type=jnp.float32), 0.0).astype(jnp.bfloat16)
    live_rows = jnp.where(living[:, None], spread_rows.astype(jnp.float32), 0.0)
    token_sum = jax.ops.segment_sum(live_rows, atom_token, num_segments=TOKENS)
    token_count = jax.ops.segment_sum(living.astype(jnp.float32), atom_token, num_segments=TOKENS)
    token_in = token_single.astype(jnp.float32) + token_sum / jnp.maximum(token_count, 1.0)[:, None]
    token_norm = normalize(token_in).astype(jnp.bfloat16)
    token_proj = jnp.dot(token_norm, w_tok_qkv, preferred_element_type=jnp.float32).astype(jnp.bfloat16)
    token_head = CT // TH
    head_query = token_proj[:, :CT].reshape(TOKENS, TH, token_head).transpose(1, 0, 2)
    head_key = token_proj[:, CT:2 * CT].reshape(TOKENS, TH, token_head).transpose(1, 0, 2)
    head_value = token_proj[:, 2 * CT:].reshape(TOKENS, TH, token_head).transpose(1, 0, 2)

    def attend(head_items):
        one_query, one_key, one_value, one_bias = head_items
        head_scores = jnp.dot(one_query, one_key.T, preferred_element_type=jnp.float32) / token_head ** 0.5 + one_bias
        head_scores = jnp.where(pair_mask == 1, head_scores, masked_score)
        head_weights = jax.nn.softmax(head_scores, axis=-1).astype(jnp.bfloat16)
        return jnp.dot(head_weights, one_value, preferred_element_type=jnp.float32)
    token_att = lax.map(attend, (head_query, head_key, head_value, token_bias)).transpose(1, 0, 2).reshape(TOKENS, CT)
    gating = jax.nn.sigmoid(jnp.dot(token_norm, w_tok_gate, preferred_element_type=jnp.float32))
    gated = (gating * token_att).astype(jnp.bfloat16)
    token_out = (token_in + jnp.dot(gated, w_tok_out, preferred_element_type=jnp.float32)).astype(jnp.bfloat16)
    back_rows = jnp.dot(token_out, w_back, preferred_element_type=jnp.float32).astype(jnp.bfloat16)
    atom_last = atom_mid + back_rows[atom_token].astype(jnp.float32)
    final_norm = normalize(atom_last).astype(jnp.bfloat16)
    update = lax.dot_general(w_pos, final_norm, (((1,), (1,)), ((), ())), preferred_element_type=jnp.float32)
    denoised = jnp.where(living[None, :], skip_scale * noisy_coords + output_scale * update, 0.0)
    return (denoised, token_out)
```

```python
import functools

import jax
import jax.numpy as jnp
from jax import lax
from jax.experimental import pallas as pl
from jax.experimental.pallas import tpu as pltpu
from jax.sharding import PartitionSpec as P

AH = 4
TH = 16
QWIN = 32
KWIN = 128
BEHIND = KWIN // 2
AHEAD = KWIN - QWIN

noise_level = 2.0
input_scale = 1.0 / 5.0**0.5
skip_scale = 1.0 / 5.0
output_scale = 2.0 / 5.0**0.5
masked_score = -1e30

F32 = jnp.float32
BF16 = jnp.bfloat16
NT = (((1,), (1,)), ((), ()))


def dot(a, b):
    return jnp.dot(a, b, preferred_element_type=F32)


def dot_nt(a, b):
    return lax.dot_general(a, b, NT, preferred_element_type=F32)


def normalize(values):
    center = values - jnp.mean(values, axis=-1, keepdims=True)
    spread = jnp.mean(center * center, axis=-1, keepdims=True)
    return center * lax.rsqrt(spread + 1e-05)


def iota(shape, dim):
    return lax.broadcasted_iota(jnp.int32, shape, dim)


VMEM = pl.BlockSpec(memory_space=pltpu.VMEM)
SMEM = pl.BlockSpec(memory_space=pltpu.SMEM)


def call(body, outs, name, specs, scratch=(), flops=10**7, limit=None):
    moved = sum(o.size * o.dtype.itemsize for o in outs)
    return pl.pallas_call(
        body,
        out_shape=tuple(outs),
        in_specs=specs,
        out_specs=tuple([VMEM] * len(outs)),
        scratch_shapes=list(scratch),
        name=name,
        cost_estimate=pl.CostEstimate(flops=flops, bytes_accessed=moved, transcendentals=0),
        compiler_params=pltpu.CompilerParams(vmem_limit_bytes=limit),
    )


def shape(dims, dtype):
    return jax.ShapeDtypeStruct(dims, dtype)


def embed_body(info, pos_ref, noise_ref, single_ref, wc_ref, wqkv_ref, start_ref, q_ref, k_ref, v_ref, pair_ref, odd_ref):
    rows, width = single_ref.shape
    scaled = input_scale * (pos_ref[...] + noise_level * noise_ref[...])
    padded = jnp.concatenate([scaled, jnp.zeros((5, rows), F32)], axis=0)
    across = jnp.transpose(padded)
    start = single_ref[...].astype(F32)
    for c in range(3):
        start = start + across[:, c : c + 1] * wc_ref[c : c + 1, :]
    start_ref[...] = start
    qkv = dot(normalize(start).astype(BF16), wqkv_ref[...]).astype(BF16)
    q_ref[...] = qkv[:, :width]
    tail = info[0] - BEHIND
    even = info[1] % 2 == 0
    for n, ref in enumerate((k_ref, v_ref)):
        at = slice(n * width, (n + 1) * width)
        ref[:rows, :] = qkv[:, (n + 1) * width : (n + 2) * width].astype(F32)
        ref[rows:, :] = jnp.zeros((AHEAD, width), F32)
        pair_ref[:, at] = ref[pl.ds(jnp.where(even, tail, 0), AHEAD), :].astype(BF16)
        odd_ref[:, at] = ref[pl.ds(jnp.where(even, 0, tail), AHEAD), :].astype(BF16)


def onehot(info, token_ref, half, block_rows):
    rows = token_ref.shape[1]
    relative = token_ref[...] - (info[1] * block_rows - half)
    living = iota((1, rows), 1) < info[0]
    hot = (iota((block_rows + 2 * half, rows), 0) == relative) & living
    return hot.astype(F32)


def atoms_body(
    half,
    info,
    offsets,
    token_ref,
    start_ref,
    q_ref,
    k_ref,
    v_ref,
    pair_ref,
    odd_ref,
    bias_ref,
    wout_ref,
    wagg_ref,
    mid_ref,
    own_ref,
    pair_out,
    odd_out,
    hot_ref,
    k_ext,
    v_ext,
    att,
):
    rows, width = start_ref.shape
    live, me, last = info[0], info[1], info[2]
    even = me % 2 == 0
    pair = pair_ref[...].astype(F32)
    odd = odd_ref[...].astype(F32)
    for n, (ref, ext) in enumerate(((k_ref, k_ext), (v_ref, v_ext))):
        at = slice(n * width, (n + 1) * width)
        ext[:BEHIND, :] = jnp.where(even, odd[:BEHIND, at], pair[:BEHIND, at])
        ext[BEHIND : BEHIND + rows + AHEAD, :] = ref[...]
        ext[pl.ds(BEHIND + live, AHEAD), :] = jnp.where(even, pair[:, at], odd[:, at])
    low = jnp.where(me > 0, 0, BEHIND)
    high = BEHIND + live + jnp.where(me < last, AHEAD, 0)
    scale = 1.0 / (width // AH) ** 0.5
    head_of_row = iota((AH * QWIN, width), 0) // QWIN
    head_of_lane = iota((AH * QWIN, width), 1) // (width // AH)
    own_head = head_of_row == head_of_lane
    lane_head = iota((QWIN, width), 1) // (width // AH)
    for m in range(rows // QWIN):
        base = BEHIND + QWIN * m + offsets[m]
        keys = k_ext[pl.ds(base, KWIN), :].astype(BF16)
        values = v_ext[pl.ds(base, KWIN), :].astype(BF16)
        window_q = q_ref[m * QWIN : (m + 1) * QWIN, :].astype(F32)
        stacked = jnp.where(own_head, jnp.concatenate([window_q] * AH, axis=0), 0.0).astype(BF16)
        bias = bias_ref[:, m * QWIN : (m + 1) * QWIN, :].reshape(AH * QWIN, KWIN)
        scores = dot_nt(stacked, keys) * scale + bias
        slots = base + iota((1, KWIN), 1)
        scores = jnp.where((slots >= low) & (slots < high), scores, masked_score)
        scores = jnp.exp(scores - jnp.max(scores, axis=-1, keepdims=True))
        weights = (scores / jnp.sum(scores, axis=-1, keepdims=True)).astype(BF16)
        mixed = dot(weights, values)
        out = mixed[:QWIN]
        for h in range(1, AH):
            out = jnp.where(lane_head == h, mixed[h * QWIN : (h + 1) * QWIN], out)
        att[m * QWIN : (m + 1) * QWIN, :] = out.astype(BF16)
    mid = start_ref[...] + dot(att[...], wout_ref[...])
    mid_ref[...] = mid
    spread = jnp.maximum(dot(mid.astype(BF16), wagg_ref[...]), 0.0).astype(BF16)
    block_rows = own_ref.shape[0]
    hot = onehot(info, token_ref, half, block_rows)
    hot_ref[...] = hot.astype(BF16)
    sums = dot(hot.astype(BF16), spread)
    counts = jnp.sum(hot, axis=1, keepdims=True)
    first = jnp.minimum(counts, 256.0)
    lane = iota((counts.shape[0], 128), 1)
    packed = jnp.where(lane == 0, first, jnp.where(lane == 1, counts - first, 0.0))
    model = wagg_ref.shape[1]
    own_ref[:, :model] = sums[half : half + block_rows]
    own_ref[:, model:] = packed[half : half + block_rows]
    lower = jnp.concatenate([sums[:half], packed[:half]], axis=1)
    upper = jnp.concatenate([sums[half + block_rows :], packed[half + block_rows :]], axis=1)
    pair_out[...] = jnp.where(even, upper, lower).astype(BF16)
    odd_out[...] = jnp.where(even, lower, upper).astype(BF16)


def token_body(info, own_ref, pair_ref, odd_ref, single_ref, in_ref, norm_ref):
    even = info[1] % 2 == 0
    model = single_ref.shape[1]
    pair = pair_ref[...].astype(F32)
    odd = odd_ref[...].astype(F32)
    both = own_ref[...] + jnp.concatenate([jnp.where(even, odd, pair), jnp.where(even, pair, odd)], axis=0)
    count = both[:, model : model + 1] + both[:, model + 1 : model + 2]
    token_in = single_ref[...].astype(F32) + both[:, :model] / jnp.maximum(count, 1.0)
    in_ref[...] = token_in
    norm_ref[...] = normalize(token_in).astype(BF16)


def query_body(norm_ref, wqkv_ref, wgate_ref, query_ref, gate_ref):
    rows, model = norm_ref.shape
    width = model // TH
    group = TH // 2
    span = group * width
    norm = norm_ref[...]
    tq = dot(norm, wqkv_ref[:, :model])
    own = iota((group * rows, span), 0) // rows == iota((group * rows, span), 1) // width
    for g in range(2):
        part = tq[:, g * span : (g + 1) * span]
        stacked = jnp.where(own, jnp.concatenate([part] * group, axis=0), 0.0).astype(BF16)
        wk = wqkv_ref[:, model + g * span : model + (g + 1) * span]
        query_ref[g * group * rows : (g + 1) * group * rows, :] = dot_nt(stacked, wk).astype(BF16)
    gate_ref[...] = jax.nn.sigmoid(dot(norm, wgate_ref[...]))


def attend_body(
    orders,
    half,
    info,
    in_ref,
    query_ref,
    gate_ref,
    all_ref,
    bias_ref,
    mask_ref,
    wqkv_ref,
    wout_ref,
    wback_ref,
    out_ref,
    back_ref,
    pair_out,
    odd_out,
    sorted_ref,
):
    rows, model = in_ref.shape
    keys = all_ref.shape[0]
    me = info[1]
    even = me % 2 == 0
    if orders is None:
        sorted_ref[...] = all_ref[...]
    else:
        for j in range(keys // rows):
            block = jnp.where(even, me ^ orders[0][j], me ^ orders[1][j])
            sorted_ref[pl.ds(pl.multiple_of(block * rows, rows), rows), :] = all_ref[j * rows : (j + 1) * rows, :]
    width = model // TH
    group = TH // 2
    span = group * width
    scale = 1.0 / width**0.5
    allowed = jnp.concatenate([mask_ref[...]] * group, axis=0) == 1
    values = sorted_ref[...]
    lane_head = iota((rows, span), 1) // width
    for g in range(2):
        at = slice(g * group * rows, (g + 1) * group * rows)
        bias = bias_ref[g * group : (g + 1) * group].reshape(group * rows, keys)
        scores = dot_nt(query_ref[at, :], values) * scale + bias
        scores = jnp.where(allowed, scores, masked_score)
        scores = jnp.exp(scores - jnp.max(scores, axis=-1, keepdims=True))
        weights = (scores / jnp.sum(scores, axis=-1, keepdims=True)).astype(BF16)
        mixed = dot(weights, values).astype(BF16)
        wide = dot(mixed, wqkv_ref[:, 2 * model + g * span : 2 * model + (g + 1) * span])
        part = wide[:rows]
        for h in range(1, group):
            part = jnp.where(lane_head == h, wide[h * rows : (h + 1) * rows], part)
        gated = (gate_ref[:, g * span : (g + 1) * span] * part).astype(BF16)
        added = dot(gated, wout_ref[g * span : (g + 1) * span, :])
        total = added if g == 0 else total + added
    token_out = (in_ref[...] + total).astype(BF16)
    out_ref[...] = token_out
    back = dot(token_out, wback_ref[...])
    back_ref[...] = back.astype(BF16)
    lower, upper = back[:half], back[rows - half :]
    pair_out[...] = jnp.where(even, upper, lower).astype(BF16)
    odd_out[...] = jnp.where(even, lower, upper).astype(BF16)


def final_body(info, hot_ref, mid_ref, back_ref, pair_ref, odd_ref, wpos_ref, pos_ref, noise_ref, out_ref):
    even = info[1] % 2 == 0
    pair = pair_ref[...].astype(F32)
    odd = odd_ref[...].astype(F32)
    near = jnp.concatenate(
        [jnp.where(even, odd, pair), back_ref[...].astype(F32), jnp.where(even, pair, odd)], axis=0
    ).astype(BF16)
    hot = jnp.transpose(hot_ref[...].astype(F32)).astype(BF16)
    last = mid_ref[...] + dot(hot, near)
    update = dot_nt(wpos_ref[...], normalize(last).astype(BF16))
    noisy = pos_ref[...] + noise_level * noise_ref[...]
    living = iota((1, noisy.shape[1]), 1) < info[0]
    out_ref[...] = jnp.where(living, skip_scale * noisy + output_scale * update, 0.0)


def exchange(pair, odd, count):
    pairs = [(i, i ^ 1) for i in range(count) if i ^ 1 < count]
    odds = [(i, i + 1) for i in range(1, count - 1, 2)]
    odds = odds + [(b, a) for a, b in odds]
    return lax.ppermute(pair, "row", pairs), lax.ppermute(odd, "row", odds)


def gather_plan(count):
    bits = [1 << b for b in range(count.bit_length() - 1)]
    if len(bits) < 2:
        return [[b, b] for b in bits[::-1]]
    even = bits[:0:-1]
    odd = even[:-2] + even[-2:][::-1] if len(even) > 1 else even
    return [[a, b] for a, b in zip(even, odd)] + [[1, 1]]


def gather(norm, count):
    if count & (count - 1) or count < 2:
        return lax.all_gather(norm, "row", axis=0, tiled=True), None
    orders = [[0], [0]]
    for step in gather_plan(count):
        perm = [(i, i ^ step[i % 2]) for i in range(count)]
        norm = jnp.concatenate([norm, lax.ppermute(norm, "row", perm)], axis=0)
        other = orders if step[0] != 1 else orders[::-1]
        orders = [orders[p] + [x ^ step[p] for x in other[p]] for p in range(2)]
    return norm, orders


def on_device(
    count,
    positions,
    noise,
    atom_single,
    atom_token,
    atom_counts,
    window_offsets,
    atom_bias,
    token_single,
    token_bias,
    pair_mask,
    w_coord,
    w_atom_qkv,
    w_atom_out,
    w_agg,
    w_tok_qkv,
    w_tok_gate,
    w_tok_out,
    w_back,
    w_pos,
):
    rows, width = atom_single.shape
    block_rows, model = token_single.shape
    half = block_rows // 2
    me = lax.axis_index("row").astype(jnp.int32)
    lane = jnp.arange(8, dtype=jnp.int32)
    info = jnp.where(lane == 0, atom_counts[0], jnp.where(lane == 1, me, count - 1))

    start, q, keys, values, pair, odd = call(
        embed_body,
        [
            shape((rows, width), F32),
            shape((rows, width), BF16),
            shape((rows + AHEAD, width), F32),
            shape((rows + AHEAD, width), F32),
            shape((AHEAD, 2 * width), BF16),
            shape((AHEAD, 2 * width), BF16),
        ],
        "embed",
        [SMEM] + [VMEM] * 5,
    )(info, positions, noise, atom_single, w_coord, w_atom_qkv)
    pair, odd = exchange(pair, odd, count)
    packed = model + 128
    mid, own, pair, odd, hot = call(
        functools.partial(atoms_body, half),
        [
            shape((rows, width), F32),
            shape((block_rows, packed), F32),
            shape((half, packed), BF16),
            shape((half, packed), BF16),
            shape((block_rows + 2 * half, rows), BF16),
        ],
        "atoms",
        [SMEM, SMEM] + [VMEM] * 10,
        [pltpu.VMEM((BEHIND + rows + AHEAD, width), F32)] * 2 + [pltpu.VMEM((rows, width), BF16)],
    )(info, window_offsets, atom_token[None], start, q, keys, values, pair, odd, atom_bias, w_atom_out, w_agg)
    pair, odd = exchange(pair, odd, count)
    token_in, norm = call(
        token_body,
        [shape((block_rows, model), F32), shape((block_rows, model), BF16)],
        "token",
        [SMEM] + [VMEM] * 4,
    )(info, own, pair, odd, token_single)
    everyone, orders = gather(norm, count)
    query, gate = call(
        query_body,
        [shape((TH * block_rows, model), BF16), shape((block_rows, model), F32)],
        "query",
        [VMEM] * 3,
    )(norm, w_tok_qkv, w_tok_gate)
    token_out, back, pair, odd = call(
        functools.partial(attend_body, orders, half),
        [
            shape((block_rows, model), BF16),
            shape((block_rows, width), BF16),
            shape((half, width), BF16),
            shape((half, width), BF16),
        ],
        "attend",
        [SMEM] + [VMEM] * 9,
        [pltpu.VMEM((count * block_rows, model), BF16)],
    )(info, token_in, query, gate, everyone, token_bias, pair_mask, w_tok_qkv, w_tok_out, w_back)
    pair, odd = exchange(pair, odd, count)
    (denoised,) = call(
        final_body,
        [shape(positions.shape, F32)],
        "final",
        [SMEM] + [VMEM] * 8,
    )(info, hot, mid, back, pair, odd, w_pos, positions, noise)
    return (denoised, token_out)


def solution(mesh):
    placed = (
        P(None, ("grp", "row")),
        P(None, ("grp", "row")),
        P(("grp", "row"), None),
        P(("grp", "row")),
        P(("grp", "row")),
        P(("grp", "row")),
        P(None, ("grp", "row"), None),
        P(("grp", "row"), None),
        P(None, ("grp", "row"), None),
        P(("grp", "row"), None),
    ) + (P(),) * 9
    return jax.shard_map(
        functools.partial(on_device, mesh.shape["row"]),
        mesh=mesh,
        in_specs=placed,
        out_specs=(P(None, ("grp", "row")), P(("grp", "row"), None)),
        check_vma=False,
    )
```

```python
import functools

import jax
import jax.numpy as jnp
from jax import lax
from jax.experimental import pallas as pl
from jax.experimental.pallas import tpu as pltpu
from jax.sharding import PartitionSpec as P

AH = 4
TH = 16
QWIN = 32
KWIN = 128
BEHIND = KWIN // 2
AHEAD = KWIN - QWIN

noise_level = 2.0
input_scale = 1.0 / 5.0**0.5
skip_scale = 1.0 / 5.0
output_scale = 2.0 / 5.0**0.5
masked_score = -1e30

F32 = jnp.float32
BF16 = jnp.bfloat16
NT = (((1,), (1,)), ((), ()))


def dot(a, b):
    return jnp.dot(a, b, preferred_element_type=F32)


def dot_nt(a, b):
    return lax.dot_general(a, b, NT, preferred_element_type=F32)


def normalize(values):
    center = values - jnp.mean(values, axis=-1, keepdims=True)
    spread = jnp.mean(center * center, axis=-1, keepdims=True)
    return center * lax.rsqrt(spread + 1e-05)


def iota(shape, dim):
    return lax.broadcasted_iota(jnp.int32, shape, dim)


VMEM = pl.BlockSpec(memory_space=pltpu.VMEM)
SMEM = pl.BlockSpec(memory_space=pltpu.SMEM)


def call(body, outs, name, specs, scratch=(), flops=10**7, limit=8):
    moved = sum(o.size * o.dtype.itemsize for o in outs)
    return pl.pallas_call(
        body,
        out_shape=tuple(outs),
        in_specs=specs,
        out_specs=tuple([VMEM] * len(outs)),
        scratch_shapes=list(scratch),
        name=name,
        cost_estimate=pl.CostEstimate(flops=flops, bytes_accessed=moved, transcendentals=0),
        compiler_params=pltpu.CompilerParams(vmem_limit_bytes=limit * 2**20),
    )


def shape(dims, dtype):
    return jax.ShapeDtypeStruct(dims, dtype)


def embed_body(info, pos_ref, noise_ref, single_ref, wc_ref, wqkv_ref, start_ref, q_ref, k_ref, v_ref, pair_ref, odd_ref):
    rows, width = single_ref.shape
    scaled = input_scale * (pos_ref[...] + noise_level * noise_ref[...])
    padded = jnp.concatenate([scaled, jnp.zeros((5, rows), F32)], axis=0)
    across = jnp.transpose(padded)
    start = single_ref[...].astype(F32)
    for c in range(3):
        start = start + across[:, c : c + 1] * wc_ref[c : c + 1, :]
    start_ref[...] = start
    qkv = dot(normalize(start).astype(BF16), wqkv_ref[...]).astype(BF16)
    q_ref[...] = qkv[:, :width]
    tail = info[0] - BEHIND
    even = info[1] % 2 == 0
    for n, ref in enumerate((k_ref, v_ref)):
        at = slice(n * width, (n + 1) * width)
        ref[:rows, :] = qkv[:, (n + 1) * width : (n + 2) * width].astype(F32)
        ref[rows:, :] = jnp.zeros((AHEAD, width), F32)
        pair_ref[:, at] = ref[pl.ds(jnp.where(even, tail, 0), AHEAD), :].astype(BF16)
        odd_ref[:, at] = ref[pl.ds(jnp.where(even, 0, tail), AHEAD), :].astype(BF16)


def onehot(info, token_ref, half, block_rows):
    rows = token_ref.shape[1]
    relative = token_ref[...] - (info[1] * block_rows - half)
    living = iota((1, rows), 1) < info[0]
    hot = (iota((block_rows + 2 * half, rows), 0) == relative) & living
    return hot.astype(F32)


def atoms_body(
    half,
    info,
    offsets,
    token_ref,
    start_ref,
    q_ref,
    k_ref,
    v_ref,
    pair_ref,
    odd_ref,
    bias_ref,
    wout_ref,
    wagg_ref,
    mid_ref,
    own_ref,
    pair_out,
    odd_out,
    hot_ref,
    k_ext,
    v_ext,
    att,
):
    rows, width = start_ref.shape
    live, me, last = info[0], info[1], info[2]
    even = me % 2 == 0
    pair = pair_ref[...].astype(F32)
    odd = odd_ref[...].astype(F32)
    for n, (ref, ext) in enumerate(((k_ref, k_ext), (v_ref, v_ext))):
        at = slice(n * width, (n + 1) * width)
        ext[:BEHIND, :] = jnp.where(even, odd[:BEHIND, at], pair[:BEHIND, at])
        ext[BEHIND : BEHIND + rows + AHEAD, :] = ref[...]
        ext[pl.ds(BEHIND + live, AHEAD), :] = jnp.where(even, pair[:, at], odd[:, at])
    low = jnp.where(me > 0, 0, BEHIND)
    high = BEHIND + live + jnp.where(me < last, AHEAD, 0)
    scale = 1.0 / (width // AH) ** 0.5
    head_of_row = iota((AH * QWIN, width), 0) // QWIN
    head_of_lane = iota((AH * QWIN, width), 1) // (width // AH)
    own_head = head_of_row == head_of_lane
    lane_head = iota((QWIN, width), 1) // (width // AH)
    for m in range(rows // QWIN):
        base = BEHIND + QWIN * m + offsets[m]
        keys = k_ext[pl.ds(base, KWIN), :].astype(BF16)
        values = v_ext[pl.ds(base, KWIN), :].astype(BF16)
        window_q = q_ref[m * QWIN : (m + 1) * QWIN, :].astype(F32)
        stacked = jnp.where(own_head, jnp.concatenate([window_q] * AH, axis=0), 0.0).astype(BF16)
        bias = bias_ref[:, m * QWIN : (m + 1) * QWIN, :].reshape(AH * QWIN, KWIN)
        scores = dot_nt(stacked, keys) * scale + bias
        slots = base + iota((1, KWIN), 1)
        scores = jnp.where((slots >= low) & (slots < high), scores, masked_score)
        scores = jnp.exp(scores - jnp.max(scores, axis=-1, keepdims=True))
        weights = (scores / jnp.sum(scores, axis=-1, keepdims=True)).astype(BF16)
        mixed = dot(weights, values)
        out = mixed[:QWIN]
        for h in range(1, AH):
            out = jnp.where(lane_head == h, mixed[h * QWIN : (h + 1) * QWIN], out)
        att[m * QWIN : (m + 1) * QWIN, :] = out.astype(BF16)
    mid = start_ref[...] + dot(att[...], wout_ref[...])
    mid_ref[...] = mid
    spread = jnp.maximum(dot(mid.astype(BF16), wagg_ref[...]), 0.0).astype(BF16)
    block_rows = own_ref.shape[0]
    hot = onehot(info, token_ref, half, block_rows)
    hot_ref[...] = hot.astype(BF16)
    sums = dot(hot.astype(BF16), spread)
    counts = jnp.sum(hot, axis=1, keepdims=True)
    first = jnp.minimum(counts, 256.0)
    lane = iota((counts.shape[0], 128), 1)
    packed = jnp.where(lane == 0, first, jnp.where(lane == 1, counts - first, 0.0))
    model = wagg_ref.shape[1]
    own_ref[:, :model] = sums[half : half + block_rows]
    own_ref[:, model:] = packed[half : half + block_rows]
    lower = jnp.concatenate([sums[:half], packed[:half]], axis=1)
    upper = jnp.concatenate([sums[half + block_rows :], packed[half + block_rows :]], axis=1)
    pair_out[...] = jnp.where(even, upper, lower).astype(BF16)
    odd_out[...] = jnp.where(even, lower, upper).astype(BF16)


def token_body(info, own_ref, pair_ref, odd_ref, single_ref, in_ref, norm_ref):
    even = info[1] % 2 == 0
    model = single_ref.shape[1]
    pair = pair_ref[...].astype(F32)
    odd = odd_ref[...].astype(F32)
    both = own_ref[...] + jnp.concatenate([jnp.where(even, odd, pair), jnp.where(even, pair, odd)], axis=0)
    count = both[:, model : model + 1] + both[:, model + 1 : model + 2]
    token_in = single_ref[...].astype(F32) + both[:, :model] / jnp.maximum(count, 1.0)
    in_ref[...] = token_in
    norm_ref[...] = normalize(token_in).astype(BF16)


def query_body(norm_ref, wqkv_ref, wgate_ref, query_ref, gate_ref):
    rows, model = norm_ref.shape
    width = model // TH
    group = TH // 2
    span = group * width
    norm = norm_ref[...]
    tq = dot(norm, wqkv_ref[:, :model])
    own = iota((group * rows, span), 0) // rows == iota((group * rows, span), 1) // width
    for g in range(2):
        part = tq[:, g * span : (g + 1) * span]
        stacked = jnp.where(own, jnp.concatenate([part] * group, axis=0), 0.0).astype(BF16)
        wk = wqkv_ref[:, model + g * span : model + (g + 1) * span]
        query_ref[g * group * rows : (g + 1) * group * rows, :] = dot_nt(stacked, wk).astype(BF16)
    gate_ref[...] = jax.nn.sigmoid(dot(norm, wgate_ref[...]))


def attend_body(
    orders,
    half,
    info,
    in_ref,
    query_ref,
    gate_ref,
    all_ref,
    bias_ref,
    mask_ref,
    wqkv_ref,
    wout_ref,
    wback_ref,
    out_ref,
    back_ref,
    pair_out,
    odd_out,
    sorted_ref,
):
    rows, model = in_ref.shape
    keys = all_ref.shape[0]
    me = info[1]
    even = me % 2 == 0
    if orders is None:
        sorted_ref[...] = all_ref[...]
    else:
        for j in range(keys // rows):
            block = jnp.where(even, me ^ orders[0][j], me ^ orders[1][j])
            sorted_ref[pl.ds(pl.multiple_of(block * rows, rows), rows), :] = all_ref[j * rows : (j + 1) * rows, :]
    width = model // TH
    group = TH // 2
    span = group * width
    scale = 1.0 / width**0.5
    allowed = jnp.concatenate([mask_ref[...]] * group, axis=0) == 1
    values = sorted_ref[...]
    lane_head = iota((rows, span), 1) // width
    for g in range(2):
        at = slice(g * group * rows, (g + 1) * group * rows)
        bias = bias_ref[g * group : (g + 1) * group].reshape(group * rows, keys)
        scores = dot_nt(query_ref[at, :], values) * scale + bias
        scores = jnp.where(allowed, scores, masked_score)
        scores = jnp.exp(scores - jnp.max(scores, axis=-1, keepdims=True))
        weights = (scores / jnp.sum(scores, axis=-1, keepdims=True)).astype(BF16)
        mixed = dot(weights, values).astype(BF16)
        wide = dot(mixed, wqkv_ref[:, 2 * model + g * span : 2 * model + (g + 1) * span])
        part = wide[:rows]
        for h in range(1, group):
            part = jnp.where(lane_head == h, wide[h * rows : (h + 1) * rows], part)
        gated = (gate_ref[:, g * span : (g + 1) * span] * part).astype(BF16)
        added = dot(gated, wout_ref[g * span : (g + 1) * span, :])
        total = added if g == 0 else total + added
    token_out = (in_ref[...] + total).astype(BF16)
    out_ref[...] = token_out
    back = dot(token_out, wback_ref[...])
    back_ref[...] = back.astype(BF16)
    lower, upper = back[:half], back[rows - half :]
    pair_out[...] = jnp.where(even, upper, lower).astype(BF16)
    odd_out[...] = jnp.where(even, lower, upper).astype(BF16)


def final_body(info, hot_ref, mid_ref, back_ref, pair_ref, odd_ref, wpos_ref, pos_ref, noise_ref, out_ref):
    even = info[1] % 2 == 0
    pair = pair_ref[...].astype(F32)
    odd = odd_ref[...].astype(F32)
    near = jnp.concatenate(
        [jnp.where(even, odd, pair), back_ref[...].astype(F32), jnp.where(even, pair, odd)], axis=0
    ).astype(BF16)
    hot = jnp.transpose(hot_ref[...].astype(F32)).astype(BF16)
    last = mid_ref[...] + dot(hot, near)
    update = dot_nt(wpos_ref[...], normalize(last).astype(BF16))
    noisy = pos_ref[...] + noise_level * noise_ref[...]
    living = iota((1, noisy.shape[1]), 1) < info[0]
    out_ref[...] = jnp.where(living, skip_scale * noisy + output_scale * update, 0.0)


def exchange(pair, odd, count):
    pairs = [(i, i ^ 1) for i in range(count) if i ^ 1 < count]
    odds = [(i, i + 1) for i in range(1, count - 1, 2)]
    odds = odds + [(b, a) for a, b in odds]
    return lax.ppermute(pair, "row", pairs), lax.ppermute(odd, "row", odds)


def gather_plan(count):
    bits = [1 << b for b in range(count.bit_length() - 1)]
    if len(bits) < 2:
        return [[b, b] for b in bits[::-1]]
    even = bits[:0:-1]
    odd = even[:-2] + even[-2:][::-1] if len(even) > 1 else even
    return [[a, b] for a, b in zip(even, odd)] + [[1, 1]]


def gather(norm, count):
    if count & (count - 1) or count < 2:
        return lax.all_gather(norm, "row", axis=0, tiled=True), None
    orders = [[0], [0]]
    for step in gather_plan(count):
        perm = [(i, i ^ step[i % 2]) for i in range(count)]
        norm = jnp.concatenate([norm, lax.ppermute(norm, "row", perm)], axis=0)
        other = orders if step[0] != 1 else orders[::-1]
        orders = [orders[p] + [x ^ step[p] for x in other[p]] for p in range(2)]
    return norm, orders


def on_device(
    count,
    positions,
    noise,
    atom_single,
    atom_token,
    atom_counts,
    window_offsets,
    atom_bias,
    token_single,
    token_bias,
    pair_mask,
    w_coord,
    w_atom_qkv,
    w_atom_out,
    w_agg,
    w_tok_qkv,
    w_tok_gate,
    w_tok_out,
    w_back,
    w_pos,
):
    rows, width = atom_single.shape
    block_rows, model = token_single.shape
    half = block_rows // 2
    me = lax.axis_index("row").astype(jnp.int32)
    lane = jnp.arange(8, dtype=jnp.int32)
    info = jnp.where(lane == 0, atom_counts[0], jnp.where(lane == 1, me, count - 1))

    start, q, keys, values, pair, odd = call(
        embed_body,
        [
            shape((rows, width), F32),
            shape((rows, width), BF16),
            shape((rows + AHEAD, width), F32),
            shape((rows + AHEAD, width), F32),
            shape((AHEAD, 2 * width), BF16),
            shape((AHEAD, 2 * width), BF16),
        ],
        "embed",
        [SMEM] + [VMEM] * 5,
    )(info, positions, noise, atom_single, w_coord, w_atom_qkv)
    pair, odd = exchange(pair, odd, count)
    packed = model + 128
    mid, own, pair, odd, hot = call(
        functools.partial(atoms_body, half),
        [
            shape((rows, width), F32),
            shape((block_rows, packed), F32),
            shape((half, packed), BF16),
            shape((half, packed), BF16),
            shape((block_rows + 2 * half, rows), BF16),
        ],
        "atoms",
        [SMEM, SMEM] + [VMEM] * 10,
        [pltpu.VMEM((BEHIND + rows + AHEAD, width), F32)] * 2 + [pltpu.VMEM((rows, width), BF16)],
    )(info, window_offsets, atom_token[None], start, q, keys, values, pair, odd, atom_bias, w_atom_out, w_agg)
    pair, odd = exchange(pair, odd, count)
    token_in, norm = call(
        token_body,
        [shape((block_rows, model), F32), shape((block_rows, model), BF16)],
        "token",
        [SMEM] + [VMEM] * 4,
    )(info, own, pair, odd, token_single)
    everyone, orders = gather(norm, count)
    query, gate = call(
        query_body,
        [shape((TH * block_rows, model), BF16), shape((block_rows, model), F32)],
        "query",
        [VMEM] * 3,
    )(norm, w_tok_qkv, w_tok_gate)
    token_out, back, pair, odd = call(
        functools.partial(attend_body, orders, half),
        [
            shape((block_rows, model), BF16),
            shape((block_rows, width), BF16),
            shape((half, width), BF16),
            shape((half, width), BF16),
        ],
        "attend",
        [SMEM] + [VMEM] * 9,
        [pltpu.VMEM((count * block_rows, model), BF16)],
    )(info, token_in, query, gate, everyone, token_bias, pair_mask, w_tok_qkv, w_tok_out, w_back)
    pair, odd = exchange(pair, odd, count)
    (denoised,) = call(
        final_body,
        [shape(positions.shape, F32)],
        "final",
        [SMEM] + [VMEM] * 8,
    )(info, hot, mid, back, pair, odd, w_pos, positions, noise)
    return (denoised, token_out)


def solution(mesh):
    placed = (
        P(None, ("grp", "row")),
        P(None, ("grp", "row")),
        P(("grp", "row"), None),
        P(("grp", "row")),
        P(("grp", "row")),
        P(("grp", "row")),
        P(None, ("grp", "row"), None),
        P(("grp", "row"), None),
        P(None, ("grp", "row"), None),
        P(("grp", "row"), None),
    ) + (P(),) * 9
    return jax.shard_map(
        functools.partial(on_device, mesh.shape["row"]),
        mesh=mesh,
        in_specs=placed,
        out_specs=(P(None, ("grp", "row")), P(("grp", "row"), None)),
        check_vma=False,
    )
```

```python
import functools

import jax
import jax.numpy as jnp
from jax import lax
from jax.experimental import pallas as pl
from jax.experimental.pallas import tpu as pltpu
from jax.sharding import PartitionSpec as P

AH = 4
TH = 16
QWIN = 32
KWIN = 128
BEHIND = KWIN // 2
AHEAD = KWIN - QWIN

noise_level = 2.0
input_scale = 1.0 / 5.0**0.5
skip_scale = 1.0 / 5.0
output_scale = 2.0 / 5.0**0.5
masked_score = -1e30

F32 = jnp.float32
BF16 = jnp.bfloat16
NT = (((1,), (1,)), ((), ()))


def dot(a, b):
    return jnp.dot(a, b, preferred_element_type=F32)


def dot_nt(a, b):
    return lax.dot_general(a, b, NT, preferred_element_type=F32)


def normalize(values):
    center = values - jnp.mean(values, axis=-1, keepdims=True)
    spread = jnp.mean(center * center, axis=-1, keepdims=True)
    return center * lax.rsqrt(spread + 1e-05)


def iota(shape, dim):
    return lax.broadcasted_iota(jnp.int32, shape, dim)


VMEM = pl.BlockSpec(memory_space=pltpu.VMEM)
SMEM = pl.BlockSpec(memory_space=pltpu.SMEM)
HBM = pl.BlockSpec(memory_space=pltpu.HBM)


def call(body, outs, name, specs, scratch=(), flops=10**7, limit=8, out_specs=None):
    moved = sum(o.size * o.dtype.itemsize for o in outs)
    return pl.pallas_call(
        body,
        out_shape=tuple(outs),
        in_specs=specs,
        out_specs=tuple(out_specs or [VMEM] * len(outs)),
        scratch_shapes=list(scratch),
        name=name,
        cost_estimate=pl.CostEstimate(flops=flops, bytes_accessed=moved, transcendentals=0),
        compiler_params=pltpu.CompilerParams(vmem_limit_bytes=limit * 2**20),
    )


def shape(dims, dtype):
    return jax.ShapeDtypeStruct(dims, dtype)


def fetch(sems, *moves):
    copies = [pltpu.make_async_copy(src, dst, sems.at[n]) for n, (src, dst) in enumerate(moves)]
    for copy in copies:
        copy.start()
    return copies


def embed_body(
    counts_hbm,
    pos_hbm,
    noise_hbm,
    single_hbm,
    wc_hbm,
    wqkv_hbm,
    info_ref,
    start_ref,
    q_ref,
    k_ref,
    v_ref,
    pair_ref,
    odd_ref,
    counts_ref,
    pos_ref,
    noise_ref,
    single_ref,
    wc_ref,
    wqkv_ref,
    sems,
):
    copies = fetch(
        sems,
        (pos_hbm, pos_ref),
        (noise_hbm, noise_ref),
        (wc_hbm, wc_ref),
        (single_hbm, single_ref),
        (wqkv_hbm, wqkv_ref),
        (counts_hbm, counts_ref),
    )
    rows, width = single_ref.shape
    for ref in (k_ref, v_ref):
        ref[rows:, :] = jnp.zeros((AHEAD, width), F32)
    for copy in copies[:3]:
        copy.wait()
    scaled = input_scale * (pos_ref[...] + noise_level * noise_ref[...])
    padded = jnp.concatenate([scaled, jnp.zeros((5, rows), F32)], axis=0)
    across = jnp.transpose(padded)
    copies[3].wait()
    start = single_ref[...].astype(F32)
    for c in range(3):
        start = start + across[:, c : c + 1] * wc_ref[c : c + 1, :]
    start_ref[...] = start
    normed = normalize(start).astype(BF16)
    copies[4].wait()
    qkv = dot(normed, wqkv_ref[...]).astype(BF16)
    q_ref[...] = qkv[:, :width]
    copies[5].wait()
    live = counts_ref[0]
    me = lax.axis_index("row")
    info_ref[0] = live
    info_ref[1] = me
    info_ref[2] = lax.axis_size("row") - 1
    tail = live - BEHIND
    even = me % 2 == 0
    for n, ref in enumerate((k_ref, v_ref)):
        at = slice(n * width, (n + 1) * width)
        ref[:rows, :] = qkv[:, (n + 1) * width : (n + 2) * width].astype(F32)
        pair_ref[:, at] = ref[pl.ds(jnp.where(even, tail, 0), AHEAD), :].astype(BF16)
        odd_ref[:, at] = ref[pl.ds(jnp.where(even, 0, tail), AHEAD), :].astype(BF16)


def one_window(queries, keys, values, bias, allowed):
    width = queries.shape[1]
    depth = width // AH
    rows = AH * QWIN
    own_head = iota((rows, width), 0) // QWIN == iota((rows, width), 1) // depth
    stacked = jnp.where(own_head, jnp.concatenate([queries] * AH, axis=0), 0.0).astype(BF16)
    scores = dot_nt(stacked, keys.astype(BF16)) * (1.0 / depth**0.5) + bias
    if allowed is not None:
        scores = jnp.where(allowed, scores, masked_score)
    scores = jnp.exp(scores - jnp.max(scores, axis=-1, keepdims=True))
    weights = (scores / jnp.sum(scores, axis=-1, keepdims=True)).astype(BF16)
    mixed = dot(weights, values.astype(BF16))
    lane_head = iota((QWIN, width), 1) // depth
    out = mixed[:QWIN]
    for h in range(1, AH):
        out = jnp.where(lane_head == h, mixed[h * QWIN : (h + 1) * QWIN], out)
    return out.astype(BF16)


def local_body(
    offsets_hbm,
    q_ref,
    k_ref,
    v_ref,
    bias_hbm,
    wout_hbm,
    wagg_hbm,
    offsets_ref,
    bias_ref,
    wout_ref,
    wagg_ref,
    att_ref,
    sems,
):
    copies = fetch(
        sems, (offsets_hbm, offsets_ref), (bias_hbm, bias_ref), (wout_hbm, wout_ref), (wagg_hbm, wagg_ref)
    )
    rows, width = q_ref.shape
    windows = rows // QWIN
    skip = BEHIND // QWIN
    stop = windows - (AHEAD - QWIN) // QWIN
    for part in (slice(0, skip * QWIN), slice(stop * QWIN, rows)):
        att_ref[part, :] = jnp.zeros((part.stop - part.start, width), BF16)
    copies[0].wait()
    copies[1].wait()
    for m in range(skip, stop):
        at = slice(m * QWIN, (m + 1) * QWIN)
        base = m * QWIN + offsets_ref[m]
        bias = bias_ref[:, at, :].reshape(AH * QWIN, KWIN)
        att_ref[at, :] = one_window(
            q_ref[at, :].astype(F32), k_ref[pl.ds(base, KWIN), :], v_ref[pl.ds(base, KWIN), :], bias, None
        )
    copies[2].wait()
    copies[3].wait()


def onehot(info, token_ref, half, block_rows):
    rows = token_ref.shape[1]
    relative = token_ref[...] - (info[1] * block_rows - half)
    living = iota((1, rows), 1) < info[0]
    hot = (iota((block_rows + 2 * half, rows), 0) == relative) & living
    return hot.astype(F32)


def atoms_body(
    half,
    info,
    offsets,
    token_ref,
    start_ref,
    q_ref,
    k_ref,
    v_ref,
    pair_ref,
    odd_ref,
    att_ref,
    bias_ref,
    wout_ref,
    wagg_ref,
    mid_ref,
    own_ref,
    pair_out,
    odd_out,
    hot_ref,
    k_ext,
    v_ext,
    att,
):
    rows, width = start_ref.shape
    live, me, last = info[0], info[1], info[2]
    even = me % 2 == 0
    pair = pair_ref[...].astype(F32)
    odd = odd_ref[...].astype(F32)
    for n, (ref, ext) in enumerate(((k_ref, k_ext), (v_ref, v_ext))):
        at = slice(n * width, (n + 1) * width)
        ext[:BEHIND, :] = jnp.where(even, odd[:BEHIND, at], pair[:BEHIND, at])
        ext[BEHIND : BEHIND + rows + AHEAD, :] = ref[...]
        ext[pl.ds(BEHIND + live, AHEAD), :] = jnp.where(even, pair[:, at], odd[:, at])
    low = jnp.where(me > 0, 0, BEHIND)
    high = BEHIND + live + jnp.where(me < last, AHEAD, 0)
    att[...] = att_ref[...]
    windows = rows // QWIN
    tails = AHEAD // QWIN
    first = jnp.minimum((live - BEHIND) // QWIN, windows - tails)
    for m in list(range(BEHIND // QWIN)) + [first + n for n in range(tails)]:
        at = pl.ds(pl.multiple_of(m * QWIN, QWIN), QWIN)
        base = BEHIND + QWIN * m + offsets[m]
        slots = base + iota((1, KWIN), 1)
        bias = bias_ref[:, at, :].reshape(AH * QWIN, KWIN)
        att[at, :] = one_window(
            q_ref[at, :].astype(F32),
            k_ext[pl.ds(base, KWIN), :],
            v_ext[pl.ds(base, KWIN), :],
            bias,
            (slots >= low) & (slots < high),
        )
    mid = start_ref[...] + dot(att[...], wout_ref[...])
    mid_ref[...] = mid
    spread = jnp.maximum(dot(mid.astype(BF16), wagg_ref[...]), 0.0).astype(BF16)
    block_rows = own_ref.shape[0]
    hot = onehot(info, token_ref, half, block_rows)
    hot_ref[...] = jnp.transpose(hot).astype(BF16)
    sums = dot(hot.astype(BF16), spread)
    counts = jnp.sum(hot, axis=1, keepdims=True)
    first = jnp.minimum(counts, 256.0)
    lane = iota((counts.shape[0], 128), 1)
    packed = jnp.where(lane == 0, first, jnp.where(lane == 1, counts - first, 0.0))
    model = wagg_ref.shape[1]
    own_ref[:, :model] = sums[half : half + block_rows]
    own_ref[:, model:] = packed[half : half + block_rows]
    lower = jnp.concatenate([sums[:half], packed[:half]], axis=1)
    upper = jnp.concatenate([sums[half + block_rows :], packed[half + block_rows :]], axis=1)
    pair_out[...] = jnp.where(even, upper, lower).astype(BF16)
    odd_out[...] = jnp.where(even, lower, upper).astype(BF16)


def token_body(info, own_ref, pair_ref, odd_ref, single_ref, in_ref, norm_ref):
    even = info[1] % 2 == 0
    model = single_ref.shape[1]
    pair = pair_ref[...].astype(F32)
    odd = odd_ref[...].astype(F32)
    lower = jnp.where(info[1] > 0, jnp.where(even, odd, pair), 0.0)
    upper = jnp.where(info[1] < info[2], jnp.where(even, pair, odd), 0.0)
    both = own_ref[...] + jnp.concatenate([lower, upper], axis=0)
    count = both[:, model : model + 1] + both[:, model + 1 : model + 2]
    token_in = single_ref[...].astype(F32) + both[:, :model] / jnp.maximum(count, 1.0)
    in_ref[...] = token_in
    norm_ref[...] = normalize(token_in).astype(BF16)


def query_body(norm_ref, wqkv_hbm, wgate_hbm, query_ref, gate_ref, wq_ref, wk_ref, wgate_ref, sems):
    rows, model = norm_ref.shape
    copies = fetch(
        sems,
        (wqkv_hbm.at[:, :model], wq_ref),
        (wqkv_hbm.at[:, model : 2 * model], wk_ref),
        (wgate_hbm, wgate_ref),
    )
    width = model // TH
    group = TH // 2
    span = group * width
    norm = norm_ref[...]
    own = iota((group * rows, span), 0) // rows == iota((group * rows, span), 1) // width
    copies[0].wait()
    tq = dot(norm, wq_ref[...])
    copies[1].wait()
    for g in range(2):
        part = tq[:, g * span : (g + 1) * span]
        stacked = jnp.where(own, jnp.concatenate([part] * group, axis=0), 0.0).astype(BF16)
        wk = wk_ref[:, g * span : (g + 1) * span]
        query_ref[g * group * rows : (g + 1) * group * rows, :] = dot_nt(stacked, wk).astype(BF16)
    copies[2].wait()
    gate_ref[...] = jax.nn.sigmoid(dot(norm, wgate_ref[...]))


def stage_body(
    after,
    bias_hbm,
    mask_hbm,
    wqkv_hbm,
    wout_hbm,
    wback_hbm,
    bias_ref,
    wv_ref,
    wout_ref,
    wback_ref,
    mask_ref,
    sems,
):
    model = wout_hbm.shape[0]
    copies = fetch(
        sems,
        (mask_hbm, mask_ref),
        (bias_hbm, bias_ref),
        (wqkv_hbm.at[:, 2 * model :], wv_ref),
        (wout_hbm, wout_ref),
        (wback_hbm, wback_ref),
    )
    copies[0].wait()
    copies[1].wait()
    allowed = mask_ref[...] == 1
    for h in range(TH):
        bias_ref[h] = jnp.where(allowed, bias_ref[h], masked_score)
    for copy in copies[2:]:
        copy.wait()


def attend_body(
    orders,
    half,
    info,
    in_ref,
    query_ref,
    gate_ref,
    all_ref,
    bias_ref,
    wv_ref,
    wout_ref,
    wback_ref,
    out_ref,
    back_ref,
    pair_out,
    odd_out,
    sorted_ref,
):
    rows, model = in_ref.shape
    keys = all_ref.shape[0]
    me = info[1]
    even = me % 2 == 0
    kind = (me ^ (me >> 1) ^ (me >> 2)) & 1
    if orders is None:
        sorted_ref[...] = all_ref[...]
    else:
        for j in range(keys // rows):
            block = me ^ jnp.where(kind == 0, orders[0][j], orders[1][j])
            sorted_ref[pl.ds(pl.multiple_of(block * rows, rows), rows), :] = all_ref[j * rows : (j + 1) * rows, :]
    width = model // TH
    group = TH // 2
    span = group * width
    scale = 1.0 / width**0.5
    values = sorted_ref[...]
    lane_head = iota((rows, span), 1) // width
    for g in range(2):
        at = slice(g * group * rows, (g + 1) * group * rows)
        bias = bias_ref[g * group : (g + 1) * group].reshape(group * rows, keys)
        scores = dot_nt(query_ref[at, :], values) * scale + bias
        scores = jnp.exp(scores - jnp.max(scores, axis=-1, keepdims=True))
        weights = (scores / jnp.sum(scores, axis=-1, keepdims=True)).astype(BF16)
        mixed = dot(weights, values).astype(BF16)
        wide = dot(mixed, wv_ref[:, g * span : (g + 1) * span])
        part = wide[:rows]
        for h in range(1, group):
            part = jnp.where(lane_head == h, wide[h * rows : (h + 1) * rows], part)
        gated = (gate_ref[:, g * span : (g + 1) * span] * part).astype(BF16)
        added = dot(gated, wout_ref[g * span : (g + 1) * span, :])
        total = added if g == 0 else total + added
    token_out = (in_ref[...] + total).astype(BF16)
    out_ref[...] = token_out
    back = dot(token_out, wback_ref[...])
    back_ref[...] = back.astype(BF16)
    lower, upper = back[:half], back[rows - half :]
    pair_out[...] = jnp.where(even, upper, lower).astype(BF16)
    odd_out[...] = jnp.where(even, lower, upper).astype(BF16)


def final_body(info, hot_ref, mid_ref, back_ref, pair_ref, odd_ref, wpos_ref, pos_ref, noise_ref, out_ref):
    even = info[1] % 2 == 0
    pair = pair_ref[...].astype(F32)
    odd = odd_ref[...].astype(F32)
    near = jnp.concatenate(
        [jnp.where(even, odd, pair), back_ref[...].astype(F32), jnp.where(even, pair, odd)], axis=0
    ).astype(BF16)
    last = mid_ref[...] + dot(hot_ref[...], near)
    update = dot_nt(wpos_ref[...], normalize(last).astype(BF16))
    noisy = pos_ref[...] + noise_level * noise_ref[...]
    living = iota((1, noisy.shape[1]), 1) < info[0]
    out_ref[...] = jnp.where(living, skip_scale * noisy + output_scale * update, 0.0)


def exchange(pair, odd, groups, count):
    near = [(i, i ^ 1) for i in range(count) if i ^ 1 < count]
    odds = [(i, i + 1) for i in range(1, count - 1, 2)]
    far = [(g * count + a, g * count + b) for g in range(groups) for a, b in odds + [(b, a) for a, b in odds]]
    if groups % 2 == 0 and count % 2 == 0:
        far += [(g * count + i, (g ^ 1) * count + i) for g in range(groups) for i in (0, count - 1)]
    return lax.ppermute(pair, "row", near), lax.ppermute(odd, ("grp", "row"), far)


def kind_of(i):
    return (i ^ (i >> 1) ^ (i >> 2)) & 1


def gather_plan(count):
    bits = [1 << b for b in range(count.bit_length() - 1, 0, -1) if 1 << b < count]
    steps = [[b | 1, b | 1] for b in bits]
    if len(bits) > 1:
        high, low = bits[-2] | 1, bits[-1] | 1
        steps[-2:] = [[high, low], [low, high]]
    return steps + [[1, 1]]


def gather(norm, count, between):
    orders = [[0], [0]]
    for n, step in enumerate(gather_plan(count)):
        perm = [(i, i ^ step[kind_of(i)]) for i in range(count)]
        arrived = lax.ppermute(norm, "row", perm)
        if n < len(between):
            arrived, between[n] = lax.optimization_barrier((arrived, between[n](n, norm)))
        norm = jnp.concatenate([norm, arrived], axis=0)
        orders = [orders[p] + [x ^ step[p] for x in orders[kind_of(p ^ step[p])]] for p in range(2)]
    return norm, orders, between


def on_device(
    groups,
    count,
    positions,
    noise,
    atom_single,
    atom_token,
    atom_counts,
    window_offsets,
    atom_bias,
    token_single,
    token_bias,
    pair_mask,
    w_coord,
    w_atom_qkv,
    w_atom_out,
    w_agg,
    w_tok_qkv,
    w_tok_gate,
    w_tok_out,
    w_back,
    w_pos,
):
    rows, width = atom_single.shape
    block_rows, model = token_single.shape
    half = block_rows // 2
    info_shape = shape((8,), jnp.int32)
    info, start, q, keys, values, pair, odd = call(
        embed_body,
        [
            info_shape,
            shape((rows, width), F32),
            shape((rows, width), BF16),
            shape((rows + AHEAD, width), F32),
            shape((rows + AHEAD, width), F32),
            shape((AHEAD, 2 * width), BF16),
            shape((AHEAD, 2 * width), BF16),
        ],
        "embed",
        [HBM] * 6,
        [
            pltpu.SMEM(atom_counts.shape, jnp.int32),
            pltpu.VMEM(positions.shape, F32),
            pltpu.VMEM(noise.shape, F32),
            pltpu.VMEM(atom_single.shape, BF16),
            pltpu.VMEM(w_coord.shape, F32),
            pltpu.VMEM(w_atom_qkv.shape, BF16),
            pltpu.SemaphoreType.DMA((6,)),
        ],
        out_specs=[SMEM] + [VMEM] * 6,
    )(atom_counts, positions, noise, atom_single, w_coord, w_atom_qkv)
    pair, odd = exchange(pair, odd, groups, count)
    offsets, bias, wout, wagg, att = call(
        local_body,
        [
            shape(window_offsets.shape, jnp.int32),
            shape(atom_bias.shape, F32),
            shape(w_atom_out.shape, BF16),
            shape(w_agg.shape, BF16),
            shape((rows, width), BF16),
        ],
        "local",
        [HBM] + [VMEM] * 3 + [HBM] * 3,
        [pltpu.SemaphoreType.DMA((4,))],
        flops=10**9,
        out_specs=[SMEM] + [VMEM] * 4,
    )(window_offsets, q, keys, values, atom_bias, w_atom_out, w_agg)
    packed = model + 128
    mid, own, pair, odd, hot = call(
        functools.partial(atoms_body, half),
        [
            shape((rows, width), F32),
            shape((block_rows, packed), F32),
            shape((half, packed), BF16),
            shape((half, packed), BF16),
            shape((rows, block_rows + 2 * half), BF16),
        ],
        "atoms",
        [SMEM, SMEM] + [VMEM] * 11,
        [pltpu.VMEM((BEHIND + rows + AHEAD, width), F32)] * 2 + [pltpu.VMEM((rows, width), BF16)],
    )(info, offsets, atom_token[None], start, q, keys, values, pair, odd, att, bias, wout, wagg)
    pair, odd = exchange(pair, odd, groups, count)
    token_in, norm = call(
        token_body,
        [shape((block_rows, model), F32), shape((block_rows, model), BF16)],
        "token",
        [SMEM] + [VMEM] * 4,
    )(info, own, pair, odd, token_single)

    def query(n, seen):
        return call(
            query_body,
            [shape((TH * block_rows, model), BF16), shape((block_rows, model), F32)],
            "query",
            [VMEM, HBM, HBM],
            [pltpu.VMEM((model, model), BF16)] * 3 + [pltpu.SemaphoreType.DMA((3,))],
            flops=10**9,
            limit=10,
        )(norm, w_tok_qkv, w_tok_gate)

    def stage(n, seen):
        return call(
            stage_body,
            [
                shape(token_bias.shape, F32),
                shape((model, model), BF16),
                shape((model, model), BF16),
                shape(w_back.shape, BF16),
            ],
            "stage",
            [VMEM] + [HBM] * 5,
            [pltpu.VMEM(pair_mask.shape, jnp.int32), pltpu.SemaphoreType.DMA((5,))],
            flops=10**9,
        )(seen, token_bias, pair_mask, w_tok_qkv, w_tok_out, w_back)

    if count & (count - 1) or count < 8:
        everyone, orders = lax.all_gather(norm, "row", axis=0, tiled=True), None
        between = [query(0, norm), stage(1, norm)]
    else:
        everyone, orders, between = gather(norm, count, [query, stage])
    (query_rows, gate), (bias, wv, wout, wback) = between
    token_out, back, pair, odd = call(
        functools.partial(attend_body, orders, half),
        [
            shape((block_rows, model), BF16),
            shape((block_rows, width), BF16),
            shape((half, width), BF16),
            shape((half, width), BF16),
        ],
        "attend",
        [SMEM] + [VMEM] * 8,
        [pltpu.VMEM((count * block_rows, model), BF16)],
    )(info, token_in, query_rows, gate, everyone, bias, wv, wout, wback)
    pair, odd = exchange(pair, odd, groups, count)
    (denoised,) = call(
        final_body,
        [shape(positions.shape, F32)],
        "final",
        [SMEM] + [VMEM] * 8,
    )(info, hot, mid, back, pair, odd, w_pos, positions, noise)
    return (denoised, token_out)


def solution(mesh):
    placed = (
        P(None, ("grp", "row")),
        P(None, ("grp", "row")),
        P(("grp", "row"), None),
        P(("grp", "row")),
        P(("grp", "row")),
        P(("grp", "row")),
        P(None, ("grp", "row"), None),
        P(("grp", "row"), None),
        P(None, ("grp", "row"), None),
        P(("grp", "row"), None),
    ) + (P(),) * 9
    return jax.shard_map(
        functools.partial(on_device, mesh.shape["grp"], mesh.shape["row"]),
        mesh=mesh,
        in_specs=placed,
        out_specs=(P(None, ("grp", "row")), P(("grp", "row"), None)),
        check_vma=False,
    )
```

```python
import functools

import jax
import jax.numpy as jnp
from jax import lax
from jax.experimental import pallas as pl
from jax.experimental.pallas import tpu as pltpu
from jax.sharding import PartitionSpec as P

AH = 4
TH = 16
QWIN = 32
KWIN = 128
BEHIND = KWIN // 2
AHEAD = KWIN - QWIN

noise_level = 2.0
input_scale = 1.0 / 5.0**0.5
skip_scale = 1.0 / 5.0
output_scale = 2.0 / 5.0**0.5
masked_score = -1e30

F32 = jnp.float32
BF16 = jnp.bfloat16
NT = (((1,), (1,)), ((), ()))


def dot(a, b):
    return jnp.dot(a, b, preferred_element_type=F32)


def dot_nt(a, b):
    return lax.dot_general(a, b, NT, preferred_element_type=F32)


def normalize(values):
    center = values - jnp.mean(values, axis=-1, keepdims=True)
    spread = jnp.mean(center * center, axis=-1, keepdims=True)
    return center * lax.rsqrt(spread + 1e-05)


def iota(shape, dim):
    return lax.broadcasted_iota(jnp.int32, shape, dim)


VMEM = pl.BlockSpec(memory_space=pltpu.VMEM)
SMEM = pl.BlockSpec(memory_space=pltpu.SMEM)
HBM = pl.BlockSpec(memory_space=pltpu.HBM)


def call(body, outs, name, specs, scratch=(), flops=10**7, limit=8, out_specs=None):
    moved = sum(o.size * o.dtype.itemsize for o in outs)
    held = [spec is HBM for spec in specs]
    run = pl.pallas_call(
        body,
        out_shape=tuple(outs),
        in_specs=specs,
        out_specs=tuple(out_specs or [VMEM] * len(outs)),
        scratch_shapes=list(scratch),
        name=name,
        cost_estimate=pl.CostEstimate(flops=flops, bytes_accessed=moved, transcendentals=0),
        compiler_params=pltpu.CompilerParams(vmem_limit_bytes=limit * 2**20),
    )
    return lambda *args: run(*[pltpu.with_memory_space_constraint(x, pltpu.HBM) if h and x.ndim > 1 else x for x, h in zip(args, held)])


def shape(dims, dtype):
    return jax.ShapeDtypeStruct(dims, dtype)


def fetch(sems, *moves):
    copies = [pltpu.make_async_copy(src, dst, sems.at[n]) for n, (src, dst) in enumerate(moves)]
    for copy in copies:
        copy.start()
    return copies


def embed_body(
    counts_hbm,
    pos_hbm,
    noise_hbm,
    single_hbm,
    wc_hbm,
    wqkv_hbm,
    info_ref,
    start_ref,
    q_ref,
    k_ref,
    v_ref,
    pair_ref,
    odd_ref,
    counts_ref,
    pos_ref,
    noise_ref,
    single_ref,
    wc_ref,
    wqkv_ref,
    sems,
):
    copies = fetch(
        sems,
        (pos_hbm, pos_ref),
        (noise_hbm, noise_ref),
        (wc_hbm, wc_ref),
        (single_hbm, single_ref),
        (wqkv_hbm, wqkv_ref),
        (counts_hbm, counts_ref),
    )
    rows, width = single_ref.shape
    for ref in (k_ref, v_ref):
        ref[rows:, :] = jnp.zeros((AHEAD, width), F32)
    for copy in copies[:3]:
        copy.wait()
    scaled = input_scale * (pos_ref[...] + noise_level * noise_ref[...])
    padded = jnp.concatenate([scaled, jnp.zeros((5, rows), F32)], axis=0)
    across = jnp.transpose(padded)
    copies[3].wait()
    start = single_ref[...].astype(F32)
    for c in range(3):
        start = start + across[:, c : c + 1] * wc_ref[c : c + 1, :]
    start_ref[...] = start
    normed = normalize(start).astype(BF16)
    copies[4].wait()
    qkv = dot(normed, wqkv_ref[...]).astype(BF16)
    q_ref[...] = qkv[:, :width]
    copies[5].wait()
    live = counts_ref[0]
    me = lax.axis_index("row")
    info_ref[0] = live
    info_ref[1] = me
    info_ref[2] = lax.axis_size("row") - 1
    tail = live - BEHIND
    even = me % 2 == 0
    for n, ref in enumerate((k_ref, v_ref)):
        at = slice(n * width, (n + 1) * width)
        ref[:rows, :] = qkv[:, (n + 1) * width : (n + 2) * width].astype(F32)
        pair_ref[:, at] = ref[pl.ds(jnp.where(even, tail, 0), AHEAD), :].astype(BF16)
        odd_ref[:, at] = ref[pl.ds(jnp.where(even, 0, tail), AHEAD), :].astype(BF16)


def one_window(queries, keys, values, bias, allowed):
    width = queries.shape[1]
    depth = width // AH
    rows = AH * QWIN
    own_head = iota((rows, width), 0) // QWIN == iota((rows, width), 1) // depth
    stacked = jnp.where(own_head, jnp.concatenate([queries] * AH, axis=0), 0.0).astype(BF16)
    scores = dot_nt(stacked, keys.astype(BF16)) * (1.0 / depth**0.5) + bias
    if allowed is not None:
        scores = jnp.where(allowed, scores, masked_score)
    scores = jnp.exp(scores - jnp.max(scores, axis=-1, keepdims=True))
    weights = (scores / jnp.sum(scores, axis=-1, keepdims=True)).astype(BF16)
    mixed = dot(weights, values.astype(BF16))
    lane_head = iota((QWIN, width), 1) // depth
    out = mixed[:QWIN]
    for h in range(1, AH):
        out = jnp.where(lane_head == h, mixed[h * QWIN : (h + 1) * QWIN], out)
    return out.astype(BF16)


def local_body(
    offsets_hbm,
    q_ref,
    k_ref,
    v_ref,
    bias_hbm,
    wout_hbm,
    wagg_hbm,
    offsets_ref,
    bias_ref,
    wout_ref,
    wagg_ref,
    att_ref,
    sems,
):
    copies = fetch(
        sems, (offsets_hbm, offsets_ref), (bias_hbm, bias_ref), (wout_hbm, wout_ref), (wagg_hbm, wagg_ref)
    )
    rows, width = q_ref.shape
    windows = rows // QWIN
    skip = BEHIND // QWIN
    stop = windows - (AHEAD - QWIN) // QWIN
    for part in (slice(0, skip * QWIN), slice(stop * QWIN, rows)):
        att_ref[part, :] = jnp.zeros((part.stop - part.start, width), BF16)
    copies[0].wait()
    copies[1].wait()
    for m in range(skip, stop):
        at = slice(m * QWIN, (m + 1) * QWIN)
        base = m * QWIN + offsets_ref[m]
        bias = bias_ref[:, at, :].reshape(AH * QWIN, KWIN)
        att_ref[at, :] = one_window(
            q_ref[at, :].astype(F32), k_ref[pl.ds(base, KWIN), :], v_ref[pl.ds(base, KWIN), :], bias, None
        )
    copies[2].wait()
    copies[3].wait()


def onehot(info, token_ref, half, block_rows):
    rows = token_ref.shape[1]
    relative = token_ref[...] - (info[1] * block_rows - half)
    living = iota((1, rows), 1) < info[0]
    hot = (iota((block_rows + 2 * half, rows), 0) == relative) & living
    return hot.astype(F32)


def atoms_body(
    half,
    info,
    offsets,
    token_ref,
    start_ref,
    q_ref,
    k_ref,
    v_ref,
    pair_ref,
    odd_ref,
    att_ref,
    bias_ref,
    wout_ref,
    wagg_ref,
    mid_ref,
    own_ref,
    pair_out,
    odd_out,
    hot_ref,
    k_ext,
    v_ext,
    att,
):
    rows, width = start_ref.shape
    live, me, last = info[0], info[1], info[2]
    even = me % 2 == 0
    pair = pair_ref[...].astype(F32)
    odd = odd_ref[...].astype(F32)
    for n, (ref, ext) in enumerate(((k_ref, k_ext), (v_ref, v_ext))):
        at = slice(n * width, (n + 1) * width)
        ext[:BEHIND, :] = jnp.where(even, odd[:BEHIND, at], pair[:BEHIND, at])
        ext[BEHIND : BEHIND + rows + AHEAD, :] = ref[...]
        ext[pl.ds(BEHIND + live, AHEAD), :] = jnp.where(even, pair[:, at], odd[:, at])
    low = jnp.where(me > 0, 0, BEHIND)
    high = BEHIND + live + jnp.where(me < last, AHEAD, 0)
    att[...] = att_ref[...]
    windows = rows // QWIN
    tails = AHEAD // QWIN
    first = jnp.minimum((live - BEHIND) // QWIN, windows - tails)
    for m in list(range(BEHIND // QWIN)) + [first + n for n in range(tails)]:
        at = pl.ds(pl.multiple_of(m * QWIN, QWIN), QWIN)
        base = BEHIND + QWIN * m + offsets[m]
        slots = base + iota((1, KWIN), 1)
        bias = bias_ref[:, at, :].reshape(AH * QWIN, KWIN)
        att[at, :] = one_window(
            q_ref[at, :].astype(F32),
            k_ext[pl.ds(base, KWIN), :],
            v_ext[pl.ds(base, KWIN), :],
            bias,
            (slots >= low) & (slots < high),
        )
    mid = start_ref[...] + dot(att[...], wout_ref[...])
    mid_ref[...] = mid
    spread = jnp.maximum(dot(mid.astype(BF16), wagg_ref[...]), 0.0).astype(BF16)
    block_rows = own_ref.shape[0]
    hot = onehot(info, token_ref, half, block_rows)
    hot_ref[...] = jnp.transpose(hot).astype(BF16)
    sums = dot(hot.astype(BF16), spread)
    counts = jnp.sum(hot, axis=1, keepdims=True)
    first = jnp.minimum(counts, 256.0)
    lane = iota((counts.shape[0], 128), 1)
    packed = jnp.where(lane == 0, first, jnp.where(lane == 1, counts - first, 0.0))
    model = wagg_ref.shape[1]
    own_ref[:, :model] = sums[half : half + block_rows]
    own_ref[:, model:] = packed[half : half + block_rows]
    lower = jnp.concatenate([sums[:half], packed[:half]], axis=1)
    upper = jnp.concatenate([sums[half + block_rows :], packed[half + block_rows :]], axis=1)
    pair_out[...] = jnp.where(even, upper, lower).astype(BF16)
    odd_out[...] = jnp.where(even, lower, upper).astype(BF16)


def token_body(info, own_ref, pair_ref, odd_ref, single_ref, in_ref, norm_ref):
    even = info[1] % 2 == 0
    model = single_ref.shape[1]
    pair = pair_ref[...].astype(F32)
    odd = odd_ref[...].astype(F32)
    lower = jnp.where(info[1] > 0, jnp.where(even, odd, pair), 0.0)
    upper = jnp.where(info[1] < info[2], jnp.where(even, pair, odd), 0.0)
    both = own_ref[...] + jnp.concatenate([lower, upper], axis=0)
    count = both[:, model : model + 1] + both[:, model + 1 : model + 2]
    token_in = single_ref[...].astype(F32) + both[:, :model] / jnp.maximum(count, 1.0)
    in_ref[...] = token_in
    norm_ref[...] = normalize(token_in).astype(BF16)


def query_body(norm_ref, wqkv_hbm, wgate_hbm, query_ref, gate_ref, wq_ref, wk_ref, wgate_ref, sems):
    rows, model = norm_ref.shape
    copies = fetch(
        sems,
        (wqkv_hbm.at[:, :model], wq_ref),
        (wqkv_hbm.at[:, model : 2 * model], wk_ref),
        (wgate_hbm, wgate_ref),
    )
    width = model // TH
    group = TH // 2
    span = group * width
    norm = norm_ref[...]
    own = iota((group * rows, span), 0) // rows == iota((group * rows, span), 1) // width
    copies[0].wait()
    tq = dot(norm, wq_ref[...])
    copies[1].wait()
    for g in range(2):
        part = tq[:, g * span : (g + 1) * span]
        stacked = jnp.where(own, jnp.concatenate([part] * group, axis=0), 0.0).astype(BF16)
        wk = wk_ref[:, g * span : (g + 1) * span]
        query_ref[g * group * rows : (g + 1) * group * rows, :] = dot_nt(stacked, wk).astype(BF16)
    copies[2].wait()
    gate_ref[...] = jax.nn.sigmoid(dot(norm, wgate_ref[...]))


def stage_body(
    after,
    bias_hbm,
    mask_hbm,
    wqkv_hbm,
    wout_hbm,
    wback_hbm,
    bias_ref,
    wv_ref,
    wout_ref,
    wback_ref,
    mask_ref,
    sems,
):
    model = wout_hbm.shape[0]
    copies = fetch(
        sems,
        (mask_hbm, mask_ref),
        (bias_hbm, bias_ref),
        (wqkv_hbm.at[:, 2 * model :], wv_ref),
        (wout_hbm, wout_ref),
        (wback_hbm, wback_ref),
    )
    copies[0].wait()
    copies[1].wait()
    allowed = mask_ref[...] == 1
    for h in range(TH):
        bias_ref[h] = jnp.where(allowed, bias_ref[h], masked_score)
    for copy in copies[2:]:
        copy.wait()


def attend_body(
    orders,
    half,
    info,
    in_ref,
    query_ref,
    gate_ref,
    all_ref,
    bias_ref,
    wv_ref,
    wout_ref,
    wback_ref,
    out_ref,
    back_ref,
    pair_out,
    odd_out,
    sorted_ref,
):
    rows, model = in_ref.shape
    keys = all_ref.shape[0]
    me = info[1]
    even = me % 2 == 0
    kind = (me ^ (me >> 1) ^ (me >> 2)) & 1
    if orders is None:
        sorted_ref[...] = all_ref[...]
    else:
        for j in range(keys // rows):
            block = me ^ jnp.where(kind == 0, orders[0][j], orders[1][j])
            sorted_ref[pl.ds(pl.multiple_of(block * rows, rows), rows), :] = all_ref[j * rows : (j + 1) * rows, :]
    width = model // TH
    group = TH // 2
    span = group * width
    scale = 1.0 / width**0.5
    values = sorted_ref[...]
    lane_head = iota((rows, span), 1) // width
    for g in range(2):
        at = slice(g * group * rows, (g + 1) * group * rows)
        bias = bias_ref[g * group : (g + 1) * group].reshape(group * rows, keys)
        scores = dot_nt(query_ref[at, :], values) * scale + bias
        scores = jnp.exp(scores - jnp.max(scores, axis=-1, keepdims=True))
        weights = (scores / jnp.sum(scores, axis=-1, keepdims=True)).astype(BF16)
        mixed = dot(weights, values).astype(BF16)
        wide = dot(mixed, wv_ref[:, g * span : (g + 1) * span])
        part = wide[:rows]
        for h in range(1, group):
            part = jnp.where(lane_head == h, wide[h * rows : (h + 1) * rows], part)
        gated = (gate_ref[:, g * span : (g + 1) * span] * part).astype(BF16)
        added = dot(gated, wout_ref[g * span : (g + 1) * span, :])
        total = added if g == 0 else total + added
    token_out = (in_ref[...] + total).astype(BF16)
    out_ref[...] = token_out
    back = dot(token_out, wback_ref[...])
    back_ref[...] = back.astype(BF16)
    lower, upper = back[:half], back[rows - half :]
    pair_out[...] = jnp.where(even, upper, lower).astype(BF16)
    odd_out[...] = jnp.where(even, lower, upper).astype(BF16)


def final_body(info, hot_ref, mid_ref, back_ref, pair_ref, odd_ref, wpos_ref, pos_ref, noise_ref, out_ref):
    even = info[1] % 2 == 0
    pair = pair_ref[...].astype(F32)
    odd = odd_ref[...].astype(F32)
    near = jnp.concatenate(
        [jnp.where(even, odd, pair), back_ref[...].astype(F32), jnp.where(even, pair, odd)], axis=0
    ).astype(BF16)
    last = mid_ref[...] + dot(hot_ref[...], near)
    update = dot_nt(wpos_ref[...], normalize(last).astype(BF16))
    noisy = pos_ref[...] + noise_level * noise_ref[...]
    living = iota((1, noisy.shape[1]), 1) < info[0]
    out_ref[...] = jnp.where(living, skip_scale * noisy + output_scale * update, 0.0)


def exchange(pair, odd, groups, count):
    near = [(i, i ^ 1) for i in range(count) if i ^ 1 < count]
    odds = [(i, i + 1) for i in range(1, count - 1, 2)]
    far = [(g * count + a, g * count + b) for g in range(groups) for a, b in odds + [(b, a) for a, b in odds]]
    if groups % 2 == 0 and count % 2 == 0:
        far += [(g * count + i, (g ^ 1) * count + i) for g in range(groups) for i in (0, count - 1)]
    return lax.ppermute(pair, "row", near), lax.ppermute(odd, ("grp", "row"), far)


def kind_of(i):
    return (i ^ (i >> 1) ^ (i >> 2)) & 1


def gather_plan(count):
    bits = [1 << b for b in range(count.bit_length() - 1, 0, -1) if 1 << b < count]
    steps = [[b | 1, b | 1] for b in bits]
    if len(bits) > 1:
        high, low = bits[-2] | 1, bits[-1] | 1
        steps[-2:] = [[high, low], [low, high]]
    return steps + [[1, 1]]


def gather(norm, count, between):
    orders = [[0], [0]]
    for n, step in enumerate(gather_plan(count)):
        perm = [(i, i ^ step[kind_of(i)]) for i in range(count)]
        arrived = lax.ppermute(norm, "row", perm)
        if n < len(between):
            arrived, between[n] = lax.optimization_barrier((arrived, between[n](n, norm)))
        norm = jnp.concatenate([norm, arrived], axis=0)
        orders = [orders[p] + [x ^ step[p] for x in orders[kind_of(p ^ step[p])]] for p in range(2)]
    return norm, orders, between


def on_device(
    groups,
    count,
    positions,
    noise,
    atom_single,
    atom_token,
    atom_counts,
    window_offsets,
    atom_bias,
    token_single,
    token_bias,
    pair_mask,
    w_coord,
    w_atom_qkv,
    w_atom_out,
    w_agg,
    w_tok_qkv,
    w_tok_gate,
    w_tok_out,
    w_back,
    w_pos,
):
    rows, width = atom_single.shape
    block_rows, model = token_single.shape
    half = block_rows // 2
    info_shape = shape((8,), jnp.int32)
    info, start, q, keys, values, pair, odd = call(
        embed_body,
        [
            info_shape,
            shape((rows, width), F32),
            shape((rows, width), BF16),
            shape((rows + AHEAD, width), F32),
            shape((rows + AHEAD, width), F32),
            shape((AHEAD, 2 * width), BF16),
            shape((AHEAD, 2 * width), BF16),
        ],
        "embed",
        [HBM] * 6,
        [
            pltpu.SMEM(atom_counts.shape, jnp.int32),
            pltpu.VMEM(positions.shape, F32),
            pltpu.VMEM(noise.shape, F32),
            pltpu.VMEM(atom_single.shape, BF16),
            pltpu.VMEM(w_coord.shape, F32),
            pltpu.VMEM(w_atom_qkv.shape, BF16),
            pltpu.SemaphoreType.DMA((6,)),
        ],
        out_specs=[SMEM] + [VMEM] * 6,
    )(atom_counts, positions, noise, atom_single, w_coord, w_atom_qkv)
    pair, odd = exchange(pair, odd, groups, count)
    offsets, bias, wout, wagg, att = call(
        local_body,
        [
            shape(window_offsets.shape, jnp.int32),
            shape(atom_bias.shape, F32),
            shape(w_atom_out.shape, BF16),
            shape(w_agg.shape, BF16),
            shape((rows, width), BF16),
        ],
        "local",
        [HBM] + [VMEM] * 3 + [HBM] * 3,
        [pltpu.SemaphoreType.DMA((4,))],
        flops=10**9,
        out_specs=[SMEM] + [VMEM] * 4,
    )(window_offsets, q, keys, values, atom_bias, w_atom_out, w_agg)
    packed = model + 128
    mid, own, pair, odd, hot = call(
        functools.partial(atoms_body, half),
        [
            shape((rows, width), F32),
            shape((block_rows, packed), F32),
            shape((half, packed), BF16),
            shape((half, packed), BF16),
            shape((rows, block_rows + 2 * half), BF16),
        ],
        "atoms",
        [SMEM, SMEM] + [VMEM] * 11,
        [pltpu.VMEM((BEHIND + rows + AHEAD, width), F32)] * 2 + [pltpu.VMEM((rows, width), BF16)],
    )(info, offsets, atom_token[None], start, q, keys, values, pair, odd, att, bias, wout, wagg)
    pair, odd = exchange(pair, odd, groups, count)
    token_in, norm = call(
        token_body,
        [shape((block_rows, model), F32), shape((block_rows, model), BF16)],
        "token",
        [SMEM] + [VMEM] * 4,
    )(info, own, pair, odd, token_single)

    def query(n, seen):
        return call(
            query_body,
            [shape((TH * block_rows, model), BF16), shape((block_rows, model), F32)],
            "query",
            [VMEM, HBM, HBM],
            [pltpu.VMEM((model, model), BF16)] * 3 + [pltpu.SemaphoreType.DMA((3,))],
            flops=10**9,
            limit=10,
        )(norm, w_tok_qkv, w_tok_gate)

    def stage(n, seen):
        return call(
            stage_body,
            [
                shape(token_bias.shape, F32),
                shape((model, model), BF16),
                shape((model, model), BF16),
                shape(w_back.shape, BF16),
            ],
            "stage",
            [VMEM] + [HBM] * 5,
            [pltpu.VMEM(pair_mask.shape, jnp.int32), pltpu.SemaphoreType.DMA((5,))],
            flops=10**9,
        )(seen, token_bias, pair_mask, w_tok_qkv, w_tok_out, w_back)

    if count & (count - 1) or count < 8:
        everyone, orders = lax.all_gather(norm, "row", axis=0, tiled=True), None
        between = [query(0, norm), stage(1, norm)]
    else:
        everyone, orders, between = gather(norm, count, [query, stage])
    (query_rows, gate), (bias, wv, wout, wback) = between
    token_out, back, pair, odd = call(
        functools.partial(attend_body, orders, half),
        [
            shape((block_rows, model), BF16),
            shape((block_rows, width), BF16),
            shape((half, width), BF16),
            shape((half, width), BF16),
        ],
        "attend",
        [SMEM] + [VMEM] * 8,
        [pltpu.VMEM((count * block_rows, model), BF16)],
    )(info, token_in, query_rows, gate, everyone, bias, wv, wout, wback)
    pair, odd = exchange(pair, odd, groups, count)
    (denoised,) = call(
        final_body,
        [shape(positions.shape, F32)],
        "final",
        [SMEM] + [VMEM] * 8,
    )(info, hot, mid, back, pair, odd, w_pos, positions, noise)
    return (denoised, token_out)


def solution(mesh):
    placed = (
        P(None, ("grp", "row")),
        P(None, ("grp", "row")),
        P(("grp", "row"), None),
        P(("grp", "row")),
        P(("grp", "row")),
        P(("grp", "row")),
        P(None, ("grp", "row"), None),
        P(("grp", "row"), None),
        P(None, ("grp", "row"), None),
        P(("grp", "row"), None),
    ) + (P(),) * 9
    return jax.shard_map(
        functools.partial(on_device, mesh.shape["grp"], mesh.shape["row"]),
        mesh=mesh,
        in_specs=placed,
        out_specs=(P(None, ("grp", "row")), P(("grp", "row"), None)),
        check_vma=False,
    )
```

```python
import functools

import jax
import jax.numpy as jnp
from jax import lax
from jax.experimental import pallas as pl
from jax.experimental.pallas import tpu as pltpu
from jax.sharding import PartitionSpec as P

AH = 4
TH = 16
QWIN = 32
KWIN = 128
BEHIND = KWIN // 2
AHEAD = KWIN - QWIN

noise_level = 2.0
input_scale = 1.0 / 5.0**0.5
skip_scale = 1.0 / 5.0
output_scale = 2.0 / 5.0**0.5
masked_score = -1e30

F32 = jnp.float32
BF16 = jnp.bfloat16
NT = (((1,), (1,)), ((), ()))


def dot(a, b):
    return jnp.dot(a, b, preferred_element_type=F32)


def dot_nt(a, b):
    return lax.dot_general(a, b, NT, preferred_element_type=F32)


def normalize(values):
    center = values - jnp.mean(values, axis=-1, keepdims=True)
    spread = jnp.mean(center * center, axis=-1, keepdims=True)
    return center * lax.rsqrt(spread + 1e-05)


def iota(shape, dim):
    return lax.broadcasted_iota(jnp.int32, shape, dim)


VMEM = pl.BlockSpec(memory_space=pltpu.VMEM)
SMEM = pl.BlockSpec(memory_space=pltpu.SMEM)
HBM = pl.BlockSpec(memory_space=pltpu.HBM)


def call(body, outs, name, specs, scratch=(), flops=10**7, limit=8, out_specs=None):
    moved = sum(o.size * o.dtype.itemsize for o in outs)
    held = [spec is HBM for spec in specs]
    run = pl.pallas_call(
        body,
        out_shape=tuple(outs),
        in_specs=specs,
        out_specs=tuple(out_specs or [VMEM] * len(outs)),
        scratch_shapes=list(scratch),
        name=name,
        cost_estimate=pl.CostEstimate(flops=flops, bytes_accessed=moved, transcendentals=0),
        compiler_params=pltpu.CompilerParams(vmem_limit_bytes=limit * 2**20),
    )
    return lambda *args: run(*[pltpu.with_memory_space_constraint(x, pltpu.HBM) if h and x.size > 1 else x for x, h in zip(args, held)])


def shape(dims, dtype):
    return jax.ShapeDtypeStruct(dims, dtype)


def fetch(sems, *moves):
    copies = [pltpu.make_async_copy(src, dst, sems.at[n]) for n, (src, dst) in enumerate(moves)]
    for copy in copies:
        copy.start()
    return copies


def embed_body(
    counts_hbm,
    pos_hbm,
    noise_hbm,
    single_hbm,
    wc_hbm,
    wqkv_hbm,
    offsets_hbm,
    token_hbm,
    bias_hbm,
    wout_hbm,
    wagg_hbm,
    info_ref,
    start_ref,
    q_ref,
    k_ref,
    v_ref,
    pair_ref,
    odd_ref,
    offsets_ref,
    token_ref,
    bias_ref,
    wout_ref,
    wagg_ref,
    counts_ref,
    pos_ref,
    noise_ref,
    single_ref,
    wc_ref,
    wqkv_ref,
    sems,
):
    copies = fetch(
        sems,
        (pos_hbm, pos_ref),
        (noise_hbm, noise_ref),
        (wc_hbm, wc_ref),
        (single_hbm, single_ref),
        (wqkv_hbm, wqkv_ref),
        (counts_hbm, counts_ref),
        (offsets_hbm, offsets_ref),
        (token_hbm, token_ref.at[0]),
        (bias_hbm, bias_ref),
        (wout_hbm, wout_ref),
        (wagg_hbm, wagg_ref),
    )
    rows, width = single_ref.shape
    for ref in (k_ref, v_ref):
        ref[rows:, :] = jnp.zeros((AHEAD, width), F32)
    for copy in copies[:3]:
        copy.wait()
    scaled = input_scale * (pos_ref[...] + noise_level * noise_ref[...])
    padded = jnp.concatenate([scaled, jnp.zeros((5, rows), F32)], axis=0)
    across = jnp.transpose(padded)
    copies[3].wait()
    start = single_ref[...].astype(F32)
    for c in range(3):
        start = start + across[:, c : c + 1] * wc_ref[c : c + 1, :]
    start_ref[...] = start
    normed = normalize(start).astype(BF16)
    copies[4].wait()
    qkv = dot(normed, wqkv_ref[...]).astype(BF16)
    q_ref[...] = qkv[:, :width]
    copies[5].wait()
    live = counts_ref[0, 0]
    me = lax.axis_index("row")
    info_ref[0] = live
    info_ref[1] = me
    info_ref[2] = lax.axis_size("row") - 1
    tail = live - BEHIND
    even = me % 2 == 0
    for n, ref in enumerate((k_ref, v_ref)):
        at = slice(n * width, (n + 1) * width)
        ref[:rows, :] = qkv[:, (n + 1) * width : (n + 2) * width].astype(F32)
        pair_ref[:, at] = ref[pl.ds(jnp.where(even, tail, 0), AHEAD), :].astype(BF16)
        odd_ref[:, at] = ref[pl.ds(jnp.where(even, 0, tail), AHEAD), :].astype(BF16)
    for copy in copies[6:]:
        copy.wait()


def windows_of(queries, keys, values, biases, masks):
    width = queries[0].shape[1]
    depth = width // AH
    rows = AH * QWIN
    own_head = iota((rows, width), 0) // QWIN == iota((rows, width), 1) // depth
    lane_head = iota((QWIN, width), 1) // depth
    stacked = [jnp.where(own_head, jnp.concatenate([q] * AH, axis=0), 0.0).astype(BF16) for q in queries]
    scores = [dot_nt(q, k) * (1.0 / depth**0.5) + b for q, k, b in zip(stacked, keys, biases)]
    if masks is not None:
        scores = [jnp.where(m, s, masked_score) for m, s in zip(masks, scores)]
    tops = [jnp.max(s, axis=-1, keepdims=True) for s in scores]
    scores = [jnp.exp(s - t) for s, t in zip(scores, tops)]
    shares = [1.0 / jnp.sum(s, axis=-1, keepdims=True) for s in scores]
    weights = [(s * r).astype(BF16) for s, r in zip(scores, shares)]
    mixed = [dot(w, v) for w, v in zip(weights, values)]
    outs = []
    for mix in mixed:
        out = mix[:QWIN]
        for h in range(1, AH):
            out = jnp.where(lane_head == h, mix[h * QWIN : (h + 1) * QWIN], out)
        outs.append(out.astype(BF16))
    return outs


def local_body(offsets, q_ref, k_ref, v_ref, bias_ref, att_ref):
    rows, width = q_ref.shape
    windows = rows // QWIN
    skip = BEHIND // QWIN
    stop = windows - (AHEAD - QWIN) // QWIN
    for part in (slice(0, skip * QWIN), slice(stop * QWIN, rows)):
        att_ref[part, :] = jnp.zeros((part.stop - part.start, width), BF16)
    at = [slice(m * QWIN, (m + 1) * QWIN) for m in range(skip, stop)]
    base = [m * QWIN + offsets[0, m] for m in range(skip, stop)]
    outs = windows_of(
        [q_ref[a, :].astype(F32) for a in at],
        [k_ref[pl.ds(b, KWIN), :].astype(BF16) for b in base],
        [v_ref[pl.ds(b, KWIN), :].astype(BF16) for b in base],
        [bias_ref[:, a, :].reshape(AH * QWIN, KWIN) for a in at],
        None,
    )
    for a, out in zip(at, outs):
        att_ref[a, :] = out


def atoms_body(
    half,
    info,
    offsets,
    token_ref,
    start_ref,
    q_ref,
    k_ref,
    v_ref,
    pair_ref,
    odd_ref,
    att_ref,
    bias_ref,
    wout_ref,
    wagg_ref,
    mid_ref,
    own_ref,
    pair_out,
    odd_out,
    hot_ref,
    living_ref,
    k_ext,
    v_ext,
    att,
):
    rows, width = start_ref.shape
    live, me, last = info[0], info[1], info[2]
    even = me % 2 == 0
    pair = pair_ref[...].astype(F32)
    odd = odd_ref[...].astype(F32)
    for n, (ref, ext) in enumerate(((k_ref, k_ext), (v_ref, v_ext))):
        at = slice(n * width, (n + 1) * width)
        ext[:BEHIND, :] = jnp.where(even, odd[:BEHIND, at], pair[:BEHIND, at])
        ext[BEHIND : BEHIND + rows + AHEAD, :] = ref[...]
        ext[pl.ds(BEHIND + live, AHEAD), :] = jnp.where(even, pair[:, at], odd[:, at])
    low = jnp.where(me > 0, 0, BEHIND)
    high = BEHIND + live + jnp.where(me < last, AHEAD, 0)
    att[...] = att_ref[...]
    windows = rows // QWIN
    tails = AHEAD // QWIN
    first = jnp.minimum((live - BEHIND) // QWIN, windows - tails)
    chosen = list(range(BEHIND // QWIN)) + [first + n for n in range(tails)]
    at = [pl.ds(pl.multiple_of(m * QWIN, QWIN), QWIN) for m in chosen]
    base = [BEHIND + QWIN * m + offsets[0, m] for m in chosen]
    slots = [b + iota((1, KWIN), 1) for b in base]
    outs = windows_of(
        [q_ref[a, :].astype(F32) for a in at],
        [k_ext[pl.ds(b, KWIN), :].astype(BF16) for b in base],
        [v_ext[pl.ds(b, KWIN), :].astype(BF16) for b in base],
        [bias_ref[:, a, :].reshape(AH * QWIN, KWIN) for a in at],
        [(s >= low) & (s < high) for s in slots],
    )
    for a, out in zip(at, outs):
        att[a, :] = out
    mid = start_ref[...] + dot(att[...], wout_ref[...])
    mid_ref[...] = mid
    spread = jnp.maximum(dot(mid.astype(BF16), wagg_ref[...]), 0.0).astype(BF16)
    block_rows = own_ref.shape[0]
    living = iota((1, rows), 1) < live
    living_ref[...] = living.astype(F32)
    relative = token_ref[...] - (me * block_rows - half)
    hot = ((iota((block_rows + 2 * half, rows), 0) == relative) & living).astype(F32)
    hot_ref[...] = jnp.transpose(hot).astype(BF16)
    sums = dot(hot.astype(BF16), spread)
    counts = jnp.sum(hot, axis=1, keepdims=True)
    first = jnp.minimum(counts, 256.0)
    lane = iota((counts.shape[0], 128), 1)
    packed = jnp.where(lane == 0, first, jnp.where(lane == 1, counts - first, 0.0))
    model = wagg_ref.shape[1]
    own_ref[:, :model] = sums[half : half + block_rows]
    own_ref[:, model:] = packed[half : half + block_rows]
    lower = jnp.concatenate([sums[:half], packed[:half]], axis=1)
    upper = jnp.concatenate([sums[half + block_rows :], packed[half + block_rows :]], axis=1)
    pair_out[...] = jnp.where(even, upper, lower).astype(BF16)
    odd_out[...] = jnp.where(even, lower, upper).astype(BF16)


def token_body(own_ref, pair_ref, odd_ref, single_ref, in_ref, norm_ref):
    me = lax.axis_index("row")
    even = me % 2 == 0
    model = single_ref.shape[1]
    pair = pair_ref[...].astype(F32)
    odd = odd_ref[...].astype(F32)
    lower = jnp.where(me > 0, jnp.where(even, odd, pair), 0.0)
    upper = jnp.where(me < lax.axis_size("row") - 1, jnp.where(even, pair, odd), 0.0)
    both = own_ref[...] + jnp.concatenate([lower, upper], axis=0)
    count = both[:, model : model + 1] + both[:, model + 1 : model + 2]
    token_in = single_ref[...].astype(F32) + both[:, :model] / jnp.maximum(count, 1.0)
    in_ref[...] = token_in
    norm_ref[...] = normalize(token_in).astype(BF16)


def query_body(norm_ref, wqkv_hbm, wgate_hbm, query_ref, gate_ref, wq_ref, wk_ref, wgate_ref, sems):
    rows, model = norm_ref.shape
    copies = fetch(
        sems,
        (wqkv_hbm.at[:, :model], wq_ref),
        (wqkv_hbm.at[:, model : 2 * model], wk_ref),
        (wgate_hbm, wgate_ref),
    )
    width = model // TH
    group = TH // 2
    span = group * width
    norm = norm_ref[...]
    own = iota((group * rows, span), 0) // rows == iota((group * rows, span), 1) // width
    copies[0].wait()
    tq = dot(norm, wq_ref[...])
    copies[1].wait()
    for g in range(2):
        part = tq[:, g * span : (g + 1) * span]
        stacked = jnp.where(own, jnp.concatenate([part] * group, axis=0), 0.0).astype(BF16)
        wk = wk_ref[:, g * span : (g + 1) * span]
        query_ref[g * group * rows : (g + 1) * group * rows, :] = dot_nt(stacked, wk).astype(BF16)
    copies[2].wait()
    gate_ref[...] = jax.nn.sigmoid(dot(norm, wgate_ref[...]))


def stage_body(
    after,
    bias_hbm,
    mask_hbm,
    wqkv_hbm,
    wout_hbm,
    wback_hbm,
    bias_ref,
    wv_ref,
    wout_ref,
    wback_ref,
    mask_ref,
    sems,
):
    model = wout_hbm.shape[0]
    copies = fetch(
        sems,
        (mask_hbm, mask_ref),
        (bias_hbm, bias_ref),
        (wqkv_hbm.at[:, 2 * model :], wv_ref),
        (wout_hbm, wout_ref),
        (wback_hbm, wback_ref),
    )
    copies[0].wait()
    copies[1].wait()
    allowed = mask_ref[...] == 1
    for h in range(TH):
        bias_ref[h] = jnp.where(allowed, bias_ref[h], masked_score)
    for copy in copies[2:]:
        copy.wait()


def attend_body(
    orders,
    half,
    in_ref,
    query_ref,
    gate_ref,
    all_ref,
    bias_ref,
    wv_ref,
    wout_ref,
    wback_ref,
    out_ref,
    back_ref,
    pair_out,
    odd_out,
    sorted_ref,
):
    rows, model = in_ref.shape
    keys = all_ref.shape[0]
    me = lax.axis_index("row")
    even = me % 2 == 0
    kind = (me ^ (me >> 1) ^ (me >> 2)) & 1
    if orders is None:
        sorted_ref[...] = all_ref[...]
    else:
        for j in range(keys // rows):
            block = me ^ jnp.where(kind == 0, orders[0][j], orders[1][j])
            sorted_ref[pl.ds(pl.multiple_of(block * rows, rows), rows), :] = all_ref[j * rows : (j + 1) * rows, :]
    width = model // TH
    group = TH // 2
    span = group * width
    scale = 1.0 / width**0.5
    values = sorted_ref[...]
    lane_head = iota((rows, span), 1) // width
    for g in range(2):
        at = slice(g * group * rows, (g + 1) * group * rows)
        bias = bias_ref[g * group : (g + 1) * group].reshape(group * rows, keys)
        scores = dot_nt(query_ref[at, :], values) * scale + bias
        scores = jnp.exp(scores - jnp.max(scores, axis=-1, keepdims=True))
        weights = (scores * (1.0 / jnp.sum(scores, axis=-1, keepdims=True))).astype(BF16)
        mixed = dot(weights, values).astype(BF16)
        wide = dot(mixed, wv_ref[:, g * span : (g + 1) * span])
        part = wide[:rows]
        for h in range(1, group):
            part = jnp.where(lane_head == h, wide[h * rows : (h + 1) * rows], part)
        gated = (gate_ref[:, g * span : (g + 1) * span] * part).astype(BF16)
        added = dot(gated, wout_ref[g * span : (g + 1) * span, :])
        total = added if g == 0 else total + added
    token_out = (in_ref[...] + total).astype(BF16)
    out_ref[...] = token_out
    back = dot(token_out, wback_ref[...])
    back_ref[...] = back.astype(BF16)
    lower, upper = back[:half], back[rows - half :]
    pair_out[...] = jnp.where(even, upper, lower).astype(BF16)
    odd_out[...] = jnp.where(even, lower, upper).astype(BF16)


def final_body(living_ref, hot_ref, mid_ref, back_ref, pair_ref, odd_ref, wpos_ref, pos_ref, noise_ref, out_ref):
    even = lax.axis_index("row") % 2 == 0
    pair = pair_ref[...].astype(F32)
    odd = odd_ref[...].astype(F32)
    near = jnp.concatenate(
        [jnp.where(even, odd, pair), back_ref[...].astype(F32), jnp.where(even, pair, odd)], axis=0
    ).astype(BF16)
    last = mid_ref[...] + dot(hot_ref[...], near)
    update = dot_nt(wpos_ref[...], normalize(last).astype(BF16))
    noisy = pos_ref[...] + noise_level * noise_ref[...]
    out_ref[...] = jnp.where(living_ref[...] > 0.0, skip_scale * noisy + output_scale * update, 0.0)


def exchange(pair, odd, groups, count):
    near = [(i, i ^ 1) for i in range(count) if i ^ 1 < count]
    odds = [(i, i + 1) for i in range(1, count - 1, 2)]
    far = [(g * count + a, g * count + b) for g in range(groups) for a, b in odds + [(b, a) for a, b in odds]]
    if groups % 2 == 0 and count % 2 == 0:
        far += [(g * count + i, (g ^ 1) * count + i) for g in range(groups) for i in (0, count - 1)]
    return lax.ppermute(pair, "row", near), lax.ppermute(odd, ("grp", "row"), far)


def kind_of(i):
    return (i ^ (i >> 1) ^ (i >> 2)) & 1


def gather_plan(count):
    bits = [1 << b for b in range(count.bit_length() - 1, 0, -1) if 1 << b < count]
    steps = [[b | 1, b | 1] for b in bits]
    if len(bits) > 1:
        high, low = bits[-2] | 1, bits[-1] | 1
        steps[-2:] = [[high, low], [low, high]]
    return steps + [[1, 1]]


def gather(norm, count, between):
    orders = [[0], [0]]
    for n, step in enumerate(gather_plan(count)):
        perm = [(i, i ^ step[kind_of(i)]) for i in range(count)]
        arrived = lax.ppermute(norm, "row", perm)
        if n < len(between):
            arrived, between[n] = lax.optimization_barrier((arrived, between[n](n, norm)))
        norm = jnp.concatenate([norm, arrived], axis=0)
        orders = [orders[p] + [x ^ step[p] for x in orders[kind_of(p ^ step[p])]] for p in range(2)]
    return norm, orders, between


def on_device(
    groups,
    count,
    positions,
    noise,
    atom_single,
    atom_token,
    atom_counts,
    window_offsets,
    atom_bias,
    token_single,
    token_bias,
    pair_mask,
    w_coord,
    w_atom_qkv,
    w_atom_out,
    w_agg,
    w_tok_qkv,
    w_tok_gate,
    w_tok_out,
    w_back,
    w_pos,
):
    rows, width = atom_single.shape
    block_rows, model = token_single.shape
    half = block_rows // 2
    info_shape = shape((8,), jnp.int32)
    info, start, q, keys, values, pair, odd, offsets, tokens, bias, wout, wagg = call(
        embed_body,
        [
            info_shape,
            shape((rows, width), F32),
            shape((rows, width), BF16),
            shape((rows + AHEAD, width), F32),
            shape((rows + AHEAD, width), F32),
            shape((AHEAD, 2 * width), BF16),
            shape((AHEAD, 2 * width), BF16),
            shape((1, rows // QWIN), jnp.int32),
            shape((1, rows), jnp.int32),
            shape(atom_bias.shape, F32),
            shape(w_atom_out.shape, BF16),
            shape(w_agg.shape, BF16),
        ],
        "embed",
        [HBM] * 11,
        [
            pltpu.SMEM((1, 1), jnp.int32),
            pltpu.VMEM(positions.shape, F32),
            pltpu.VMEM(noise.shape, F32),
            pltpu.VMEM(atom_single.shape, BF16),
            pltpu.VMEM(w_coord.shape, F32),
            pltpu.VMEM(w_atom_qkv.shape, BF16),
            pltpu.SemaphoreType.DMA((11,)),
        ],
        out_specs=[SMEM] + [VMEM] * 6 + [SMEM] + [VMEM] * 4,
    )(
        atom_counts[None],
        positions,
        noise,
        atom_single,
        w_coord,
        w_atom_qkv,
        window_offsets[None],
        atom_token,
        atom_bias,
        w_atom_out,
        w_agg,
    )
    pair, odd = exchange(pair, odd, groups, count)
    (att,) = call(
        local_body,
        [shape((rows, width), BF16)],
        "local",
        [SMEM] + [VMEM] * 4,
        flops=10**9,
    )(offsets, q, keys, values, bias)
    packed = model + 128
    mid, own, pair, odd, hot, living = call(
        functools.partial(atoms_body, half),
        [
            shape((rows, width), F32),
            shape((block_rows, packed), F32),
            shape((half, packed), BF16),
            shape((half, packed), BF16),
            shape((rows, block_rows + 2 * half), BF16),
            shape((1, rows), F32),
        ],
        "atoms",
        [SMEM, SMEM] + [VMEM] * 11,
        [pltpu.VMEM((BEHIND + rows + AHEAD, width), F32)] * 2 + [pltpu.VMEM((rows, width), BF16)],
    )(info, offsets, tokens, start, q, keys, values, pair, odd, att, bias, wout, wagg)
    pair, odd = exchange(pair, odd, groups, count)
    token_in, norm = call(
        token_body,
        [shape((block_rows, model), F32), shape((block_rows, model), BF16)],
        "token",
        [VMEM] * 4,
    )(own, pair, odd, token_single)

    def query(n, seen):
        return call(
            query_body,
            [shape((TH * block_rows, model), BF16), shape((block_rows, model), F32)],
            "query",
            [VMEM, HBM, HBM],
            [pltpu.VMEM((model, model), BF16)] * 3 + [pltpu.SemaphoreType.DMA((3,))],
            flops=10**9,
            limit=10,
        )(norm, w_tok_qkv, w_tok_gate)

    def stage(n, seen):
        return call(
            stage_body,
            [
                shape(token_bias.shape, F32),
                shape((model, model), BF16),
                shape((model, model), BF16),
                shape(w_back.shape, BF16),
            ],
            "stage",
            [VMEM] + [HBM] * 5,
            [pltpu.VMEM(pair_mask.shape, jnp.int32), pltpu.SemaphoreType.DMA((5,))],
            flops=10**9,
        )(seen, token_bias, pair_mask, w_tok_qkv, w_tok_out, w_back)

    if count & (count - 1) or count < 8:
        everyone, orders = lax.all_gather(norm, "row", axis=0, tiled=True), None
        between = [query(0, norm), stage(1, norm)]
    else:
        everyone, orders, between = gather(norm, count, [query, stage])
    (query_rows, gate), (bias, wv, wout, wback) = between
    token_out, back, pair, odd = call(
        functools.partial(attend_body, orders, half),
        [
            shape((block_rows, model), BF16),
            shape((block_rows, width), BF16),
            shape((half, width), BF16),
            shape((half, width), BF16),
        ],
        "attend",
        [VMEM] * 8,
        [pltpu.VMEM((count * block_rows, model), BF16)],
    )(token_in, query_rows, gate, everyone, bias, wv, wout, wback)
    pair, odd = exchange(pair, odd, groups, count)
    (denoised,) = call(
        final_body,
        [shape(positions.shape, F32)],
        "final",
        [VMEM] * 9,
    )(living, hot, mid, back, pair, odd, w_pos, positions, noise)
    return (denoised, token_out)


def solution(mesh):
    placed = (
        P(None, ("grp", "row")),
        P(None, ("grp", "row")),
        P(("grp", "row"), None),
        P(("grp", "row")),
        P(("grp", "row")),
        P(("grp", "row")),
        P(None, ("grp", "row"), None),
        P(("grp", "row"), None),
        P(None, ("grp", "row"), None),
        P(("grp", "row"), None),
    ) + (P(),) * 9
    return jax.shard_map(
        functools.partial(on_device, mesh.shape["grp"], mesh.shape["row"]),
        mesh=mesh,
        in_specs=placed,
        out_specs=(P(None, ("grp", "row")), P(("grp", "row"), None)),
        check_vma=False,
    )
```

```python
import functools

import jax
import jax.numpy as jnp
from jax import lax
from jax.experimental import pallas as pl
from jax.experimental.pallas import tpu as pltpu
from jax.sharding import PartitionSpec as P

AH = 4
TH = 16
QWIN = 32
KWIN = 128
BEHIND = KWIN // 2
AHEAD = KWIN - QWIN

noise_level = 2.0
input_scale = 1.0 / 5.0**0.5
skip_scale = 1.0 / 5.0
output_scale = 2.0 / 5.0**0.5
masked_score = -1e30

F32 = jnp.float32
BF16 = jnp.bfloat16
NT = (((1,), (1,)), ((), ()))


def dot(a, b):
    return jnp.dot(a, b, preferred_element_type=F32)


def dot_nt(a, b):
    return lax.dot_general(a, b, NT, preferred_element_type=F32)


def normalize(values):
    center = values - jnp.mean(values, axis=-1, keepdims=True)
    spread = jnp.mean(center * center, axis=-1, keepdims=True)
    return center * lax.rsqrt(spread + 1e-05)


def iota(shape, dim):
    return lax.broadcasted_iota(jnp.int32, shape, dim)


VMEM = pl.BlockSpec(memory_space=pltpu.VMEM)
SMEM = pl.BlockSpec(memory_space=pltpu.SMEM)
HBM = pl.BlockSpec(memory_space=pltpu.HBM)


def call(body, outs, name, specs, scratch=(), flops=10**7, limit=8, out_specs=None):
    moved = sum(o.size * o.dtype.itemsize for o in outs)
    held = [spec is HBM for spec in specs]
    run = pl.pallas_call(
        body,
        out_shape=tuple(outs),
        in_specs=specs,
        out_specs=tuple(out_specs or [VMEM] * len(outs)),
        scratch_shapes=list(scratch),
        name=name,
        cost_estimate=pl.CostEstimate(flops=flops, bytes_accessed=moved, transcendentals=0),
        compiler_params=pltpu.CompilerParams(vmem_limit_bytes=limit * 2**20),
    )
    return lambda *args: run(*[pltpu.with_memory_space_constraint(x, pltpu.HBM) if h and x.size > 1 else x for x, h in zip(args, held)])


def shape(dims, dtype):
    return jax.ShapeDtypeStruct(dims, dtype)


def fetch(sems, *moves):
    copies = [pltpu.make_async_copy(src, dst, sems.at[n]) for n, (src, dst) in enumerate(moves)]
    for copy in copies:
        copy.start()
    return copies


def embed_body(
    counts_hbm,
    pos_hbm,
    noise_hbm,
    single_hbm,
    wc_hbm,
    wqkv_hbm,
    offsets_hbm,
    token_hbm,
    bias_hbm,
    wout_hbm,
    wagg_hbm,
    info_ref,
    start_ref,
    q_ref,
    k_ref,
    v_ref,
    pair_ref,
    odd_ref,
    offsets_ref,
    token_ref,
    bias_ref,
    wout_ref,
    wagg_ref,
    counts_ref,
    pos_ref,
    noise_ref,
    single_ref,
    wc_ref,
    wqkv_ref,
    sems,
):
    copies = fetch(
        sems,
        (pos_hbm, pos_ref),
        (noise_hbm, noise_ref),
        (wc_hbm, wc_ref),
        (single_hbm, single_ref),
        (wqkv_hbm, wqkv_ref),
        (counts_hbm, counts_ref),
        (offsets_hbm, offsets_ref),
        (token_hbm, token_ref.at[0]),
        (bias_hbm, bias_ref),
        (wout_hbm, wout_ref),
        (wagg_hbm, wagg_ref),
    )
    rows, width = single_ref.shape
    for ref in (k_ref, v_ref):
        ref[rows:, :] = jnp.zeros((AHEAD, width), F32)
    for copy in copies[:3]:
        copy.wait()
    scaled = input_scale * (pos_ref[...] + noise_level * noise_ref[...])
    padded = jnp.concatenate([scaled, jnp.zeros((5, rows), F32)], axis=0)
    across = jnp.transpose(padded)
    copies[3].wait()
    start = single_ref[...].astype(F32)
    for c in range(3):
        start = start + across[:, c : c + 1] * wc_ref[c : c + 1, :]
    start_ref[...] = start
    normed = normalize(start).astype(BF16)
    copies[4].wait()
    qkv = dot(normed, wqkv_ref[...]).astype(BF16)
    q_ref[...] = qkv[:, :width]
    copies[5].wait()
    live = counts_ref[0, 0]
    me = lax.axis_index("row")
    info_ref[0] = live
    info_ref[1] = me
    info_ref[2] = lax.axis_size("row") - 1
    tail = live - BEHIND
    even = me % 2 == 0
    for n, ref in enumerate((k_ref, v_ref)):
        at = slice(n * width, (n + 1) * width)
        ref[:rows, :] = qkv[:, (n + 1) * width : (n + 2) * width].astype(F32)
        pair_ref[:, at] = ref[pl.ds(jnp.where(even, tail, 0), AHEAD), :].astype(BF16)
        odd_ref[:, at] = ref[pl.ds(jnp.where(even, 0, tail), AHEAD), :].astype(BF16)
    for copy in copies[6:]:
        copy.wait()


def windows_of(queries, keys, values, biases, masks):
    width = queries[0].shape[1]
    depth = width // AH
    rows = AH * QWIN
    own_head = iota((rows, width), 0) // QWIN == iota((rows, width), 1) // depth
    lane_head = iota((QWIN, width), 1) // depth
    stacked = [jnp.where(own_head, jnp.concatenate([q] * AH, axis=0), 0.0).astype(BF16) for q in queries]
    scores = [dot_nt(q, k) * (1.0 / depth**0.5) + b for q, k, b in zip(stacked, keys, biases)]
    if masks is not None:
        scores = [jnp.where(m, s, masked_score) for m, s in zip(masks, scores)]
    tops = [jnp.max(s, axis=-1, keepdims=True) for s in scores]
    scores = [jnp.exp(s - t) for s, t in zip(scores, tops)]
    shares = [1.0 / jnp.sum(s, axis=-1, keepdims=True) for s in scores]
    weights = [(s * r).astype(BF16) for s, r in zip(scores, shares)]
    mixed = [dot(w, v) for w, v in zip(weights, values)]
    outs = []
    for mix in mixed:
        out = mix[:QWIN]
        for h in range(1, AH):
            out = jnp.where(lane_head == h, mix[h * QWIN : (h + 1) * QWIN], out)
        outs.append(out.astype(BF16))
    return outs


def local_body(offsets, q_ref, k_ref, v_ref, bias_ref, wgate_hbm, att_ref, wgate_ref, sems):
    copies = fetch(sems, (wgate_hbm, wgate_ref))
    rows, width = q_ref.shape
    windows = rows // QWIN
    skip = BEHIND // QWIN
    stop = windows - (AHEAD - QWIN) // QWIN
    for part in (slice(0, skip * QWIN), slice(stop * QWIN, rows)):
        att_ref[part, :] = jnp.zeros((part.stop - part.start, width), BF16)
    at = [slice(m * QWIN, (m + 1) * QWIN) for m in range(skip, stop)]
    base = [m * QWIN + offsets[0, m] for m in range(skip, stop)]
    outs = windows_of(
        [q_ref[a, :].astype(F32) for a in at],
        [k_ref[pl.ds(b, KWIN), :].astype(BF16) for b in base],
        [v_ref[pl.ds(b, KWIN), :].astype(BF16) for b in base],
        [bias_ref[:, a, :].reshape(AH * QWIN, KWIN) for a in at],
        None,
    )
    for a, out in zip(at, outs):
        att_ref[a, :] = out
    copies[0].wait()


def atoms_body(
    half,
    info,
    offsets,
    token_ref,
    start_ref,
    q_ref,
    k_ref,
    v_ref,
    pair_ref,
    odd_ref,
    att_ref,
    bias_ref,
    wout_ref,
    wagg_ref,
    mid_ref,
    own_ref,
    pair_out,
    odd_out,
    hot_ref,
    living_ref,
    k_ext,
    v_ext,
    att,
):
    rows, width = start_ref.shape
    live, me, last = info[0], info[1], info[2]
    even = me % 2 == 0
    pair = pair_ref[...].astype(F32)
    odd = odd_ref[...].astype(F32)
    for n, (ref, ext) in enumerate(((k_ref, k_ext), (v_ref, v_ext))):
        at = slice(n * width, (n + 1) * width)
        ext[:BEHIND, :] = jnp.where(even, odd[:BEHIND, at], pair[:BEHIND, at])
        ext[BEHIND : BEHIND + rows + AHEAD, :] = ref[...]
        ext[pl.ds(BEHIND + live, AHEAD), :] = jnp.where(even, pair[:, at], odd[:, at])
    low = jnp.where(me > 0, 0, BEHIND)
    high = BEHIND + live + jnp.where(me < last, AHEAD, 0)
    att[...] = att_ref[...]
    windows = rows // QWIN
    tails = AHEAD // QWIN
    first = jnp.minimum((live - BEHIND) // QWIN, windows - tails)
    chosen = list(range(BEHIND // QWIN)) + [first + n for n in range(tails)]
    at = [pl.ds(pl.multiple_of(m * QWIN, QWIN), QWIN) for m in chosen]
    base = [BEHIND + QWIN * m + offsets[0, m] for m in chosen]
    slots = [b + iota((1, KWIN), 1) for b in base]
    outs = windows_of(
        [q_ref[a, :].astype(F32) for a in at],
        [k_ext[pl.ds(b, KWIN), :].astype(BF16) for b in base],
        [v_ext[pl.ds(b, KWIN), :].astype(BF16) for b in base],
        [bias_ref[:, a, :].reshape(AH * QWIN, KWIN) for a in at],
        [(s >= low) & (s < high) for s in slots],
    )
    for a, out in zip(at, outs):
        att[a, :] = out
    mid = start_ref[...] + dot(att[...], wout_ref[...])
    mid_ref[...] = mid
    spread = jnp.maximum(dot(mid.astype(BF16), wagg_ref[...]), 0.0).astype(BF16)
    block_rows = own_ref.shape[0]
    living = iota((1, rows), 1) < live
    living_ref[...] = living.astype(F32)
    relative = token_ref[...] - (me * block_rows - half)
    hot = ((iota((block_rows + 2 * half, rows), 0) == relative) & living).astype(F32)
    hot_ref[...] = jnp.transpose(hot).astype(BF16)
    sums = dot(hot.astype(BF16), spread)
    counts = jnp.sum(hot, axis=1, keepdims=True)
    first = jnp.minimum(counts, 256.0)
    lane = iota((counts.shape[0], 128), 1)
    packed = jnp.where(lane == 0, first, jnp.where(lane == 1, counts - first, 0.0))
    model = wagg_ref.shape[1]
    own_ref[:, :model] = sums[half : half + block_rows]
    own_ref[:, model:] = packed[half : half + block_rows]
    lower = jnp.concatenate([sums[:half], packed[:half]], axis=1)
    upper = jnp.concatenate([sums[half + block_rows :], packed[half + block_rows :]], axis=1)
    pair_out[...] = jnp.where(even, upper, lower).astype(BF16)
    odd_out[...] = jnp.where(even, lower, upper).astype(BF16)


def token_body(own_ref, pair_ref, odd_ref, single_ref, in_ref, norm_ref):
    me = lax.axis_index("row")
    even = me % 2 == 0
    model = single_ref.shape[1]
    pair = pair_ref[...].astype(F32)
    odd = odd_ref[...].astype(F32)
    lower = jnp.where(me > 0, jnp.where(even, odd, pair), 0.0)
    upper = jnp.where(me < lax.axis_size("row") - 1, jnp.where(even, pair, odd), 0.0)
    both = own_ref[...] + jnp.concatenate([lower, upper], axis=0)
    count = both[:, model : model + 1] + both[:, model + 1 : model + 2]
    token_in = single_ref[...].astype(F32) + both[:, :model] / jnp.maximum(count, 1.0)
    in_ref[...] = token_in
    norm_ref[...] = normalize(token_in).astype(BF16)


def query_body(norm_ref, wqkv_ref, wgate_ref, query_ref, gate_ref):
    rows, model = norm_ref.shape
    width = model // TH
    group = TH // 2
    span = group * width
    norm = norm_ref[...]
    own = iota((group * rows, span), 0) // rows == iota((group * rows, span), 1) // width
    tq = dot(norm, wqkv_ref[:, :model])
    for g in range(2):
        part = tq[:, g * span : (g + 1) * span]
        stacked = jnp.where(own, jnp.concatenate([part] * group, axis=0), 0.0).astype(BF16)
        wk = wqkv_ref[:, model + g * span : model + (g + 1) * span]
        query_ref[g * group * rows : (g + 1) * group * rows, :] = dot_nt(stacked, wk).astype(BF16)
    gate_ref[...] = jax.nn.sigmoid(dot(norm, wgate_ref[...]))


def stage_body(
    lists,
    after,
    bias_hbm,
    mask_hbm,
    wout_hbm,
    wback_hbm,
    out_ref,
    wout_ref,
    wback_ref,
    bias_ref,
    mask_ref,
    sems,
):
    copies = fetch(
        sems, (mask_hbm, mask_ref), (bias_hbm, bias_ref), (wout_hbm, wout_ref), (wback_hbm, wback_ref)
    )
    copies[0].wait()
    copies[1].wait()
    allowed = mask_ref[...] == 1
    heads, rows, keys = bias_ref.shape
    if lists is None:
        for h in range(heads):
            out_ref[0, h * rows : (h + 1) * rows, :] = jnp.where(allowed, bias_ref[h], masked_score)
    else:
        for h in range(heads):
            bias_ref[h] = jnp.where(allowed, bias_ref[h], masked_score)
        me = lax.axis_index("row")
        kind = kind_of(me)
        per = 128 // rows
        lane_block = iota((heads * rows, 128), 1) // rows
        for c in range(len(lists[0])):
            for tile in range(len(lists[0][c]) // per):
                for j in range(per):
                    n = tile * per + j
                    block = me ^ jnp.where(kind == 0, lists[0][c][n], lists[1][c][n])
                    source = pl.ds(pl.multiple_of((block // per) * 128, 128), 128)
                    piece = bias_ref[:, :, source].reshape(heads * rows, 128)
                    piece = pltpu.roll(piece, ((j + per - block % per) % per) * rows, 1)
                    merged = piece if j == 0 else jnp.where(lane_block == j, piece, merged)
                out_ref[c, :, tile * 128 : (tile + 1) * 128] = merged
    for copy in copies[2:]:
        copy.wait()


def part_of(rows, query_ref, keys_ref, bias, wqkv_ref):
    model = query_ref.shape[1]
    width = model // TH
    group = TH // 2
    span = group * width
    keys = keys_ref[...]
    values = dot(keys, wqkv_ref[:, 2 * model :]).astype(BF16)
    lane_head = iota((rows, span), 1) // width

    def by_head(stacked):
        out = jnp.broadcast_to(stacked[:rows], (rows, span))
        for h in range(1, group):
            out = jnp.where(lane_head == h, stacked[h * rows : (h + 1) * rows], out)
        return out

    found = []
    for g in range(2):
        at = slice(g * group * rows, (g + 1) * group * rows)
        scores = dot_nt(query_ref[at, :], keys) * (1.0 / width**0.5) + bias(at)
        top = jnp.max(scores, axis=-1, keepdims=True)
        scores = jnp.exp(scores - top)
        total = jnp.sum(scores, axis=-1, keepdims=True)
        mixed = dot(scores.astype(BF16), values[:, g * span : (g + 1) * span])
        found.append((by_head(top), by_head(total), by_head(mixed)))
    return [jnp.concatenate([found[0][n], found[1][n]], axis=1) for n in range(3)]


def part_body(chunk, query_ref, keys_ref, bias_ref, wqkv_ref, part_ref):
    found = part_of(part_ref.shape[1], query_ref, keys_ref, lambda at: bias_ref[chunk, at, :], wqkv_ref)
    for n in range(3):
        part_ref[n] = found[n]


def attend_body(
    half,
    chunk,
    in_ref,
    query_ref,
    gate_ref,
    keys_ref,
    bias_ref,
    wqkv_ref,
    wout_ref,
    wback_ref,
    *rest,
):
    parts, (out_ref, back_ref, pair_out, odd_out) = rest[:-4], rest[-4:]
    rows, model = in_ref.shape
    even = lax.axis_index("row") % 2 == 0
    found = part_of(rows, query_ref, keys_ref, lambda at: bias_ref[chunk, at, :], wqkv_ref)
    found = [[part[n] for n in range(3)] for part in parts] + [found]
    top = functools.reduce(jnp.maximum, [f[0] for f in found])
    shares = [jnp.exp(f[0] - top) for f in found]
    total = sum(f[1] * w for f, w in zip(found, shares))
    mixed = sum(f[2] * w for f, w in zip(found, shares))
    gated = (gate_ref[...] * (mixed / total)).astype(BF16)
    token_out = (in_ref[...] + dot(gated, wout_ref[...])).astype(BF16)
    out_ref[...] = token_out
    back = dot(token_out, wback_ref[...])
    back_ref[...] = back.astype(BF16)
    lower, upper = back[:half], back[rows - half :]
    pair_out[...] = jnp.where(even, upper, lower).astype(BF16)
    odd_out[...] = jnp.where(even, lower, upper).astype(BF16)


def final_body(living_ref, hot_ref, mid_ref, back_ref, pair_ref, odd_ref, wpos_ref, pos_ref, noise_ref, out_ref):
    even = lax.axis_index("row") % 2 == 0
    pair = pair_ref[...].astype(F32)
    odd = odd_ref[...].astype(F32)
    near = jnp.concatenate(
        [jnp.where(even, odd, pair), back_ref[...].astype(F32), jnp.where(even, pair, odd)], axis=0
    ).astype(BF16)
    last = mid_ref[...] + dot(hot_ref[...], near)
    update = dot_nt(wpos_ref[...], normalize(last).astype(BF16))
    noisy = pos_ref[...] + noise_level * noise_ref[...]
    out_ref[...] = jnp.where(living_ref[...] > 0.0, skip_scale * noisy + output_scale * update, 0.0)


def exchange(pair, odd, groups, count):
    near = [(i, i ^ 1) for i in range(count) if i ^ 1 < count]
    odds = [(i, i + 1) for i in range(1, count - 1, 2)]
    far = [(g * count + a, g * count + b) for g in range(groups) for a, b in odds + [(b, a) for a, b in odds]]
    if groups % 2 == 0 and count % 2 == 0:
        far += [(g * count + i, (g ^ 1) * count + i) for g in range(groups) for i in (0, count - 1)]
    return lax.ppermute(pair, "row", near), lax.ppermute(odd, ("grp", "row"), far)


def kind_of(i):
    return (i ^ (i >> 1) ^ (i >> 2)) & 1


def gather_plan(count):
    bits = [1 << b for b in range(count.bit_length() - 1, 0, -1) if 1 << b < count]
    steps = [[b | 1, b | 1] for b in bits]
    high, low = bits[-2] | 1, bits[-1] | 1
    steps[-2:] = [[high, low], [low, high]]
    lists = [[0], [0]]
    for step in steps[:-1]:
        lists = [lists[p] + [x ^ step[p] for x in lists[p ^ kind_of(step[p])]] for p in range(2)]
    near = [[1 ^ x for x in lists[1 - p]] for p in range(2)]
    last = [[x ^ steps[-1][p] for x in lists[p]] for p in range(2)]
    end = [[1 ^ x for x in last[1 - p]] for p in range(2)]
    return steps, [[lists[p], near[p], last[p], end[p]] for p in range(2)]


def swap(value, count, step):
    return lax.ppermute(value, "row", [(i, i ^ step[kind_of(i)]) for i in range(count)])


def on_device(
    groups,
    count,
    positions,
    noise,
    atom_single,
    atom_token,
    atom_counts,
    window_offsets,
    atom_bias,
    token_single,
    token_bias,
    pair_mask,
    w_coord,
    w_atom_qkv,
    w_atom_out,
    w_agg,
    w_tok_qkv,
    w_tok_gate,
    w_tok_out,
    w_back,
    w_pos,
):
    rows, width = atom_single.shape
    block_rows, model = token_single.shape
    half = block_rows // 2
    info_shape = shape((8,), jnp.int32)
    info, start, q, keys, values, pair, odd, offsets, tokens, bias, wout, wagg = call(
        embed_body,
        [
            info_shape,
            shape((rows, width), F32),
            shape((rows, width), BF16),
            shape((rows + AHEAD, width), F32),
            shape((rows + AHEAD, width), F32),
            shape((AHEAD, 2 * width), BF16),
            shape((AHEAD, 2 * width), BF16),
            shape((1, rows // QWIN), jnp.int32),
            shape((1, rows), jnp.int32),
            shape(atom_bias.shape, F32),
            shape(w_atom_out.shape, BF16),
            shape(w_agg.shape, BF16),
        ],
        "embed",
        [HBM] * 11,
        [
            pltpu.SMEM((1, 1), jnp.int32),
            pltpu.VMEM(positions.shape, F32),
            pltpu.VMEM(noise.shape, F32),
            pltpu.VMEM(atom_single.shape, BF16),
            pltpu.VMEM(w_coord.shape, F32),
            pltpu.VMEM(w_atom_qkv.shape, BF16),
            pltpu.SemaphoreType.DMA((11,)),
        ],
        out_specs=[SMEM] + [VMEM] * 6 + [SMEM] + [VMEM] * 4,
    )(
        atom_counts[None],
        positions,
        noise,
        atom_single,
        w_coord,
        w_atom_qkv,
        window_offsets[None],
        atom_token,
        atom_bias,
        w_atom_out,
        w_agg,
    )
    pair, odd = exchange(pair, odd, groups, count)
    att, wgate = call(
        local_body,
        [shape((rows, width), BF16), shape(w_tok_gate.shape, BF16)],
        "local",
        [SMEM] + [VMEM] * 4 + [HBM],
        [pltpu.SemaphoreType.DMA((1,))],
        flops=10**9,
    )(offsets, q, keys, values, bias, w_tok_gate)
    packed = model + 128
    mid, own, pair, odd, hot, living = call(
        functools.partial(atoms_body, half),
        [
            shape((rows, width), F32),
            shape((block_rows, packed), F32),
            shape((half, packed), BF16),
            shape((half, packed), BF16),
            shape((rows, block_rows + 2 * half), BF16),
            shape((1, rows), F32),
        ],
        "atoms",
        [SMEM, SMEM] + [VMEM] * 11,
        [pltpu.VMEM((BEHIND + rows + AHEAD, width), F32)] * 2 + [pltpu.VMEM((rows, width), BF16)],
    )(info, offsets, tokens, start, q, keys, values, pair, odd, att, bias, wout, wagg)
    pair, odd = exchange(pair, odd, groups, count)
    token_in, norm = call(
        token_body,
        [shape((block_rows, model), F32), shape((block_rows, model), BF16)],
        "token",
        [VMEM] * 4,
    )(own, pair, odd, token_single)

    doubling = count & (count - 1) == 0 and count >= 16 and 128 % block_rows == 0
    steps, lists = gather_plan(count) if doubling else ([], None)
    chunks = 4 if doubling else 1
    span = count * block_rows // chunks

    def query(seen):
        return call(
            query_body,
            [shape((TH * block_rows, model), BF16), shape((block_rows, model), F32)],
            "query",
            [VMEM, VMEM, VMEM],
            flops=10**9,
        )(seen, w_tok_qkv, wgate)

    def stage(seen):
        return call(
            functools.partial(stage_body, lists),
            [
                shape((chunks, TH * block_rows, span), F32),
                shape(w_tok_out.shape, BF16),
                shape(w_back.shape, BF16),
            ],
            "stage",
            [VMEM] + [HBM] * 4,
            [
                pltpu.VMEM(token_bias.shape, F32),
                pltpu.VMEM(pair_mask.shape, jnp.int32),
                pltpu.SemaphoreType.DMA((4,)),
            ],
            flops=10**9,
        )(seen, token_bias, pair_mask, w_tok_out, w_back)

    def part(chunk, seen):
        return call(
            functools.partial(part_body, chunk),
            [shape((3, block_rows, model), F32)],
            "part",
            [VMEM] * 4,
            flops=10**9,
        )(query_rows, seen, score_bias, w_tok_qkv)[0]

    if doubling:
        held = norm
        for n, step in enumerate(steps[:-1]):
            arrived = swap(held, count, step)
            if n == 0:
                arrived, (query_rows, gate) = lax.optimization_barrier((arrived, query(norm)))
            if n == 1:
                arrived, (score_bias, wout, wback) = lax.optimization_barrier((arrived, stage(held)))
            held = jnp.concatenate([held, arrived], axis=0)
        last = swap(held, count, steps[-1])
        near = swap(held, count, [1, 1])
        parts = [part(0, held), part(1, near)]
        last, parts = lax.optimization_barrier((last, parts))
        end = swap(last, count, [1, 1])
        parts = parts + [part(2, last)]
    else:
        end = lax.all_gather(norm, "row", axis=0, tiled=True)
        query_rows, gate = query(norm)
        score_bias, wout, wback = stage(norm)
        parts = []
    token_out, back, pair, odd = call(
        functools.partial(attend_body, half, chunks - 1),
        [
            shape((block_rows, model), BF16),
            shape((block_rows, width), BF16),
            shape((half, width), BF16),
            shape((half, width), BF16),
        ],
        "attend",
        [VMEM] * (8 + len(parts)),
    )(token_in, query_rows, gate, end, score_bias, w_tok_qkv, wout, wback, *parts)
    pair, odd = exchange(pair, odd, groups, count)
    (denoised,) = call(
        final_body,
        [shape(positions.shape, F32)],
        "final",
        [VMEM] * 9,
    )(living, hot, mid, back, pair, odd, w_pos, positions, noise)
    return (denoised, token_out)


def solution(mesh):
    placed = (
        P(None, ("grp", "row")),
        P(None, ("grp", "row")),
        P(("grp", "row"), None),
        P(("grp", "row")),
        P(("grp", "row")),
        P(("grp", "row")),
        P(None, ("grp", "row"), None),
        P(("grp", "row"), None),
        P(None, ("grp", "row"), None),
        P(("grp", "row"), None),
    ) + (P(),) * 9
    return jax.shard_map(
        functools.partial(on_device, mesh.shape["grp"], mesh.shape["row"]),
        mesh=mesh,
        in_specs=placed,
        out_specs=(P(None, ("grp", "row")), P(("grp", "row"), None)),
        check_vma=False,
    )
```

```python
import functools

import jax
import jax.numpy as jnp
from jax import lax
from jax.experimental import pallas as pl
from jax.experimental.pallas import tpu as pltpu
from jax.sharding import PartitionSpec as P

AH = 4
TH = 16
QWIN = 32
KWIN = 128
BEHIND = KWIN // 2
AHEAD = KWIN - QWIN

noise_level = 2.0
input_scale = 1.0 / 5.0**0.5
skip_scale = 1.0 / 5.0
output_scale = 2.0 / 5.0**0.5
masked_score = -1e30

F32 = jnp.float32
BF16 = jnp.bfloat16
NT = (((1,), (1,)), ((), ()))


def dot(a, b):
    return jnp.dot(a, b, preferred_element_type=F32)


def dot_nt(a, b):
    return lax.dot_general(a, b, NT, preferred_element_type=F32)


def normalize(values):
    center = values - jnp.mean(values, axis=-1, keepdims=True)
    spread = jnp.mean(center * center, axis=-1, keepdims=True)
    return center * lax.rsqrt(spread + 1e-05)


def iota(shape, dim):
    return lax.broadcasted_iota(jnp.int32, shape, dim)


VMEM = pl.BlockSpec(memory_space=pltpu.VMEM)
SMEM = pl.BlockSpec(memory_space=pltpu.SMEM)
HBM = pl.BlockSpec(memory_space=pltpu.HBM)


def call(body, outs, specs, scratch=(), flops=10**7, limit=8, out_specs=None):
    moved = sum(o.size * o.dtype.itemsize for o in outs)
    held = [spec is HBM for spec in specs]
    run = pl.pallas_call(
        body,
        out_shape=tuple(outs),
        in_specs=specs,
        out_specs=tuple(out_specs or [VMEM] * len(outs)),
        scratch_shapes=list(scratch),
        cost_estimate=pl.CostEstimate(flops=flops, bytes_accessed=moved, transcendentals=0),
        compiler_params=pltpu.CompilerParams(vmem_limit_bytes=limit * 2**20),
    )
    return lambda *args: run(*[pltpu.with_memory_space_constraint(x, pltpu.HBM) if h and x.size > 1 else x for x, h in zip(args, held)])


def shape(dims, dtype):
    return jax.ShapeDtypeStruct(dims, dtype)


def fetch(sems, *moves):
    copies = [pltpu.make_async_copy(src, dst, sems.at[n]) for n, (src, dst) in enumerate(moves)]
    for copy in copies:
        copy.start()
    return copies


def embed_body(
    counts_hbm,
    pos_hbm,
    noise_hbm,
    single_hbm,
    wc_hbm,
    wqkv_hbm,
    offsets_hbm,
    token_hbm,
    bias_hbm,
    wout_hbm,
    wagg_hbm,
    info_ref,
    start_ref,
    q_ref,
    k_ref,
    v_ref,
    pair_ref,
    odd_ref,
    offsets_ref,
    token_ref,
    bias_ref,
    wout_ref,
    wagg_ref,
    counts_ref,
    pos_ref,
    noise_ref,
    single_ref,
    wc_ref,
    wqkv_ref,
    sems,
):
    copies = fetch(
        sems,
        (pos_hbm, pos_ref),
        (noise_hbm, noise_ref),
        (wc_hbm, wc_ref),
        (single_hbm, single_ref),
        (wqkv_hbm, wqkv_ref),
        (counts_hbm, counts_ref),
        (offsets_hbm, offsets_ref),
        (token_hbm, token_ref.at[0]),
        (bias_hbm, bias_ref),
        (wout_hbm, wout_ref),
        (wagg_hbm, wagg_ref),
    )
    rows, width = single_ref.shape
    for ref in (k_ref, v_ref):
        ref[rows:, :] = jnp.zeros((AHEAD, width), F32)
    for copy in copies[:3]:
        copy.wait()
    scaled = input_scale * (pos_ref[...] + noise_level * noise_ref[...])
    padded = jnp.concatenate([scaled, jnp.zeros((5, rows), F32)], axis=0)
    across = jnp.transpose(padded)
    copies[3].wait()
    start = single_ref[...].astype(F32)
    for c in range(3):
        start = start + across[:, c : c + 1] * wc_ref[c : c + 1, :]
    start_ref[...] = start
    normed = normalize(start).astype(BF16)
    copies[4].wait()
    qkv = dot(normed, wqkv_ref[...]).astype(BF16)
    q_ref[...] = qkv[:, :width]
    copies[5].wait()
    live = counts_ref[0, 0]
    me = lax.axis_index("row")
    info_ref[0] = live
    info_ref[1] = me
    info_ref[2] = lax.axis_size("row") - 1
    tail = live - BEHIND
    even = me % 2 == 0
    for n, ref in enumerate((k_ref, v_ref)):
        at = slice(n * width, (n + 1) * width)
        ref[:rows, :] = qkv[:, (n + 1) * width : (n + 2) * width].astype(F32)
        pair_ref[:, at] = ref[pl.ds(jnp.where(even, tail, 0), AHEAD), :].astype(BF16)
        odd_ref[:, at] = ref[pl.ds(jnp.where(even, 0, tail), AHEAD), :].astype(BF16)
    for copy in copies[6:]:
        copy.wait()


def windows_of(queries, keys, values, biases, masks):
    width = queries[0].shape[1]
    depth = width // AH
    rows = AH * QWIN
    own_head = iota((rows, width), 0) // QWIN == iota((rows, width), 1) // depth
    lane_head = iota((QWIN, width), 1) // depth
    stacked = [jnp.where(own_head, jnp.concatenate([q] * AH, axis=0), 0.0).astype(BF16) for q in queries]
    scores = [dot_nt(q, k) * (1.0 / depth**0.5) + b for q, k, b in zip(stacked, keys, biases)]
    if masks is not None:
        scores = [jnp.where(m, s, masked_score) for m, s in zip(masks, scores)]
    tops = [jnp.max(s, axis=-1, keepdims=True) for s in scores]
    scores = [jnp.exp(s - t) for s, t in zip(scores, tops)]
    shares = [1.0 / jnp.sum(s, axis=-1, keepdims=True) for s in scores]
    weights = [(s * r).astype(BF16) for s, r in zip(scores, shares)]
    mixed = [dot(w, v) for w, v in zip(weights, values)]
    outs = []
    for mix in mixed:
        out = mix[:QWIN]
        for h in range(1, AH):
            out = jnp.where(lane_head == h, mix[h * QWIN : (h + 1) * QWIN], out)
        outs.append(out.astype(BF16))
    return outs


def local_body(offsets, q_ref, k_ref, v_ref, bias_ref, att_ref):
    rows, width = q_ref.shape
    windows = rows // QWIN
    skip = BEHIND // QWIN
    stop = windows - (AHEAD - QWIN) // QWIN
    for part in (slice(0, skip * QWIN), slice(stop * QWIN, rows)):
        att_ref[part, :] = jnp.zeros((part.stop - part.start, width), BF16)
    at = [slice(m * QWIN, (m + 1) * QWIN) for m in range(skip, stop)]
    base = [m * QWIN + offsets[0, m] for m in range(skip, stop)]
    outs = windows_of(
        [q_ref[a, :].astype(F32) for a in at],
        [k_ref[pl.ds(b, KWIN), :].astype(BF16) for b in base],
        [v_ref[pl.ds(b, KWIN), :].astype(BF16) for b in base],
        [bias_ref[:, a, :].reshape(AH * QWIN, KWIN) for a in at],
        None,
    )
    for a, out in zip(at, outs):
        att_ref[a, :] = out


def atoms_body(
    half,
    info,
    offsets,
    token_ref,
    start_ref,
    q_ref,
    k_ref,
    v_ref,
    pair_ref,
    odd_ref,
    att_ref,
    bias_ref,
    wout_ref,
    wagg_ref,
    mid_ref,
    own_ref,
    pair_out,
    odd_out,
    hot_ref,
    living_ref,
    k_ext,
    v_ext,
    att,
):
    rows, width = start_ref.shape
    live, me, last = info[0], info[1], info[2]
    even = me % 2 == 0
    pair = pair_ref[...].astype(F32)
    odd = odd_ref[...].astype(F32)
    for n, (ref, ext) in enumerate(((k_ref, k_ext), (v_ref, v_ext))):
        at = slice(n * width, (n + 1) * width)
        ext[:BEHIND, :] = jnp.where(even, odd[:BEHIND, at], pair[:BEHIND, at])
        ext[BEHIND : BEHIND + rows + AHEAD, :] = ref[...]
        ext[pl.ds(BEHIND + live, AHEAD), :] = jnp.where(even, pair[:, at], odd[:, at])
    low = jnp.where(me > 0, 0, BEHIND)
    high = BEHIND + live + jnp.where(me < last, AHEAD, 0)
    att[...] = att_ref[...]
    windows = rows // QWIN
    tails = AHEAD // QWIN
    first = jnp.minimum((live - BEHIND) // QWIN, windows - tails)
    chosen = list(range(BEHIND // QWIN)) + [first + n for n in range(tails)]
    at = [pl.ds(pl.multiple_of(m * QWIN, QWIN), QWIN) for m in chosen]
    base = [BEHIND + QWIN * m + offsets[0, m] for m in chosen]
    slots = [b + iota((1, KWIN), 1) for b in base]
    outs = windows_of(
        [q_ref[a, :].astype(F32) for a in at],
        [k_ext[pl.ds(b, KWIN), :].astype(BF16) for b in base],
        [v_ext[pl.ds(b, KWIN), :].astype(BF16) for b in base],
        [bias_ref[:, a, :].reshape(AH * QWIN, KWIN) for a in at],
        [(s >= low) & (s < high) for s in slots],
    )
    for a, out in zip(at, outs):
        att[a, :] = out
    mid = start_ref[...] + dot(att[...], wout_ref[...])
    mid_ref[...] = mid
    spread = jnp.maximum(dot(mid.astype(BF16), wagg_ref[...]), 0.0).astype(BF16)
    block_rows = own_ref.shape[0]
    living = iota((1, rows), 1) < live
    living_ref[...] = living.astype(F32)
    relative = token_ref[...] - (me * block_rows - half)
    hot = ((iota((block_rows + 2 * half, rows), 0) == relative) & living).astype(F32)
    hot_ref[...] = jnp.transpose(hot).astype(BF16)
    sums = dot(hot.astype(BF16), spread)
    counts = jnp.sum(hot, axis=1, keepdims=True)
    first = jnp.minimum(counts, 256.0)
    lane = iota((counts.shape[0], 128), 1)
    packed = jnp.where(lane == 0, first, jnp.where(lane == 1, counts - first, 0.0))
    model = wagg_ref.shape[1]
    own_ref[:, :model] = sums[half : half + block_rows]
    own_ref[:, model:] = packed[half : half + block_rows]
    lower = jnp.concatenate([sums[:half], packed[:half]], axis=1)
    upper = jnp.concatenate([sums[half + block_rows :], packed[half + block_rows :]], axis=1)
    pair_out[...] = jnp.where(even, upper, lower).astype(BF16)
    odd_out[...] = jnp.where(even, lower, upper).astype(BF16)


def token_body(own_ref, pair_ref, odd_ref, single_ref, in_ref, norm_ref):
    me = lax.axis_index("row")
    even = me % 2 == 0
    model = single_ref.shape[1]
    pair = pair_ref[...].astype(F32)
    odd = odd_ref[...].astype(F32)
    lower = jnp.where(me > 0, jnp.where(even, odd, pair), 0.0)
    upper = jnp.where(me < lax.axis_size("row") - 1, jnp.where(even, pair, odd), 0.0)
    both = own_ref[...] + jnp.concatenate([lower, upper], axis=0)
    count = both[:, model : model + 1] + both[:, model + 1 : model + 2]
    token_in = single_ref[...].astype(F32) + both[:, :model] / jnp.maximum(count, 1.0)
    in_ref[...] = token_in
    norm_ref[...] = normalize(token_in).astype(BF16)


def weights_body(after, wgate_hbm, wout_hbm, wback_hbm, wgate_ref, wout_ref, wback_ref, both_ref, sems):
    copies = fetch(sems, (wout_hbm, wout_ref), (wback_hbm, wback_ref), (wgate_hbm, wgate_ref))
    copies[0].wait()
    copies[1].wait()
    both_ref[...] = dot(wout_ref[...], wback_ref[...]).astype(BF16)
    copies[2].wait()


def query_body(norm_ref, in_ref, wqkv_ref, wgate_ref, wback_ref, query_ref, gate_ref, back_ref):
    rows, model = norm_ref.shape
    width = model // TH
    group = TH // 2
    span = group * width
    norm = norm_ref[...]
    own = iota((group * rows, span), 0) // rows == iota((group * rows, span), 1) // width
    tq = dot(norm, wqkv_ref[:, :model])
    for g in range(2):
        part = tq[:, g * span : (g + 1) * span]
        stacked = jnp.where(own, jnp.concatenate([part] * group, axis=0), 0.0).astype(BF16)
        wk = wqkv_ref[:, model + g * span : model + (g + 1) * span]
        query_ref[g * group * rows : (g + 1) * group * rows, :] = dot_nt(stacked, wk).astype(BF16)
    gate_ref[...] = jax.nn.sigmoid(dot(norm, wgate_ref[...]))
    back_ref[...] = dot(in_ref[...].astype(BF16), wback_ref[...])


def stage_body(
    lists,
    after,
    bias_hbm,
    mask_hbm,
    out_ref,
    bias_ref,
    mask_ref,
    sems,
):
    copies = fetch(sems, (mask_hbm, mask_ref), (bias_hbm, bias_ref))
    copies[0].wait()
    copies[1].wait()
    allowed = mask_ref[...] == 1
    heads, rows, _ = bias_ref.shape
    if lists is None:
        for h in range(heads):
            out_ref[0, h * rows : (h + 1) * rows, :] = jnp.where(allowed, bias_ref[h], masked_score)
    else:
        for h in range(heads):
            bias_ref[h] = jnp.where(allowed, bias_ref[h], masked_score)
        me = lax.axis_index("row")
        kind = kind_of(me)
        per = 128 // rows
        lane_block = iota((heads * rows, 128), 1) // rows
        for c in range(len(lists[0])):
            for tile in range(len(lists[0][c]) // per):
                for j in range(per):
                    n = tile * per + j
                    block = me ^ jnp.where(kind == 0, lists[0][c][n], lists[1][c][n])
                    source = pl.ds(pl.multiple_of((block // per) * 128, 128), 128)
                    piece = bias_ref[:, :, source].reshape(heads * rows, 128)
                    piece = pltpu.roll(piece, ((j + per - block % per) % per) * rows, 1)
                    merged = piece if j == 0 else jnp.where(lane_block == j, piece, merged)
                out_ref[c, :, tile * 128 : (tile + 1) * 128] = merged


def part_of(rows, query_ref, keys_ref, bias, wqkv_ref):
    model = query_ref.shape[1]
    width = model // TH
    group = TH // 2
    span = group * width
    keys = keys_ref[...]
    values = dot(keys, wqkv_ref[:, 2 * model :]).astype(BF16)
    lane_head = iota((rows, span), 1) // width

    def by_head(stacked):
        out = jnp.broadcast_to(stacked[:rows], (rows, span))
        for h in range(1, group):
            out = jnp.where(lane_head == h, stacked[h * rows : (h + 1) * rows], out)
        return out

    found = []
    for g in range(2):
        at = slice(g * group * rows, (g + 1) * group * rows)
        scores = dot_nt(query_ref[at, :], keys) * (1.0 / width**0.5) + bias(at)
        top = jnp.max(scores, axis=-1, keepdims=True)
        scores = jnp.exp(scores - top)
        total = jnp.sum(scores, axis=-1, keepdims=True)
        mixed = dot(scores.astype(BF16), values[:, g * span : (g + 1) * span])
        found.append((by_head(top), by_head(total), by_head(mixed)))
    return [jnp.concatenate([found[0][n], found[1][n]], axis=1) for n in range(3)]


def part_body(chunk, query_ref, keys_ref, bias_ref, wqkv_ref, part_ref):
    found = part_of(part_ref.shape[1], query_ref, keys_ref, lambda at: bias_ref[chunk, at, :], wqkv_ref)
    for n in range(3):
        part_ref[n] = found[n]


def attend_body(
    half,
    chunk,
    base_ref,
    query_ref,
    gate_ref,
    keys_ref,
    bias_ref,
    wqkv_ref,
    both_ref,
    *rest,
):
    parts, (gated_ref, back_ref, pair_out, odd_out) = rest[:-4], rest[-4:]
    rows, _ = gate_ref.shape
    even = lax.axis_index("row") % 2 == 0
    found = part_of(rows, query_ref, keys_ref, lambda at: bias_ref[chunk, at, :], wqkv_ref)
    found = [[part[n] for n in range(3)] for part in parts] + [found]
    top = functools.reduce(jnp.maximum, [f[0] for f in found])
    shares = [jnp.exp(f[0] - top) for f in found]
    total = sum(f[1] * w for f, w in zip(found, shares))
    mixed = sum(f[2] * w for f, w in zip(found, shares))
    gated = (gate_ref[...] * (mixed / total)).astype(BF16)
    gated_ref[...] = gated
    back = base_ref[...] + dot(gated, both_ref[...])
    back_ref[...] = back.astype(BF16)
    lower, upper = back[:half], back[rows - half :]
    pair_out[...] = jnp.where(even, upper, lower).astype(BF16)
    odd_out[...] = jnp.where(even, lower, upper).astype(BF16)


def out_body(in_ref, gated_ref, wout_ref, out_ref):
    out_ref[...] = (in_ref[...] + dot(gated_ref[...], wout_ref[...])).astype(BF16)


def final_body(living_ref, hot_ref, mid_ref, back_ref, pair_ref, odd_ref, wpos_ref, pos_ref, noise_ref, out_ref):
    even = lax.axis_index("row") % 2 == 0
    pair = pair_ref[...].astype(F32)
    odd = odd_ref[...].astype(F32)
    near = jnp.concatenate(
        [jnp.where(even, odd, pair), back_ref[...].astype(F32), jnp.where(even, pair, odd)], axis=0
    ).astype(BF16)
    last = mid_ref[...] + dot(hot_ref[...], near)
    update = dot_nt(wpos_ref[...], normalize(last).astype(BF16))
    noisy = pos_ref[...] + noise_level * noise_ref[...]
    out_ref[...] = jnp.where(living_ref[...] > 0.0, skip_scale * noisy + output_scale * update, 0.0)


def exchange(pair, odd, groups, count):
    near = [(i, i ^ 1) for i in range(count) if i ^ 1 < count]
    odds = [(i, i + 1) for i in range(1, count - 1, 2)]
    far = [(g * count + a, g * count + b) for g in range(groups) for a, b in odds + [(b, a) for a, b in odds]]
    if groups % 2 == 0 and count % 2 == 0:
        far += [(g * count + i, (g ^ 1) * count + i) for g in range(groups) for i in (0, count - 1)]
    odd = lax.ppermute(odd, ("grp", "row"), far)
    pair = lax.ppermute(pair, "row", near)
    return pair, odd


def kind_of(i):
    return (i ^ (i >> 1) ^ (i >> 2)) & 1


def gather_plan(count):
    bits = [1 << b for b in range(count.bit_length() - 1, 0, -1) if 1 << b < count]
    steps = [[b | 1, b | 1] for b in bits]
    high, low = bits[-2] | 1, bits[-1] | 1
    steps[-2:] = [[high, low], [low, high]]
    lists = [[0], [0]]
    for step in steps[:-1]:
        lists = [lists[p] + [x ^ step[p] for x in lists[p ^ kind_of(step[p])]] for p in range(2)]
    near = [[1 ^ x for x in lists[1 - p]] for p in range(2)]
    last = [[x ^ steps[-1][p] for x in lists[p]] for p in range(2)]
    end = [[1 ^ x for x in last[1 - p]] for p in range(2)]
    return steps, [[lists[p], near[p], last[p], end[p]] for p in range(2)]


def swap(value, count, step):
    return lax.ppermute(value, "row", [(i, i ^ step[kind_of(i)]) for i in range(count)])


def on_device(
    groups,
    count,
    positions,
    noise,
    atom_single,
    atom_token,
    atom_counts,
    window_offsets,
    atom_bias,
    token_single,
    token_bias,
    pair_mask,
    w_coord,
    w_atom_qkv,
    w_atom_out,
    w_agg,
    w_tok_qkv,
    w_tok_gate,
    w_tok_out,
    w_back,
    w_pos,
):
    rows, width = atom_single.shape
    block_rows, model = token_single.shape
    half = block_rows // 2
    info_shape = shape((8,), jnp.int32)
    info, start, q, keys, values, pair, odd, offsets, tokens, bias, wout, wagg = call(
        embed_body,
        [
            info_shape,
            shape((rows, width), F32),
            shape((rows, width), BF16),
            shape((rows + AHEAD, width), F32),
            shape((rows + AHEAD, width), F32),
            shape((AHEAD, 2 * width), BF16),
            shape((AHEAD, 2 * width), BF16),
            shape((1, rows // QWIN), jnp.int32),
            shape((1, rows), jnp.int32),
            shape(atom_bias.shape, F32),
            shape(w_atom_out.shape, BF16),
            shape(w_agg.shape, BF16),
        ],
        [HBM] * 11,
        [
            pltpu.SMEM((1, 1), jnp.int32),
            pltpu.VMEM(positions.shape, F32),
            pltpu.VMEM(noise.shape, F32),
            pltpu.VMEM(atom_single.shape, BF16),
            pltpu.VMEM(w_coord.shape, F32),
            pltpu.VMEM(w_atom_qkv.shape, BF16),
            pltpu.SemaphoreType.DMA((11,)),
        ],
        out_specs=[SMEM] + [VMEM] * 6 + [SMEM] + [VMEM] * 4,
    )(
        atom_counts[None],
        positions,
        noise,
        atom_single,
        w_coord,
        w_atom_qkv,
        window_offsets[None],
        atom_token,
        atom_bias,
        w_atom_out,
        w_agg,
    )
    pair, odd = exchange(pair, odd, groups, count)
    (att,) = call(
        local_body, [shape((rows, width), BF16)], [SMEM] + [VMEM] * 4, flops=10**9
    )(offsets, q, keys, values, bias)
    packed = model + 128
    mid, own, pair, odd, hot, living = call(
        functools.partial(atoms_body, half),
        [
            shape((rows, width), F32),
            shape((block_rows, packed), F32),
            shape((half, packed), BF16),
            shape((half, packed), BF16),
            shape((rows, block_rows + 2 * half), BF16),
            shape((1, rows), F32),
        ],
        [SMEM, SMEM] + [VMEM] * 11,
        [pltpu.VMEM((BEHIND + rows + AHEAD, width), F32)] * 2 + [pltpu.VMEM((rows, width), BF16)],
    )(info, offsets, tokens, start, q, keys, values, pair, odd, att, bias, wout, wagg)
    pair, odd = exchange(pair, odd, groups, count)
    wgate, wout, wback, both = call(
        weights_body,
        [
            shape(w_tok_gate.shape, BF16),
            shape(w_tok_out.shape, BF16),
            shape(w_back.shape, BF16),
            shape(w_back.shape, BF16),
        ],
        [VMEM] + [HBM] * 3,
        [pltpu.SemaphoreType.DMA((3,))],
        flops=10**9,
    )(own, w_tok_gate, w_tok_out, w_back)
    odd, wgate, wout, wback, both = lax.optimization_barrier((odd, wgate, wout, wback, both))
    token_in, norm = call(
        token_body, [shape((block_rows, model), F32), shape((block_rows, model), BF16)], [VMEM] * 4
    )(own, pair, odd, token_single)

    doubling = count & (count - 1) == 0 and count >= 16 and 128 % block_rows == 0
    steps, lists = gather_plan(count) if doubling else ([], None)
    chunks = 4 if doubling else 1
    span = count * block_rows // chunks

    def query(seen):
        return call(
            query_body,
            [
                shape((TH * block_rows, model), BF16),
                shape((block_rows, model), F32),
                shape((block_rows, width), F32),
            ],
            [VMEM] * 5,
            flops=10**9,
        )(seen, token_in, w_tok_qkv, wgate, wback)

    def stage(seen):
        return call(
            functools.partial(stage_body, lists),
            [shape((chunks, TH * block_rows, span), F32)],
            [VMEM] + [HBM] * 2,
            [
                pltpu.VMEM(token_bias.shape, F32),
                pltpu.VMEM(pair_mask.shape, jnp.int32),
                pltpu.SemaphoreType.DMA((2,)),
            ],
            flops=10**9,
        )(seen, token_bias, pair_mask)[0]

    def part(chunk, seen):
        return call(
            functools.partial(part_body, chunk),
            [shape((3, block_rows, model), F32)],
            [VMEM] * 4,
            flops=10**9,
        )(query_rows, seen, score_bias, w_tok_qkv)[0]

    if doubling:
        held = norm
        for n, step in enumerate(steps[:-1]):
            arrived = swap(held, count, step)
            if n == 0:
                arrived, (query_rows, gate, base) = lax.optimization_barrier((arrived, query(norm)))
            if n == 1:
                arrived, score_bias = lax.optimization_barrier((arrived, stage(held)))
            held = jnp.concatenate([held, arrived], axis=0)
        last = swap(held, count, steps[-1])
        near = swap(held, count, [1, 1])
        parts = [part(0, held), part(1, near)]
        last, parts = lax.optimization_barrier((last, parts))
        end = swap(last, count, [1, 1])
        parts = parts + [part(2, last)]
    else:
        end = lax.all_gather(norm, "row", axis=0, tiled=True)
        query_rows, gate, base = query(norm)
        score_bias = stage(norm)
        parts = []
    gated, back, pair, odd = call(
        functools.partial(attend_body, half, chunks - 1),
        [
            shape((block_rows, model), BF16),
            shape((block_rows, width), BF16),
            shape((half, width), BF16),
            shape((half, width), BF16),
        ],
        [VMEM] * (7 + len(parts)),
    )(base, query_rows, gate, end, score_bias, w_tok_qkv, both, *parts)
    pair, odd = exchange(pair, odd, groups, count)
    (token_out,) = call(
        out_body, [shape((block_rows, model), BF16)], [VMEM] * 3, flops=10**9
    )(token_in, gated, wout)
    odd, token_out = lax.optimization_barrier((odd, token_out))
    (denoised,) = call(
        final_body, [shape(positions.shape, F32)], [VMEM] * 9
    )(living, hot, mid, back, pair, odd, w_pos, positions, noise)
    return (denoised, token_out)


def solution(mesh):
    placed = (
        P(None, ("grp", "row")),
        P(None, ("grp", "row")),
        P(("grp", "row"), None),
        P(("grp", "row")),
        P(("grp", "row")),
        P(("grp", "row")),
        P(None, ("grp", "row"), None),
        P(("grp", "row"), None),
        P(None, ("grp", "row"), None),
        P(("grp", "row"), None),
    ) + (P(),) * 9
    return jax.shard_map(
        functools.partial(on_device, mesh.shape["grp"], mesh.shape["row"]),
        mesh=mesh,
        in_specs=placed,
        out_specs=(P(None, ("grp", "row")), P(("grp", "row"), None)),
        check_vma=False,
    )
```

```python
import functools

import jax
import jax.numpy as jnp
from jax import lax
from jax.experimental import pallas as pl
from jax.experimental.pallas import tpu as pltpu
from jax.sharding import PartitionSpec as P

AH = 4
TH = 16
QWIN = 32
KWIN = 128
BEHIND = KWIN // 2
AHEAD = KWIN - QWIN

noise_level = 2.0
input_scale = 1.0 / 5.0**0.5
skip_scale = 1.0 / 5.0
output_scale = 2.0 / 5.0**0.5
masked_score = -1e30

F32 = jnp.float32
BF16 = jnp.bfloat16
NT = (((1,), (1,)), ((), ()))


def dot(a, b):
    return jnp.dot(a, b, preferred_element_type=F32)


def dot_nt(a, b):
    return lax.dot_general(a, b, NT, preferred_element_type=F32)


def normalize(values):
    center = values - jnp.mean(values, axis=-1, keepdims=True)
    spread = jnp.mean(center * center, axis=-1, keepdims=True)
    return center * lax.rsqrt(spread + 1e-05)


def iota(shape, dim):
    return lax.broadcasted_iota(jnp.int32, shape, dim)


VMEM = pl.BlockSpec(memory_space=pltpu.VMEM)
SMEM = pl.BlockSpec(memory_space=pltpu.SMEM)
HBM = pl.BlockSpec(memory_space=pltpu.HBM)


def call(body, outs, specs, scratch=(), flops=10**7, limit=8, out_specs=None):
    moved = sum(o.size * o.dtype.itemsize for o in outs)
    held = [spec is HBM for spec in specs]
    run = pl.pallas_call(
        body,
        out_shape=tuple(outs),
        in_specs=specs,
        out_specs=tuple(out_specs or [VMEM] * len(outs)),
        scratch_shapes=list(scratch),
        cost_estimate=pl.CostEstimate(flops=flops, bytes_accessed=moved, transcendentals=0),
        compiler_params=pltpu.CompilerParams(vmem_limit_bytes=limit * 2**20),
    )
    return lambda *args: run(*[pltpu.with_memory_space_constraint(x, pltpu.HBM) if h and x.size > 1 else x for x, h in zip(args, held)])


def shape(dims, dtype):
    return jax.ShapeDtypeStruct(dims, dtype)


def fetch(sems, *moves):
    copies = [pltpu.make_async_copy(src, dst, sems.at[n]) for n, (src, dst) in enumerate(moves)]
    for copy in copies:
        copy.start()
    return copies


def quarters(src, dst):
    step = src.shape[0] // 4
    return [(src.at[pl.ds(n * step, step)], dst.at[pl.ds(n * step, step)]) for n in range(4)]


def embed_body(
    counts_hbm,
    pos_hbm,
    noise_hbm,
    single_hbm,
    wc_hbm,
    wqkv_hbm,
    offsets_hbm,
    token_hbm,
    bias_hbm,
    wout_hbm,
    wagg_hbm,
    info_ref,
    start_ref,
    normed_ref,
    pair_ref,
    odd_ref,
    offsets_ref,
    token_ref,
    bias_ref,
    wout_ref,
    wagg_ref,
    wqkv_ref,
    counts_ref,
    pos_ref,
    noise_ref,
    single_ref,
    wc_ref,
    wide_ref,
    sems,
):
    copies = fetch(
        sems,
        (pos_hbm, pos_ref),
        (noise_hbm, noise_ref),
        (wc_hbm, wc_ref),
        (single_hbm, single_ref),
        (counts_hbm, counts_ref),
        (wqkv_hbm, wqkv_ref),
        (offsets_hbm, offsets_ref),
        (token_hbm, token_ref.at[0]),
        *quarters(bias_hbm, bias_ref),
        (wout_hbm, wout_ref),
        (wagg_hbm, wagg_ref),
    )
    rows, width = single_ref.shape
    wide_ref[rows:, :] = jnp.zeros((AHEAD, width), F32)
    for copy in copies[:3]:
        copy.wait()
    scaled = input_scale * (pos_ref[...] + noise_level * noise_ref[...])
    padded = jnp.concatenate([scaled, jnp.zeros((5, rows), F32)], axis=0)
    across = jnp.transpose(padded)
    copies[3].wait()
    start = single_ref[...].astype(F32)
    for c in range(3):
        start = start + across[:, c : c + 1] * wc_ref[c : c + 1, :]
    start_ref[...] = start
    normed = normalize(start)
    normed_ref[...] = normed.astype(BF16)
    wide_ref[:rows, :] = normed
    copies[4].wait()
    live = counts_ref[0, 0]
    me = lax.axis_index("row")
    info_ref[0] = live
    info_ref[1] = me
    info_ref[2] = lax.axis_size("row") - 1
    tail = live - BEHIND
    even = me % 2 == 0
    pair_ref[...] = wide_ref[pl.ds(jnp.where(even, tail, 0), AHEAD), :].astype(BF16)
    odd_ref[...] = wide_ref[pl.ds(jnp.where(even, 0, tail), AHEAD), :].astype(BF16)
    for copy in copies[5:]:
        copy.wait()


def windows_of(queries, keys, values, biases, masks):
    width = queries[0].shape[1]
    depth = width // AH
    rows = AH * QWIN
    own_head = iota((rows, width), 0) // QWIN == iota((rows, width), 1) // depth
    lane_head = iota((QWIN, width), 1) // depth
    stacked = [jnp.where(own_head, jnp.concatenate([q] * AH, axis=0), 0.0).astype(BF16) for q in queries]
    scores = [dot_nt(q, k) * (1.0 / depth**0.5) + b for q, k, b in zip(stacked, keys, biases)]
    if masks is not None:
        scores = [jnp.where(m, s, masked_score) for m, s in zip(masks, scores)]
    tops = [jnp.max(s, axis=-1, keepdims=True) for s in scores]
    scores = [jnp.exp(s - t) for s, t in zip(scores, tops)]
    shares = [1.0 / jnp.sum(s, axis=-1, keepdims=True) for s in scores]
    weights = [(s * r).astype(BF16) for s, r in zip(scores, shares)]
    mixed = [dot(w, v) for w, v in zip(weights, values)]
    outs = []
    for mix in mixed:
        out = mix[:QWIN]
        for h in range(1, AH):
            out = jnp.where(lane_head == h, mix[h * QWIN : (h + 1) * QWIN], out)
        outs.append(out.astype(BF16))
    return outs


def local_body(offsets, normed_ref, wqkv_ref, bias_ref, q_ref, k_ref, v_ref, att_ref):
    rows, width = normed_ref.shape
    qkv = dot(normed_ref[...], wqkv_ref[...]).astype(BF16)
    q_ref[...] = qkv[:, :width]
    for n, ref in enumerate((k_ref, v_ref)):
        ref[:rows, :] = qkv[:, (n + 1) * width : (n + 2) * width].astype(F32)
        ref[rows:, :] = jnp.zeros((AHEAD, width), F32)
    windows = rows // QWIN
    skip = BEHIND // QWIN
    stop = windows - (AHEAD - QWIN) // QWIN
    for part in (slice(0, skip * QWIN), slice(stop * QWIN, rows)):
        att_ref[part, :] = jnp.zeros((part.stop - part.start, width), BF16)
    at = [slice(m * QWIN, (m + 1) * QWIN) for m in range(skip, stop)]
    base = [m * QWIN + offsets[0, m] for m in range(skip, stop)]
    outs = windows_of(
        [q_ref[a, :].astype(F32) for a in at],
        [k_ref[pl.ds(b, KWIN), :].astype(BF16) for b in base],
        [v_ref[pl.ds(b, KWIN), :].astype(BF16) for b in base],
        [bias_ref[:, a, :].reshape(AH * QWIN, KWIN) for a in at],
        None,
    )
    for a, out in zip(at, outs):
        att_ref[a, :] = out


def atoms_body(
    half,
    info,
    offsets,
    token_ref,
    start_ref,
    q_ref,
    k_ref,
    v_ref,
    pair_ref,
    odd_ref,
    att_ref,
    bias_ref,
    wout_ref,
    wagg_ref,
    wqkv_ref,
    mid_ref,
    own_ref,
    pair_out,
    odd_out,
    hot_ref,
    living_ref,
    k_ext,
    v_ext,
    att,
):
    rows, width = start_ref.shape
    live, me, last = info[0], info[1], info[2]
    even = me % 2 == 0
    pair = dot(pair_ref[...], wqkv_ref[:, width:]).astype(BF16).astype(F32)
    odd = dot(odd_ref[...], wqkv_ref[:, width:]).astype(BF16).astype(F32)
    for n, (ref, ext) in enumerate(((k_ref, k_ext), (v_ref, v_ext))):
        at = slice(n * width, (n + 1) * width)
        ext[:BEHIND, :] = jnp.where(even, odd[:BEHIND, at], pair[:BEHIND, at])
        ext[BEHIND : BEHIND + rows + AHEAD, :] = ref[...]
        ext[pl.ds(BEHIND + live, AHEAD), :] = jnp.where(even, pair[:, at], odd[:, at])
    low = jnp.where(me > 0, 0, BEHIND)
    high = BEHIND + live + jnp.where(me < last, AHEAD, 0)
    att[...] = att_ref[...]
    windows = rows // QWIN
    tails = AHEAD // QWIN
    first = jnp.minimum((live - BEHIND) // QWIN, windows - tails)
    chosen = list(range(BEHIND // QWIN)) + [first + n for n in range(tails)]
    at = [pl.ds(pl.multiple_of(m * QWIN, QWIN), QWIN) for m in chosen]
    base = [BEHIND + QWIN * m + offsets[0, m] for m in chosen]
    slots = [b + iota((1, KWIN), 1) for b in base]
    outs = windows_of(
        [q_ref[a, :].astype(F32) for a in at],
        [k_ext[pl.ds(b, KWIN), :].astype(BF16) for b in base],
        [v_ext[pl.ds(b, KWIN), :].astype(BF16) for b in base],
        [bias_ref[:, a, :].reshape(AH * QWIN, KWIN) for a in at],
        [(s >= low) & (s < high) for s in slots],
    )
    for a, out in zip(at, outs):
        att[a, :] = out
    mid = start_ref[...] + dot(att[...], wout_ref[...])
    mid_ref[...] = mid
    spread = jnp.maximum(dot(mid.astype(BF16), wagg_ref[...]), 0.0).astype(BF16)
    block_rows = own_ref.shape[0]
    living = iota((1, rows), 1) < live
    living_ref[...] = living.astype(F32)
    relative = token_ref[...] - (me * block_rows - half)
    hot = ((iota((block_rows + 2 * half, rows), 0) == relative) & living).astype(F32)
    hot_ref[...] = jnp.transpose(hot).astype(BF16)
    sums = dot(hot.astype(BF16), spread)
    counts = jnp.sum(hot, axis=1, keepdims=True)
    first = jnp.minimum(counts, 256.0)
    lane = iota((counts.shape[0], 128), 1)
    packed = jnp.where(lane == 0, first, jnp.where(lane == 1, counts - first, 0.0))
    model = wagg_ref.shape[1]
    own_ref[:, :model] = sums[half : half + block_rows]
    own_ref[:, model:] = packed[half : half + block_rows]
    lower = jnp.concatenate([sums[:half], packed[:half]], axis=1)
    upper = jnp.concatenate([sums[half + block_rows :], packed[half + block_rows :]], axis=1)
    pair_out[...] = jnp.where(even, upper, lower).astype(BF16)
    odd_out[...] = jnp.where(even, lower, upper).astype(BF16)


def token_body(own_ref, pair_ref, odd_ref, single_ref, in_ref, norm_ref):
    me = lax.axis_index("row")
    even = me % 2 == 0
    model = single_ref.shape[1]
    pair = pair_ref[...].astype(F32)
    odd = odd_ref[...].astype(F32)
    lower = jnp.where(me > 0, jnp.where(even, odd, pair), 0.0)
    upper = jnp.where(me < lax.axis_size("row") - 1, jnp.where(even, pair, odd), 0.0)
    both = own_ref[...] + jnp.concatenate([lower, upper], axis=0)
    count = both[:, model : model + 1] + both[:, model + 1 : model + 2]
    token_in = single_ref[...].astype(F32) + both[:, :model] / jnp.maximum(count, 1.0)
    in_ref[...] = token_in
    norm_ref[...] = normalize(token_in).astype(BF16)


def weights_body(after, wgate_hbm, wout_hbm, wback_hbm, wgate_ref, wout_ref, wback_ref, both_ref, sems):
    copies = fetch(sems, (wback_hbm, wback_ref), *quarters(wout_hbm, wout_ref), *quarters(wgate_hbm, wgate_ref))
    for copy in copies[:5]:
        copy.wait()
    both_ref[...] = dot(wout_ref[...], wback_ref[...]).astype(BF16)
    for copy in copies[5:]:
        copy.wait()


def query_body(
    norm_ref,
    in_ref,
    wqkv_ref,
    wgate_ref,
    wback_ref,
    bias_hbm,
    mask_hbm,
    query_ref,
    gate_ref,
    back_ref,
    bias_ref,
    mask_ref,
    sems,
):
    copies = fetch(sems, (mask_hbm, mask_ref), *quarters(bias_hbm, bias_ref))
    rows, model = norm_ref.shape
    width = model // TH
    group = TH // 2
    span = group * width
    norm = norm_ref[...]
    own = iota((group * rows, span), 0) // rows == iota((group * rows, span), 1) // width
    tq = dot(norm, wqkv_ref[:, :model])
    for g in range(2):
        part = tq[:, g * span : (g + 1) * span]
        stacked = jnp.where(own, jnp.concatenate([part] * group, axis=0), 0.0).astype(BF16)
        wk = wqkv_ref[:, model + g * span : model + (g + 1) * span]
        query_ref[g * group * rows : (g + 1) * group * rows, :] = dot_nt(stacked, wk).astype(BF16)
    gate_ref[...] = jax.nn.sigmoid(dot(norm, wgate_ref[...]))
    back_ref[...] = dot(in_ref[...].astype(BF16), wback_ref[...])
    for copy in copies:
        copy.wait()


def stage_body(lists, after, bias_ref, mask_ref, out_ref):
    allowed = mask_ref[...] == 1
    heads, rows, _ = bias_ref.shape
    if lists is None:
        for h in range(heads):
            out_ref[0, h * rows : (h + 1) * rows, :] = jnp.where(allowed, bias_ref[h], masked_score)
        return
    me = lax.axis_index("row")
    kind = kind_of(me)
    per = 128 // rows
    lane_block = iota((heads * rows, 128), 1) // rows
    for c in range(len(lists[0])):
        for tile in range(len(lists[0][c]) // per):
            for j in range(per):
                n = tile * per + j
                block = me ^ jnp.where(kind == 0, lists[0][c][n], lists[1][c][n])
                source = pl.ds(pl.multiple_of((block // per) * 128, 128), 128)
                piece = jnp.where((mask_ref[:, source] == 1)[None], bias_ref[:, :, source], masked_score)
                piece = piece.reshape(heads * rows, 128)
                piece = pltpu.roll(piece, ((j + per - block % per) % per) * rows, 1)
                merged = piece if j == 0 else jnp.where(lane_block == j, piece, merged)
            out_ref[c, :, tile * 128 : (tile + 1) * 128] = merged


def part_of(rows, query_ref, keys_ref, bias, wqkv_ref):
    model = query_ref.shape[1]
    width = model // TH
    group = TH // 2
    span = group * width
    keys = keys_ref[...]
    values = dot(keys, wqkv_ref[:, 2 * model :]).astype(BF16)
    lane_head = iota((rows, span), 1) // width

    def by_head(stacked):
        out = jnp.broadcast_to(stacked[:rows], (rows, span))
        for h in range(1, group):
            out = jnp.where(lane_head == h, stacked[h * rows : (h + 1) * rows], out)
        return out

    found = []
    for g in range(2):
        at = slice(g * group * rows, (g + 1) * group * rows)
        scores = dot_nt(query_ref[at, :], keys) * (1.0 / width**0.5) + bias(at)
        top = jnp.max(scores, axis=-1, keepdims=True)
        scores = jnp.exp(scores - top)
        total = jnp.sum(scores, axis=-1, keepdims=True)
        mixed = dot(scores.astype(BF16), values[:, g * span : (g + 1) * span])
        found.append((by_head(top), by_head(total), by_head(mixed)))
    return [jnp.concatenate([found[0][n], found[1][n]], axis=1) for n in range(3)]


def part_body(chunk, query_ref, keys_ref, bias_ref, wqkv_ref, part_ref):
    found = part_of(part_ref.shape[1], query_ref, keys_ref, lambda at: bias_ref[chunk, at, :], wqkv_ref)
    for n in range(3):
        part_ref[n] = found[n]


def attend_body(
    half,
    chunk,
    base_ref,
    query_ref,
    gate_ref,
    keys_ref,
    bias_ref,
    wqkv_ref,
    both_ref,
    *rest,
):
    parts, (gated_ref, back_ref, pair_out, odd_out) = rest[:-4], rest[-4:]
    rows, _ = gate_ref.shape
    even = lax.axis_index("row") % 2 == 0
    found = part_of(rows, query_ref, keys_ref, lambda at: bias_ref[chunk, at, :], wqkv_ref)
    found = [[part[n] for n in range(3)] for part in parts] + [found]
    top = functools.reduce(jnp.maximum, [f[0] for f in found])
    shares = [jnp.exp(f[0] - top) for f in found]
    total = sum(f[1] * w for f, w in zip(found, shares))
    mixed = sum(f[2] * w for f, w in zip(found, shares))
    gated = (gate_ref[...] * (mixed / total)).astype(BF16)
    gated_ref[...] = gated
    back = base_ref[...] + dot(gated, both_ref[...])
    back_ref[...] = back.astype(BF16)
    lower, upper = back[:half], back[rows - half :]
    pair_out[...] = jnp.where(even, upper, lower).astype(BF16)
    odd_out[...] = jnp.where(even, lower, upper).astype(BF16)


def out_body(in_ref, gated_ref, wout_ref, out_ref):
    out_ref[...] = (in_ref[...] + dot(gated_ref[...], wout_ref[...])).astype(BF16)


def final_body(living_ref, hot_ref, mid_ref, back_ref, pair_ref, odd_ref, wpos_ref, pos_ref, noise_ref, out_ref):
    even = lax.axis_index("row") % 2 == 0
    pair = pair_ref[...].astype(F32)
    odd = odd_ref[...].astype(F32)
    near = jnp.concatenate(
        [jnp.where(even, odd, pair), back_ref[...].astype(F32), jnp.where(even, pair, odd)], axis=0
    ).astype(BF16)
    last = mid_ref[...] + dot(hot_ref[...], near)
    update = dot_nt(wpos_ref[...], normalize(last).astype(BF16))
    noisy = pos_ref[...] + noise_level * noise_ref[...]
    out_ref[...] = jnp.where(living_ref[...] > 0.0, skip_scale * noisy + output_scale * update, 0.0)


def exchange(pair, odd, groups, count):
    near = [(i, i ^ 1) for i in range(count) if i ^ 1 < count]
    odds = [(i, i + 1) for i in range(1, count - 1, 2)]
    far = [(g * count + a, g * count + b) for g in range(groups) for a, b in odds + [(b, a) for a, b in odds]]
    if groups % 2 == 0 and count % 2 == 0:
        far += [(g * count + i, (g ^ 1) * count + i) for g in range(groups) for i in (0, count - 1)]
    odd = lax.ppermute(odd, ("grp", "row"), far)
    pair = lax.ppermute(pair, "row", near)
    return pair, odd


def kind_of(i):
    return (i ^ (i >> 1) ^ (i >> 2)) & 1


def gather_plan(count):
    bits = [1 << b for b in range(count.bit_length() - 1, 0, -1) if 1 << b < count]
    steps = [[b | 1, b | 1] for b in bits]
    high, low = bits[-2] | 1, bits[-1] | 1
    steps[-2:] = [[high, low], [low, high]]
    lists = [[0], [0]]
    for step in steps[:-1]:
        lists = [lists[p] + [x ^ step[p] for x in lists[p ^ kind_of(step[p])]] for p in range(2)]
    near = [[1 ^ x for x in lists[1 - p]] for p in range(2)]
    last = [[x ^ steps[-1][p] for x in lists[p]] for p in range(2)]
    end = [[1 ^ x for x in last[1 - p]] for p in range(2)]
    return steps, [[lists[p], near[p], last[p], end[p]] for p in range(2)]


def swap(value, count, step):
    return lax.ppermute(value, "row", [(i, i ^ step[kind_of(i)]) for i in range(count)])


def on_device(
    groups,
    count,
    positions,
    noise,
    atom_single,
    atom_token,
    atom_counts,
    window_offsets,
    atom_bias,
    token_single,
    token_bias,
    pair_mask,
    w_coord,
    w_atom_qkv,
    w_atom_out,
    w_agg,
    w_tok_qkv,
    w_tok_gate,
    w_tok_out,
    w_back,
    w_pos,
):
    rows, width = atom_single.shape
    block_rows, model = token_single.shape
    half = block_rows // 2
    info_shape = shape((8,), jnp.int32)
    info, start, normed, pair, odd, offsets, tokens, bias, wout, wagg, wqkv = call(
        embed_body,
        [
            info_shape,
            shape((rows, width), F32),
            shape((rows, width), BF16),
            shape((AHEAD, width), BF16),
            shape((AHEAD, width), BF16),
            shape((1, rows // QWIN), jnp.int32),
            shape((1, rows), jnp.int32),
            shape(atom_bias.shape, F32),
            shape(w_atom_out.shape, BF16),
            shape(w_agg.shape, BF16),
            shape(w_atom_qkv.shape, BF16),
        ],
        [HBM] * 11,
        [
            pltpu.SMEM((1, 1), jnp.int32),
            pltpu.VMEM(positions.shape, F32),
            pltpu.VMEM(noise.shape, F32),
            pltpu.VMEM(atom_single.shape, BF16),
            pltpu.VMEM(w_coord.shape, F32),
            pltpu.VMEM((rows + AHEAD, width), F32),
            pltpu.SemaphoreType.DMA((14,)),
        ],
        out_specs=[SMEM] + [VMEM] * 4 + [SMEM] + [VMEM] * 5,
    )(
        atom_counts[None],
        positions,
        noise,
        atom_single,
        w_coord,
        w_atom_qkv,
        window_offsets[None],
        atom_token,
        atom_bias,
        w_atom_out,
        w_agg,
    )
    pair, odd = exchange(pair, odd, groups, count)
    q, keys, values, att = call(
        local_body,
        [
            shape((rows, width), BF16),
            shape((rows + AHEAD, width), F32),
            shape((rows + AHEAD, width), F32),
            shape((rows, width), BF16),
        ],
        [SMEM] + [VMEM] * 3,
        flops=10**9,
    )(offsets, normed, wqkv, bias)
    packed = model + 128
    mid, own, pair, odd, hot, living = call(
        functools.partial(atoms_body, half),
        [
            shape((rows, width), F32),
            shape((block_rows, packed), F32),
            shape((half, packed), BF16),
            shape((half, packed), BF16),
            shape((rows, block_rows + 2 * half), BF16),
            shape((1, rows), F32),
        ],
        [SMEM, SMEM] + [VMEM] * 12,
        [pltpu.VMEM((BEHIND + rows + AHEAD, width), F32)] * 2 + [pltpu.VMEM((rows, width), BF16)],
    )(info, offsets, tokens, start, q, keys, values, pair, odd, att, bias, wout, wagg, wqkv)
    pair, odd = exchange(pair, odd, groups, count)
    wgate, wout, wback, both = call(
        weights_body,
        [
            shape(w_tok_gate.shape, BF16),
            shape(w_tok_out.shape, BF16),
            shape(w_back.shape, BF16),
            shape(w_back.shape, BF16),
        ],
        [VMEM] + [HBM] * 3,
        [pltpu.SemaphoreType.DMA((9,))],
        flops=10**9,
    )(own, w_tok_gate, w_tok_out, w_back)
    odd, wgate, wout, wback, both = lax.optimization_barrier((odd, wgate, wout, wback, both))
    token_in, norm = call(
        token_body, [shape((block_rows, model), F32), shape((block_rows, model), BF16)], [VMEM] * 4
    )(own, pair, odd, token_single)

    doubling = count & (count - 1) == 0 and count >= 16 and 128 % block_rows == 0
    steps, lists = gather_plan(count) if doubling else ([], None)
    chunks = 4 if doubling else 1
    span = count * block_rows // chunks

    def query(seen):
        return call(
            query_body,
            [
                shape((TH * block_rows, model), BF16),
                shape((block_rows, model), F32),
                shape((block_rows, width), F32),
                shape(token_bias.shape, F32),
                shape(pair_mask.shape, jnp.int32),
            ],
            [VMEM] * 5 + [HBM] * 2,
            [pltpu.SemaphoreType.DMA((5,))],
            flops=10**9,
        )(seen, token_in, w_tok_qkv, wgate, wback, token_bias, pair_mask)

    def stage(seen, bias, mask):
        return call(
            functools.partial(stage_body, lists),
            [shape((chunks, TH * block_rows, span), F32)],
            [VMEM] * 3,
            flops=10**9,
        )(seen, bias, mask)[0]

    def part(chunk, seen):
        return call(
            functools.partial(part_body, chunk),
            [shape((3, block_rows, model), F32)],
            [VMEM] * 4,
            flops=10**9,
        )(query_rows, seen, score_bias, w_tok_qkv)[0]

    if doubling:
        held = norm
        for n, step in enumerate(steps[:-1]):
            arrived = swap(held, count, step)
            if n == 0:
                arrived, (query_rows, gate, base, raw, mask) = lax.optimization_barrier((arrived, query(norm)))
            if n == 1:
                arrived, score_bias = lax.optimization_barrier((arrived, stage(held, raw, mask)))
            held = jnp.concatenate([held, arrived], axis=0)
        last = swap(held, count, steps[-1])
        near = swap(held, count, [1, 1])
        parts = [part(0, held), part(1, near)]
        last, parts = lax.optimization_barrier((last, parts))
        end = swap(last, count, [1, 1])
        parts = parts + [part(2, last)]
    else:
        end = lax.all_gather(norm, "row", axis=0, tiled=True)
        query_rows, gate, base, raw, mask = query(norm)
        score_bias = stage(norm, raw, mask)
        parts = []
    gated, back, pair, odd = call(
        functools.partial(attend_body, half, chunks - 1),
        [
            shape((block_rows, model), BF16),
            shape((block_rows, width), BF16),
            shape((half, width), BF16),
            shape((half, width), BF16),
        ],
        [VMEM] * (7 + len(parts)),
    )(base, query_rows, gate, end, score_bias, w_tok_qkv, both, *parts)
    pair, odd = exchange(pair, odd, groups, count)
    (token_out,) = call(
        out_body, [shape((block_rows, model), BF16)], [VMEM] * 3, flops=10**9
    )(token_in, gated, wout)
    odd, token_out = lax.optimization_barrier((odd, token_out))
    (denoised,) = call(
        final_body, [shape(positions.shape, F32)], [VMEM] * 9
    )(living, hot, mid, back, pair, odd, w_pos, positions, noise)
    return (denoised, token_out)


def solution(mesh):
    placed = (
        P(None, ("grp", "row")),
        P(None, ("grp", "row")),
        P(("grp", "row"), None),
        P(("grp", "row")),
        P(("grp", "row")),
        P(("grp", "row")),
        P(None, ("grp", "row"), None),
        P(("grp", "row"), None),
        P(None, ("grp", "row"), None),
        P(("grp", "row"), None),
    ) + (P(),) * 9
    return jax.shard_map(
        functools.partial(on_device, mesh.shape["grp"], mesh.shape["row"]),
        mesh=mesh,
        in_specs=placed,
        out_specs=(P(None, ("grp", "row")), P(("grp", "row"), None)),
        check_vma=False,
    )
```

```python
import functools

import jax
import jax.numpy as jnp
from jax import lax
from jax.experimental import pallas as pl
from jax.experimental.pallas import tpu as pltpu
from jax.sharding import PartitionSpec as P

AH = 4
TH = 16
QWIN = 32
KWIN = 128
BEHIND = KWIN // 2
AHEAD = KWIN - QWIN

noise_level = 2.0
input_scale = 1.0 / 5.0**0.5
skip_scale = 1.0 / 5.0
output_scale = 2.0 / 5.0**0.5
masked_score = -1e30

F32 = jnp.float32
BF16 = jnp.bfloat16
NT = (((1,), (1,)), ((), ()))


def dot(a, b):
    return jnp.dot(a, b, preferred_element_type=F32)


def dot_nt(a, b):
    return lax.dot_general(a, b, NT, preferred_element_type=F32)


def normalize(values):
    center = values - jnp.mean(values, axis=-1, keepdims=True)
    spread = jnp.mean(center * center, axis=-1, keepdims=True)
    return center * lax.rsqrt(spread + 1e-05)


def iota(shape, dim):
    return lax.broadcasted_iota(jnp.int32, shape, dim)


VMEM = pl.BlockSpec(memory_space=pltpu.VMEM)
SMEM = pl.BlockSpec(memory_space=pltpu.SMEM)
HBM = pl.BlockSpec(memory_space=pltpu.HBM)


def call(body, outs, specs, scratch=(), flops=10**7, limit=8, out_specs=None):
    moved = sum(o.size * o.dtype.itemsize for o in outs)
    held = [spec is HBM for spec in specs]
    run = pl.pallas_call(
        body,
        out_shape=tuple(outs),
        in_specs=specs,
        out_specs=tuple(out_specs or [VMEM] * len(outs)),
        scratch_shapes=list(scratch),
        cost_estimate=pl.CostEstimate(flops=flops, bytes_accessed=moved, transcendentals=0),
        compiler_params=pltpu.CompilerParams(vmem_limit_bytes=limit * 2**20),
    )
    return lambda *args: run(*[pltpu.with_memory_space_constraint(x, pltpu.HBM) if h and x.size > 1 else x for x, h in zip(args, held)])


def shape(dims, dtype):
    return jax.ShapeDtypeStruct(dims, dtype)


def fetch(sems, *moves):
    copies = [pltpu.make_async_copy(src, dst, sems.at[n]) for n, (src, dst) in enumerate(moves)]
    for copy in copies:
        copy.start()
    return copies


def quarters(src, dst):
    step = src.shape[0] // 4
    return [(src.at[pl.ds(n * step, step)], dst.at[pl.ds(n * step, step)]) for n in range(4)]


def embed_body(
    counts_hbm,
    pos_hbm,
    noise_hbm,
    single_hbm,
    wc_hbm,
    wqkv_hbm,
    offsets_hbm,
    token_hbm,
    bias_hbm,
    wout_hbm,
    wagg_hbm,
    info_ref,
    start_ref,
    normed_ref,
    pair_ref,
    odd_ref,
    offsets_ref,
    token_ref,
    bias_ref,
    wout_ref,
    wagg_ref,
    wqkv_ref,
    counts_ref,
    pos_ref,
    noise_ref,
    single_ref,
    wc_ref,
    wide_ref,
    sems,
):
    copies = fetch(
        sems,
        (pos_hbm, pos_ref),
        (noise_hbm, noise_ref),
        (wc_hbm, wc_ref),
        (single_hbm, single_ref),
        (counts_hbm, counts_ref),
        (wqkv_hbm, wqkv_ref),
        (offsets_hbm, offsets_ref),
        (token_hbm, token_ref.at[0]),
        *quarters(bias_hbm, bias_ref),
        (wout_hbm, wout_ref),
        (wagg_hbm, wagg_ref),
    )
    rows, width = single_ref.shape
    wide_ref[rows:, :] = jnp.zeros((AHEAD, width), F32)
    for copy in copies[:3]:
        copy.wait()
    scaled = input_scale * (pos_ref[...] + noise_level * noise_ref[...])
    moved = lax.dot_general(
        jnp.concatenate([scaled, jnp.zeros((5, rows), F32)], axis=0),
        jnp.concatenate([wc_ref[...], jnp.zeros((5, width), F32)], axis=0),
        (((0,), (0,)), ((), ())),
        precision=lax.Precision.HIGHEST,
        preferred_element_type=F32,
    )
    copies[3].wait()
    start = single_ref[...].astype(F32) + moved
    start_ref[...] = start
    normed = normalize(start)
    normed_ref[...] = normed.astype(BF16)
    wide_ref[:rows, :] = normed
    copies[4].wait()
    live = counts_ref[0, 0]
    me = lax.axis_index("row")
    info_ref[0] = live
    info_ref[1] = me
    info_ref[2] = lax.axis_size("row") - 1
    tail = live - BEHIND
    even = me % 2 == 0
    pair_ref[...] = wide_ref[pl.ds(jnp.where(even, tail, 0), AHEAD), :].astype(BF16)
    odd_ref[...] = wide_ref[pl.ds(jnp.where(even, 0, tail), AHEAD), :].astype(BF16)
    for copy in copies[5:]:
        copy.wait()


def windows_of(queries, keys, values, biases, masks):
    width = queries[0].shape[1]
    depth = width // AH
    rows = AH * QWIN
    own_head = iota((rows, width), 0) // QWIN == iota((rows, width), 1) // depth
    lane_head = iota((QWIN, width), 1) // depth
    stacked = [jnp.where(own_head, jnp.concatenate([q] * AH, axis=0), 0.0).astype(BF16) for q in queries]
    scores = [dot_nt(q, k) * (1.0 / depth**0.5) + b for q, k, b in zip(stacked, keys, biases)]
    if masks is not None:
        scores = [jnp.where(m, s, masked_score) for m, s in zip(masks, scores)]
    tops = [jnp.max(s, axis=-1, keepdims=True) for s in scores]
    scores = [jnp.exp(s - t) for s, t in zip(scores, tops)]
    shares = [1.0 / jnp.sum(s, axis=-1, keepdims=True) for s in scores]
    weights = [(s * r).astype(BF16) for s, r in zip(scores, shares)]
    mixed = [dot(w, v) for w, v in zip(weights, values)]
    outs = []
    for mix in mixed:
        out = mix[:QWIN]
        for h in range(1, AH):
            out = jnp.where(lane_head == h, mix[h * QWIN : (h + 1) * QWIN], out)
        outs.append(out.astype(BF16))
    return outs


def local_body(
    offsets,
    normed_ref,
    wqkv_ref,
    bias_ref,
    token_bias_hbm,
    mask_hbm,
    q_ref,
    k_ref,
    v_ref,
    att_ref,
    token_bias_ref,
    mask_ref,
    sems,
):
    copies = fetch(sems, (mask_hbm, mask_ref), *quarters(token_bias_hbm, token_bias_ref))
    rows, width = normed_ref.shape
    qkv = dot(normed_ref[...], wqkv_ref[...]).astype(BF16)
    q_ref[...] = qkv[:, :width]
    for n, ref in enumerate((k_ref, v_ref)):
        ref[:rows, :] = qkv[:, (n + 1) * width : (n + 2) * width].astype(F32)
        ref[rows:, :] = jnp.zeros((AHEAD, width), F32)
    windows = rows // QWIN
    skip = BEHIND // QWIN
    stop = windows - (AHEAD - QWIN) // QWIN
    for part in (slice(0, skip * QWIN), slice(stop * QWIN, rows)):
        att_ref[part, :] = jnp.zeros((part.stop - part.start, width), BF16)
    at = [slice(m * QWIN, (m + 1) * QWIN) for m in range(skip, stop)]
    base = [m * QWIN + offsets[0, m] for m in range(skip, stop)]
    outs = windows_of(
        [q_ref[a, :].astype(F32) for a in at],
        [k_ref[pl.ds(b, KWIN), :].astype(BF16) for b in base],
        [v_ref[pl.ds(b, KWIN), :].astype(BF16) for b in base],
        [bias_ref[:, a, :].reshape(AH * QWIN, KWIN) for a in at],
        None,
    )
    for a, out in zip(at, outs):
        att_ref[a, :] = out
    for copy in copies:
        copy.wait()


def atoms_body(
    half,
    info,
    offsets,
    token_ref,
    start_ref,
    q_ref,
    k_ref,
    v_ref,
    pair_ref,
    odd_ref,
    att_ref,
    bias_ref,
    wout_ref,
    wagg_ref,
    wqkv_ref,
    wgate_hbm,
    wback_hbm,
    mid_ref,
    own_ref,
    pair_out,
    odd_out,
    hot_ref,
    living_ref,
    wgate_ref,
    wback_ref,
    k_ext,
    v_ext,
    att,
    sems,
):
    copies = fetch(sems, (wback_hbm, wback_ref), *quarters(wgate_hbm, wgate_ref))
    rows, width = start_ref.shape
    live, me, last = info[0], info[1], info[2]
    even = me % 2 == 0
    pair = dot(pair_ref[...], wqkv_ref[:, width:]).astype(BF16).astype(F32)
    odd = dot(odd_ref[...], wqkv_ref[:, width:]).astype(BF16).astype(F32)
    for n, (ref, ext) in enumerate(((k_ref, k_ext), (v_ref, v_ext))):
        at = slice(n * width, (n + 1) * width)
        ext[:BEHIND, :] = jnp.where(even, odd[:BEHIND, at], pair[:BEHIND, at])
        ext[BEHIND : BEHIND + rows + AHEAD, :] = ref[...]
        ext[pl.ds(BEHIND + live, AHEAD), :] = jnp.where(even, pair[:, at], odd[:, at])
    low = jnp.where(me > 0, 0, BEHIND)
    high = BEHIND + live + jnp.where(me < last, AHEAD, 0)
    att[...] = att_ref[...]
    windows = rows // QWIN
    tails = AHEAD // QWIN
    first = jnp.minimum((live - BEHIND) // QWIN, windows - tails)
    chosen = list(range(BEHIND // QWIN)) + [first + n for n in range(tails)]
    at = [pl.ds(pl.multiple_of(m * QWIN, QWIN), QWIN) for m in chosen]
    base = [BEHIND + QWIN * m + offsets[0, m] for m in chosen]
    slots = [b + iota((1, KWIN), 1) for b in base]
    outs = windows_of(
        [q_ref[a, :].astype(F32) for a in at],
        [k_ext[pl.ds(b, KWIN), :].astype(BF16) for b in base],
        [v_ext[pl.ds(b, KWIN), :].astype(BF16) for b in base],
        [bias_ref[:, a, :].reshape(AH * QWIN, KWIN) for a in at],
        [(s >= low) & (s < high) for s in slots],
    )
    for a, out in zip(at, outs):
        att[a, :] = out
    mid = start_ref[...] + dot(att[...], wout_ref[...])
    mid_ref[...] = mid
    spread = jnp.maximum(dot(mid.astype(BF16), wagg_ref[...]), 0.0).astype(BF16)
    block_rows = own_ref.shape[0]
    living = iota((1, rows), 1) < live
    living_ref[...] = living.astype(F32)
    relative = token_ref[...] - (me * block_rows - half)
    hot = ((iota((block_rows + 2 * half, rows), 0) == relative) & living).astype(F32)
    hot_ref[...] = jnp.transpose(hot).astype(BF16)
    sums = dot(hot.astype(BF16), spread)
    counts = jnp.sum(hot, axis=1, keepdims=True)
    first = jnp.minimum(counts, 256.0)
    lane = iota((counts.shape[0], 128), 1)
    packed = jnp.where(lane == 0, first, jnp.where(lane == 1, counts - first, 0.0))
    model = wagg_ref.shape[1]
    own_ref[:, :model] = sums[half : half + block_rows]
    own_ref[:, model:] = packed[half : half + block_rows]
    lower = jnp.concatenate([sums[:half], packed[:half]], axis=1)
    upper = jnp.concatenate([sums[half + block_rows :], packed[half + block_rows :]], axis=1)
    pair_out[...] = jnp.where(even, upper, lower).astype(BF16)
    odd_out[...] = jnp.where(even, lower, upper).astype(BF16)
    for copy in copies:
        copy.wait()


def token_body(own_ref, pair_ref, odd_ref, single_ref, in_ref, norm_ref):
    me = lax.axis_index("row")
    even = me % 2 == 0
    model = single_ref.shape[1]
    pair = pair_ref[...].astype(F32)
    odd = odd_ref[...].astype(F32)
    lower = jnp.where(me > 0, jnp.where(even, odd, pair), 0.0)
    upper = jnp.where(me < lax.axis_size("row") - 1, jnp.where(even, pair, odd), 0.0)
    both = own_ref[...] + jnp.concatenate([lower, upper], axis=0)
    count = both[:, model : model + 1] + both[:, model + 1 : model + 2]
    token_in = single_ref[...].astype(F32) + both[:, :model] / jnp.maximum(count, 1.0)
    in_ref[...] = token_in
    norm_ref[...] = normalize(token_in).astype(BF16)


def weights_body(after, wback_ref, wout_hbm, wout_ref, both_ref, sems):
    for copy in fetch(sems, *quarters(wout_hbm, wout_ref)):
        copy.wait()
    both_ref[...] = dot(wout_ref[...], wback_ref[...]).astype(BF16)


def query_body(
    norm_ref,
    in_ref,
    wqkv_ref,
    wgate_ref,
    wback_ref,
    query_ref,
    gate_ref,
    back_ref,
):
    rows, model = norm_ref.shape
    width = model // TH
    group = TH // 2
    span = group * width
    norm = norm_ref[...]
    own = iota((group * rows, span), 0) // rows == iota((group * rows, span), 1) // width
    tq = dot(norm, wqkv_ref[:, :model])
    for g in range(2):
        part = tq[:, g * span : (g + 1) * span]
        stacked = jnp.where(own, jnp.concatenate([part] * group, axis=0), 0.0).astype(BF16)
        wk = wqkv_ref[:, model + g * span : model + (g + 1) * span]
        query_ref[g * group * rows : (g + 1) * group * rows, :] = dot_nt(stacked, wk).astype(BF16)
    gate_ref[...] = jax.nn.sigmoid(dot(norm, wgate_ref[...]))
    back_ref[...] = dot(in_ref[...].astype(BF16), wback_ref[...])


def stage_body(lists, after, bias_ref, mask_ref, out_ref):
    allowed = mask_ref[...] == 1
    heads, rows, _ = bias_ref.shape
    if lists is None:
        for h in range(heads):
            out_ref[0, h * rows : (h + 1) * rows, :] = jnp.where(allowed, bias_ref[h], masked_score)
        return
    me = lax.axis_index("row")
    kind = kind_of(me)
    per = 128 // rows
    lane_block = iota((heads * rows, 128), 1) // rows
    for c in range(len(lists[0])):
        for tile in range(len(lists[0][c]) // per):
            for j in range(per):
                n = tile * per + j
                block = me ^ jnp.where(kind == 0, lists[0][c][n], lists[1][c][n])
                source = pl.ds(pl.multiple_of((block // per) * 128, 128), 128)
                piece = jnp.where((mask_ref[:, source] == 1)[None], bias_ref[:, :, source], masked_score)
                piece = piece.reshape(heads * rows, 128)
                piece = pltpu.roll(piece, ((j + per - block % per) % per) * rows, 1)
                merged = piece if j == 0 else jnp.where(lane_block == j, piece, merged)
            out_ref[c, :, tile * 128 : (tile + 1) * 128] = merged


def part_of(rows, query_ref, keys_ref, bias, wqkv_ref):
    model = query_ref.shape[1]
    width = model // TH
    group = TH // 2
    span = group * width
    keys = keys_ref[...]
    values = dot(keys, wqkv_ref[:, 2 * model :]).astype(BF16)
    lane_head = iota((rows, span), 1) // width

    def by_head(stacked):
        out = jnp.broadcast_to(stacked[:rows], (rows, span))
        for h in range(1, group):
            out = jnp.where(lane_head == h, stacked[h * rows : (h + 1) * rows], out)
        return out

    found = []
    for g in range(2):
        at = slice(g * group * rows, (g + 1) * group * rows)
        scores = dot_nt(query_ref[at, :], keys) * (1.0 / width**0.5) + bias(at)
        top = jnp.max(scores, axis=-1, keepdims=True)
        scores = jnp.exp(scores - top)
        total = jnp.sum(scores, axis=-1, keepdims=True)
        mixed = dot(scores.astype(BF16), values[:, g * span : (g + 1) * span])
        found.append((by_head(top), by_head(total), by_head(mixed)))
    return [jnp.concatenate([found[0][n], found[1][n]], axis=1) for n in range(3)]


def part_body(chunk, query_ref, keys_ref, bias_ref, wqkv_ref, part_ref):
    found = part_of(part_ref.shape[1], query_ref, keys_ref, lambda at: bias_ref[chunk, at, :], wqkv_ref)
    for n in range(3):
        part_ref[n] = found[n]


def attend_body(
    half,
    chunk,
    base_ref,
    query_ref,
    gate_ref,
    keys_ref,
    bias_ref,
    wqkv_ref,
    both_ref,
    *rest,
):
    parts, (gated_ref, back_ref, pair_out, odd_out) = rest[:-4], rest[-4:]
    rows, _ = gate_ref.shape
    even = lax.axis_index("row") % 2 == 0
    found = part_of(rows, query_ref, keys_ref, lambda at: bias_ref[chunk, at, :], wqkv_ref)
    found = [[part[n] for n in range(3)] for part in parts] + [found]
    top = functools.reduce(jnp.maximum, [f[0] for f in found])
    shares = [jnp.exp(f[0] - top) for f in found]
    total = sum(f[1] * w for f, w in zip(found, shares))
    mixed = sum(f[2] * w for f, w in zip(found, shares))
    gated = (gate_ref[...] * (mixed / total)).astype(BF16)
    gated_ref[...] = gated
    back = base_ref[...] + dot(gated, both_ref[...])
    back_ref[...] = back.astype(BF16)
    lower, upper = back[:half], back[rows - half :]
    pair_out[...] = jnp.where(even, upper, lower).astype(BF16)
    odd_out[...] = jnp.where(even, lower, upper).astype(BF16)


def out_body(in_ref, gated_ref, wout_ref, out_ref):
    out_ref[...] = (in_ref[...] + dot(gated_ref[...], wout_ref[...])).astype(BF16)


def final_body(living_ref, hot_ref, mid_ref, back_ref, pair_ref, odd_ref, wpos_ref, pos_ref, noise_ref, out_ref):
    even = lax.axis_index("row") % 2 == 0
    pair = pair_ref[...].astype(F32)
    odd = odd_ref[...].astype(F32)
    near = jnp.concatenate(
        [jnp.where(even, odd, pair), back_ref[...].astype(F32), jnp.where(even, pair, odd)], axis=0
    ).astype(BF16)
    last = mid_ref[...] + dot(hot_ref[...], near)
    update = dot_nt(wpos_ref[...], normalize(last).astype(BF16))
    noisy = pos_ref[...] + noise_level * noise_ref[...]
    out_ref[...] = jnp.where(living_ref[...] > 0.0, skip_scale * noisy + output_scale * update, 0.0)


def exchange(pair, odd, groups, count):
    near = [(i, i ^ 1) for i in range(count) if i ^ 1 < count]
    odds = [(i, i + 1) for i in range(1, count - 1, 2)]
    far = [(g * count + a, g * count + b) for g in range(groups) for a, b in odds + [(b, a) for a, b in odds]]
    if groups % 2 == 0 and count % 2 == 0:
        far += [(g * count + i, (g ^ 1) * count + i) for g in range(groups) for i in (0, count - 1)]
    odd = lax.ppermute(odd, ("grp", "row"), far)
    pair = lax.ppermute(pair, "row", near)
    return pair, odd


def kind_of(i):
    return (i ^ (i >> 1) ^ (i >> 2)) & 1


def gather_plan(count):
    bits = [1 << b for b in range(count.bit_length() - 1, 0, -1) if 1 << b < count]
    steps = [[b | 1, b | 1] for b in bits]
    high, low = bits[-2] | 1, bits[-1] | 1
    steps[-2:] = [[high, low], [low, high]]
    lists = [[0], [0]]
    for step in steps[:-1]:
        lists = [lists[p] + [x ^ step[p] for x in lists[p ^ kind_of(step[p])]] for p in range(2)]
    near = [[1 ^ x for x in lists[1 - p]] for p in range(2)]
    last = [[x ^ steps[-1][p] for x in lists[p]] for p in range(2)]
    end = [[1 ^ x for x in last[1 - p]] for p in range(2)]
    return steps, [[lists[p], near[p], last[p], end[p]] for p in range(2)]


def swap(value, count, step):
    return lax.ppermute(value, "row", [(i, i ^ step[kind_of(i)]) for i in range(count)])


def on_device(
    groups,
    count,
    positions,
    noise,
    atom_single,
    atom_token,
    atom_counts,
    window_offsets,
    atom_bias,
    token_single,
    token_bias,
    pair_mask,
    w_coord,
    w_atom_qkv,
    w_atom_out,
    w_agg,
    w_tok_qkv,
    w_tok_gate,
    w_tok_out,
    w_back,
    w_pos,
):
    rows, width = atom_single.shape
    block_rows, model = token_single.shape
    half = block_rows // 2
    info_shape = shape((8,), jnp.int32)
    info, start, normed, pair, odd, offsets, tokens, bias, wout, wagg, wqkv = call(
        embed_body,
        [
            info_shape,
            shape((rows, width), F32),
            shape((rows, width), BF16),
            shape((AHEAD, width), BF16),
            shape((AHEAD, width), BF16),
            shape((1, rows // QWIN), jnp.int32),
            shape((1, rows), jnp.int32),
            shape(atom_bias.shape, F32),
            shape(w_atom_out.shape, BF16),
            shape(w_agg.shape, BF16),
            shape(w_atom_qkv.shape, BF16),
        ],
        [HBM] * 11,
        [
            pltpu.SMEM((1, 1), jnp.int32),
            pltpu.VMEM(positions.shape, F32),
            pltpu.VMEM(noise.shape, F32),
            pltpu.VMEM(atom_single.shape, BF16),
            pltpu.VMEM(w_coord.shape, F32),
            pltpu.VMEM((rows + AHEAD, width), F32),
            pltpu.SemaphoreType.DMA((14,)),
        ],
        out_specs=[SMEM] + [VMEM] * 4 + [SMEM] + [VMEM] * 5,
    )(
        atom_counts[None],
        positions,
        noise,
        atom_single,
        w_coord,
        w_atom_qkv,
        window_offsets[None],
        atom_token,
        atom_bias,
        w_atom_out,
        w_agg,
    )
    pair, odd = exchange(pair, odd, groups, count)
    q, keys, values, att, raw, mask = call(
        local_body,
        [
            shape((rows, width), BF16),
            shape((rows + AHEAD, width), F32),
            shape((rows + AHEAD, width), F32),
            shape((rows, width), BF16),
            shape(token_bias.shape, F32),
            shape(pair_mask.shape, jnp.int32),
        ],
        [SMEM] + [VMEM] * 3 + [HBM] * 2,
        [pltpu.SemaphoreType.DMA((5,))],
        flops=10**9,
    )(offsets, normed, wqkv, bias, token_bias, pair_mask)
    packed = model + 128
    mid, own, pair, odd, hot, living, wgate, wback = call(
        functools.partial(atoms_body, half),
        [
            shape((rows, width), F32),
            shape((block_rows, packed), F32),
            shape((half, packed), BF16),
            shape((half, packed), BF16),
            shape((rows, block_rows + 2 * half), BF16),
            shape((1, rows), F32),
            shape(w_tok_gate.shape, BF16),
            shape(w_back.shape, BF16),
        ],
        [SMEM, SMEM] + [VMEM] * 12 + [HBM] * 2,
        [pltpu.VMEM((BEHIND + rows + AHEAD, width), F32)] * 2
        + [pltpu.VMEM((rows, width), BF16), pltpu.SemaphoreType.DMA((5,))],
    )(info, offsets, tokens, start, q, keys, values, pair, odd, att, bias, wout, wagg, wqkv, w_tok_gate, w_back)
    pair, odd = exchange(pair, odd, groups, count)
    wout, both = call(
        weights_body,
        [shape(w_tok_out.shape, BF16), shape(w_back.shape, BF16)],
        [VMEM, VMEM, HBM],
        [pltpu.SemaphoreType.DMA((4,))],
        flops=10**9,
    )(own, wback, w_tok_out)
    odd, wout, both = lax.optimization_barrier((odd, wout, both))
    token_in, norm = call(
        token_body, [shape((block_rows, model), F32), shape((block_rows, model), BF16)], [VMEM] * 4
    )(own, pair, odd, token_single)

    doubling = count & (count - 1) == 0 and count >= 16 and 128 % block_rows == 0
    steps, lists = gather_plan(count) if doubling else ([], None)
    chunks = 4 if doubling else 1
    span = count * block_rows // chunks

    def query(seen):
        return call(
            query_body,
            [
                shape((TH * block_rows, model), BF16),
                shape((block_rows, model), F32),
                shape((block_rows, width), F32),
            ],
            [VMEM] * 5,
            flops=10**9,
        )(seen, token_in, w_tok_qkv, wgate, wback)

    def stage(seen, bias, mask):
        return call(
            functools.partial(stage_body, lists),
            [shape((chunks, TH * block_rows, span), F32)],
            [VMEM] * 3,
            flops=10**9,
        )(seen, bias, mask)[0]

    def part(chunk, seen):
        return call(
            functools.partial(part_body, chunk),
            [shape((3, block_rows, model), F32)],
            [VMEM] * 4,
            flops=10**9,
        )(query_rows, seen, score_bias, w_tok_qkv)[0]

    if doubling:
        held = norm
        for n, step in enumerate(steps[:-1]):
            arrived = swap(held, count, step)
            if n == 0:
                arrived, (query_rows, gate, base) = lax.optimization_barrier((arrived, query(norm)))
            if n == 1:
                arrived, score_bias = lax.optimization_barrier((arrived, stage(held, raw, mask)))
            held = jnp.concatenate([held, arrived], axis=0)
        last = swap(held, count, steps[-1])
        near = swap(held, count, [1, 1])
        parts = [part(0, held), part(1, near)]
        last, parts = lax.optimization_barrier((last, parts))
        end = swap(last, count, [1, 1])
        parts = parts + [part(2, last)]
    else:
        end = lax.all_gather(norm, "row", axis=0, tiled=True)
        query_rows, gate, base = query(norm)
        score_bias = stage(norm, raw, mask)
        parts = []
    gated, back, pair, odd = call(
        functools.partial(attend_body, half, chunks - 1),
        [
            shape((block_rows, model), BF16),
            shape((block_rows, width), BF16),
            shape((half, width), BF16),
            shape((half, width), BF16),
        ],
        [VMEM] * (7 + len(parts)),
    )(base, query_rows, gate, end, score_bias, w_tok_qkv, both, *parts)
    pair, odd = exchange(pair, odd, groups, count)
    (token_out,) = call(
        out_body, [shape((block_rows, model), BF16)], [VMEM] * 3, flops=10**9
    )(token_in, gated, wout)
    odd, token_out = lax.optimization_barrier((odd, token_out))
    (denoised,) = call(
        final_body, [shape(positions.shape, F32)], [VMEM] * 9
    )(living, hot, mid, back, pair, odd, w_pos, positions, noise)
    return (denoised, token_out)


def solution(mesh):
    placed = (
        P(None, ("grp", "row")),
        P(None, ("grp", "row")),
        P(("grp", "row"), None),
        P(("grp", "row")),
        P(("grp", "row")),
        P(("grp", "row")),
        P(None, ("grp", "row"), None),
        P(("grp", "row"), None),
        P(None, ("grp", "row"), None),
        P(("grp", "row"), None),
    ) + (P(),) * 9
    return jax.shard_map(
        functools.partial(on_device, mesh.shape["grp"], mesh.shape["row"]),
        mesh=mesh,
        in_specs=placed,
        out_specs=(P(None, ("grp", "row")), P(("grp", "row"), None)),
        check_vma=False,
    )
```

```python
import functools

import jax
import jax.numpy as jnp
from jax import lax
from jax.experimental import pallas as pl
from jax.experimental.pallas import tpu as pltpu
from jax.sharding import PartitionSpec as P

AH = 4
TH = 16
QWIN = 32
KWIN = 128
BEHIND = KWIN // 2
AHEAD = KWIN - QWIN

noise_level = 2.0
input_scale = 1.0 / 5.0**0.5
skip_scale = 1.0 / 5.0
output_scale = 2.0 / 5.0**0.5
masked_score = -1e30

F32 = jnp.float32
BF16 = jnp.bfloat16
NT = (((1,), (1,)), ((), ()))


def dot(a, b):
    return jnp.dot(a, b, preferred_element_type=F32)


def dot_nt(a, b):
    return lax.dot_general(a, b, NT, preferred_element_type=F32)


def normalize(values):
    center = values - jnp.mean(values, axis=-1, keepdims=True)
    spread = jnp.mean(center * center, axis=-1, keepdims=True)
    return center * lax.rsqrt(spread + 1e-05)


def iota(shape, dim):
    return lax.broadcasted_iota(jnp.int32, shape, dim)


VMEM = pl.BlockSpec(memory_space=pltpu.VMEM)
SMEM = pl.BlockSpec(memory_space=pltpu.SMEM)
HBM = pl.BlockSpec(memory_space=pltpu.HBM)


def call(body, outs, specs, scratch=(), flops=10**7, limit=8, out_specs=None):
    moved = sum(o.size * o.dtype.itemsize for o in outs)
    held = [spec is HBM for spec in specs]
    run = pl.pallas_call(
        body,
        out_shape=tuple(outs),
        in_specs=specs,
        out_specs=tuple(out_specs or [VMEM] * len(outs)),
        scratch_shapes=list(scratch),
        cost_estimate=pl.CostEstimate(flops=flops, bytes_accessed=moved, transcendentals=0),
        compiler_params=pltpu.CompilerParams(vmem_limit_bytes=limit * 2**20),
    )
    return lambda *args: run(*[pltpu.with_memory_space_constraint(x, pltpu.HBM) if h and x.size > 1 else x for x, h in zip(args, held)])


def shape(dims, dtype):
    return jax.ShapeDtypeStruct(dims, dtype)


def fetch(sems, *moves):
    copies = [pltpu.make_async_copy(src, dst, sems.at[n]) for n, (src, dst) in enumerate(moves)]
    for copy in copies:
        copy.start()
    return copies


def quarters(src, dst):
    step = src.shape[0] // 4
    return [(src.at[pl.ds(n * step, step)], dst.at[pl.ds(n * step, step)]) for n in range(4)]


def embed_body(
    counts_hbm,
    pos_hbm,
    noise_hbm,
    single_hbm,
    wc_hbm,
    wqkv_hbm,
    offsets_hbm,
    token_hbm,
    bias_hbm,
    wout_hbm,
    wagg_hbm,
    info_ref,
    start_ref,
    normed_ref,
    pair_ref,
    odd_ref,
    offsets_ref,
    token_ref,
    bias_ref,
    wout_ref,
    wagg_ref,
    wqkv_ref,
    counts_ref,
    pos_ref,
    noise_ref,
    single_ref,
    wc_ref,
    wide_ref,
    sems,
):
    copies = fetch(
        sems,
        (pos_hbm, pos_ref),
        (noise_hbm, noise_ref),
        (wc_hbm, wc_ref),
        (single_hbm, single_ref),
        (counts_hbm, counts_ref),
        (wqkv_hbm, wqkv_ref),
        (offsets_hbm, offsets_ref),
        (token_hbm, token_ref.at[0]),
        *quarters(bias_hbm, bias_ref),
        (wout_hbm, wout_ref),
        (wagg_hbm, wagg_ref),
    )
    rows, width = single_ref.shape
    wide_ref[rows:, :] = jnp.zeros((AHEAD, width), F32)
    for copy in copies[:3]:
        copy.wait()
    scaled = input_scale * (pos_ref[...] + noise_level * noise_ref[...])
    padded = jnp.concatenate([scaled, jnp.zeros((5, rows), F32)], axis=0)
    across = jnp.transpose(padded)
    copies[3].wait()
    start = single_ref[...].astype(F32)
    for c in range(3):
        start = start + across[:, c : c + 1] * wc_ref[c : c + 1, :]
    start_ref[...] = start
    normed = normalize(start)
    normed_ref[...] = normed.astype(BF16)
    wide_ref[:rows, :] = normed
    copies[4].wait()
    live = counts_ref[0, 0]
    me = lax.axis_index("row")
    info_ref[0] = live
    info_ref[1] = me
    info_ref[2] = lax.axis_size("row") - 1
    tail = live - BEHIND
    even = me % 2 == 0
    pair_ref[...] = wide_ref[pl.ds(jnp.where(even, tail, 0), AHEAD), :].astype(BF16)
    odd_ref[...] = wide_ref[pl.ds(jnp.where(even, 0, tail), AHEAD), :].astype(BF16)
    for copy in copies[5:]:
        copy.wait()


def windows_of(queries, keys, values, biases, masks):
    width = queries[0].shape[1]
    depth = width // AH
    rows = AH * QWIN
    own_head = iota((rows, width), 0) // QWIN == iota((rows, width), 1) // depth
    lane_head = iota((QWIN, width), 1) // depth
    stacked = [jnp.where(own_head, jnp.concatenate([q] * AH, axis=0), 0.0).astype(BF16) for q in queries]
    scores = [dot_nt(q, k) * (1.0 / depth**0.5) + b for q, k, b in zip(stacked, keys, biases)]
    if masks is not None:
        scores = [jnp.where(m, s, masked_score) for m, s in zip(masks, scores)]
    tops = [jnp.max(s, axis=-1, keepdims=True) for s in scores]
    scores = [jnp.exp(s - t) for s, t in zip(scores, tops)]
    shares = [1.0 / jnp.sum(s, axis=-1, keepdims=True) for s in scores]
    weights = [(s * r).astype(BF16) for s, r in zip(scores, shares)]
    mixed = [dot(w, v) for w, v in zip(weights, values)]
    outs = []
    for mix in mixed:
        out = mix[:QWIN]
        for h in range(1, AH):
            out = jnp.where(lane_head == h, mix[h * QWIN : (h + 1) * QWIN], out)
        outs.append(out.astype(BF16))
    return outs


def local_body(offsets, normed_ref, wqkv_ref, bias_ref, q_ref, k_ref, v_ref, att_ref):
    rows, width = normed_ref.shape
    qkv = dot(normed_ref[...], wqkv_ref[...]).astype(BF16)
    q_ref[...] = qkv[:, :width]
    for n, ref in enumerate((k_ref, v_ref)):
        ref[:rows, :] = qkv[:, (n + 1) * width : (n + 2) * width].astype(F32)
        ref[rows:, :] = jnp.zeros((AHEAD, width), F32)
    windows = rows // QWIN
    skip = BEHIND // QWIN
    stop = windows - (AHEAD - QWIN) // QWIN
    for part in (slice(0, skip * QWIN), slice(stop * QWIN, rows)):
        att_ref[part, :] = jnp.zeros((part.stop - part.start, width), BF16)
    at = [slice(m * QWIN, (m + 1) * QWIN) for m in range(skip, stop)]
    base = [m * QWIN + offsets[0, m] for m in range(skip, stop)]
    outs = windows_of(
        [q_ref[a, :].astype(F32) for a in at],
        [k_ref[pl.ds(b, KWIN), :].astype(BF16) for b in base],
        [v_ref[pl.ds(b, KWIN), :].astype(BF16) for b in base],
        [bias_ref[:, a, :].reshape(AH * QWIN, KWIN) for a in at],
        None,
    )
    for a, out in zip(at, outs):
        att_ref[a, :] = out


def atoms_body(
    half,
    info,
    offsets,
    token_ref,
    start_ref,
    q_ref,
    k_ref,
    v_ref,
    pair_ref,
    odd_ref,
    att_ref,
    bias_ref,
    wout_ref,
    wagg_ref,
    wqkv_ref,
    mid_ref,
    own_ref,
    pair_out,
    odd_out,
    hot_ref,
    living_ref,
    k_ext,
    v_ext,
    att,
):
    rows, width = start_ref.shape
    live, me, last = info[0], info[1], info[2]
    even = me % 2 == 0
    pair = dot(pair_ref[...], wqkv_ref[:, width:]).astype(BF16).astype(F32)
    odd = dot(odd_ref[...], wqkv_ref[:, width:]).astype(BF16).astype(F32)
    for n, (ref, ext) in enumerate(((k_ref, k_ext), (v_ref, v_ext))):
        at = slice(n * width, (n + 1) * width)
        ext[:BEHIND, :] = jnp.where(even, odd[:BEHIND, at], pair[:BEHIND, at])
        ext[BEHIND : BEHIND + rows + AHEAD, :] = ref[...]
        ext[pl.ds(BEHIND + live, AHEAD), :] = jnp.where(even, pair[:, at], odd[:, at])
    low = jnp.where(me > 0, 0, BEHIND)
    high = BEHIND + live + jnp.where(me < last, AHEAD, 0)
    att[...] = att_ref[...]
    windows = rows // QWIN
    tails = AHEAD // QWIN
    first = jnp.minimum((live - BEHIND) // QWIN, windows - tails)
    chosen = list(range(BEHIND // QWIN)) + [first + n for n in range(tails)]
    at = [pl.ds(pl.multiple_of(m * QWIN, QWIN), QWIN) for m in chosen]
    base = [BEHIND + QWIN * m + offsets[0, m] for m in chosen]
    slots = [b + iota((1, KWIN), 1) for b in base]
    outs = windows_of(
        [q_ref[a, :].astype(F32) for a in at],
        [k_ext[pl.ds(b, KWIN), :].astype(BF16) for b in base],
        [v_ext[pl.ds(b, KWIN), :].astype(BF16) for b in base],
        [bias_ref[:, a, :].reshape(AH * QWIN, KWIN) for a in at],
        [(s >= low) & (s < high) for s in slots],
    )
    for a, out in zip(at, outs):
        att[a, :] = out
    mid = start_ref[...] + dot(att[...], wout_ref[...])
    mid_ref[...] = mid
    spread = jnp.maximum(dot(mid.astype(BF16), wagg_ref[...]), 0.0).astype(BF16)
    block_rows = own_ref.shape[0]
    living = iota((1, rows), 1) < live
    living_ref[...] = living.astype(F32)
    relative = token_ref[...] - (me * block_rows - half)
    hot = ((iota((block_rows + 2 * half, rows), 0) == relative) & living).astype(F32)
    hot_ref[...] = jnp.transpose(hot).astype(BF16)
    sums = dot(hot.astype(BF16), spread)
    counts = jnp.sum(hot, axis=1, keepdims=True)
    first = jnp.minimum(counts, 256.0)
    lane = iota((counts.shape[0], 128), 1)
    packed = jnp.where(lane == 0, first, jnp.where(lane == 1, counts - first, 0.0))
    model = wagg_ref.shape[1]
    own_ref[:, :model] = sums[half : half + block_rows]
    own_ref[:, model:] = packed[half : half + block_rows]
    lower = jnp.concatenate([sums[:half], packed[:half]], axis=1)
    upper = jnp.concatenate([sums[half + block_rows :], packed[half + block_rows :]], axis=1)
    pair_out[...] = jnp.where(even, upper, lower).astype(BF16)
    odd_out[...] = jnp.where(even, lower, upper).astype(BF16)


def token_body(own_ref, pair_ref, odd_ref, single_ref, in_ref, norm_ref):
    me = lax.axis_index("row")
    even = me % 2 == 0
    model = single_ref.shape[1]
    pair = pair_ref[...].astype(F32)
    odd = odd_ref[...].astype(F32)
    lower = jnp.where(me > 0, jnp.where(even, odd, pair), 0.0)
    upper = jnp.where(me < lax.axis_size("row") - 1, jnp.where(even, pair, odd), 0.0)
    both = own_ref[...] + jnp.concatenate([lower, upper], axis=0)
    count = both[:, model : model + 1] + both[:, model + 1 : model + 2]
    token_in = single_ref[...].astype(F32) + both[:, :model] / jnp.maximum(count, 1.0)
    in_ref[...] = token_in
    norm_ref[...] = normalize(token_in).astype(BF16)


def bias_body(after, bias_hbm, mask_hbm, bias_ref, mask_ref, sems):
    for copy in fetch(sems, (mask_hbm, mask_ref), *quarters(bias_hbm, bias_ref)):
        copy.wait()


def query_body(norm_ref, wqkv_ref, query_ref):
    rows, model = norm_ref.shape
    width = model // TH
    group = TH // 2
    span = group * width
    own = iota((group * rows, span), 0) // rows == iota((group * rows, span), 1) // width
    tq = dot(norm_ref[...], wqkv_ref[:, :model])
    for g in range(2):
        part = tq[:, g * span : (g + 1) * span]
        stacked = jnp.where(own, jnp.concatenate([part] * group, axis=0), 0.0).astype(BF16)
        wk = wqkv_ref[:, model + g * span : model + (g + 1) * span]
        query_ref[g * group * rows : (g + 1) * group * rows, :] = dot_nt(stacked, wk).astype(BF16)


def stage_body(lists, after, norm_ref, bias_ref, mask_ref, wgate_hbm, out_ref, gate_ref, wgate_ref, sems):
    copies = fetch(sems, *quarters(wgate_hbm, wgate_ref))

    @pl.when(lax.axis_index("row") >= 0)
    def _():
        heads, rows, _ = bias_ref.shape
        if lists is None:
            allowed = mask_ref[...] == 1
            for h in range(heads):
                out_ref[0, h * rows : (h + 1) * rows, :] = jnp.where(allowed, bias_ref[h], masked_score)
        else:
            me = lax.axis_index("row")
            kind = kind_of(me)
            per = 128 // rows
            lane_block = iota((heads * rows, 128), 1) // rows
            for c in range(len(lists[0])):
                for tile in range(len(lists[0][c]) // per):
                    for j in range(per):
                        n = tile * per + j
                        block = me ^ jnp.where(kind == 0, lists[0][c][n], lists[1][c][n])
                        source = pl.ds(pl.multiple_of((block // per) * 128, 128), 128)
                        piece = jnp.where((mask_ref[:, source] == 1)[None], bias_ref[:, :, source], masked_score)
                        piece = piece.reshape(heads * rows, 128)
                        piece = pltpu.roll(piece, ((j + per - block % per) % per) * rows, 1)
                        merged = piece if j == 0 else jnp.where(lane_block == j, piece, merged)
                    out_ref[c, :, tile * 128 : (tile + 1) * 128] = merged

    for copy in copies:
        copy.wait()
    gate_ref[...] = jax.nn.sigmoid(dot(norm_ref[...], wgate_ref[...]))


def weights_of(copies, in_ref, wout_ref, wback_ref, both_ref, base_ref):
    for copy in copies:
        copy.wait()
    both_ref[...] = dot(wout_ref[...], wback_ref[...]).astype(BF16)
    base_ref[...] = dot(in_ref[...].astype(BF16), wback_ref[...])


def weights_body(in_ref, wout_hbm, wback_hbm, wout_ref, both_ref, base_ref, wback_ref, sems):
    copies = fetch(sems, (wback_hbm, wback_ref), *quarters(wout_hbm, wout_ref))
    weights_of(copies, in_ref, wout_ref, wback_ref, both_ref, base_ref)


def part_of(rows, query_ref, keys_ref, bias, wqkv_ref):
    model = query_ref.shape[1]
    width = model // TH
    group = TH // 2
    span = group * width
    keys = keys_ref[...]
    values = dot(keys, wqkv_ref[:, 2 * model :]).astype(BF16)
    lane_head = iota((rows, span), 1) // width

    def by_head(stacked):
        out = jnp.broadcast_to(stacked[:rows], (rows, span))
        for h in range(1, group):
            out = jnp.where(lane_head == h, stacked[h * rows : (h + 1) * rows], out)
        return out

    found = []
    for g in range(2):
        at = slice(g * group * rows, (g + 1) * group * rows)
        scores = dot_nt(query_ref[at, :], keys) * (1.0 / width**0.5) + bias(at)
        top = jnp.max(scores, axis=-1, keepdims=True)
        scores = jnp.exp(scores - top)
        total = jnp.sum(scores, axis=-1, keepdims=True)
        mixed = dot(scores.astype(BF16), values[:, g * span : (g + 1) * span])
        found.append((by_head(top), by_head(total), by_head(mixed)))
    return [jnp.concatenate([found[0][n], found[1][n]], axis=1) for n in range(3)]


def part_body(chunk, query_ref, keys_ref, bias_ref, wqkv_ref, part_ref):
    found = part_of(part_ref.shape[1], query_ref, keys_ref, lambda at: bias_ref[chunk, at, :], wqkv_ref)
    for n in range(3):
        part_ref[n] = found[n]


def second_body(
    chunk,
    query_ref,
    keys_ref,
    bias_ref,
    wqkv_ref,
    in_ref,
    wout_hbm,
    wback_hbm,
    part_ref,
    wout_ref,
    both_ref,
    base_ref,
    wback_ref,
    sems,
):
    copies = fetch(sems, (wback_hbm, wback_ref), *quarters(wout_hbm, wout_ref))

    @pl.when(lax.axis_index("row") >= 0)
    def _():
        part_body(chunk, query_ref, keys_ref, bias_ref, wqkv_ref, part_ref)

    weights_of(copies, in_ref, wout_ref, wback_ref, both_ref, base_ref)


def attend_body(
    half,
    chunk,
    base_ref,
    query_ref,
    gate_ref,
    keys_ref,
    bias_ref,
    wqkv_ref,
    both_ref,
    *rest,
):
    parts, (gated_ref, back_ref, pair_out, odd_out) = rest[:-4], rest[-4:]
    rows, _ = gate_ref.shape
    even = lax.axis_index("row") % 2 == 0
    found = part_of(rows, query_ref, keys_ref, lambda at: bias_ref[chunk, at, :], wqkv_ref)
    found = [[part[n] for n in range(3)] for part in parts] + [found]
    top = functools.reduce(jnp.maximum, [f[0] for f in found])
    shares = [jnp.exp(f[0] - top) for f in found]
    total = sum(f[1] * w for f, w in zip(found, shares))
    mixed = sum(f[2] * w for f, w in zip(found, shares))
    gated = (gate_ref[...] * (mixed / total)).astype(BF16)
    gated_ref[...] = gated
    back = base_ref[...] + dot(gated, both_ref[...])
    back_ref[...] = back.astype(BF16)
    lower, upper = back[:half], back[rows - half :]
    pair_out[...] = jnp.where(even, upper, lower).astype(BF16)
    odd_out[...] = jnp.where(even, lower, upper).astype(BF16)


def out_body(in_ref, gated_ref, wout_ref, out_ref):
    out_ref[...] = (in_ref[...] + dot(gated_ref[...], wout_ref[...])).astype(BF16)


def final_body(living_ref, hot_ref, mid_ref, back_ref, pair_ref, odd_ref, wpos_ref, pos_ref, noise_ref, out_ref):
    even = lax.axis_index("row") % 2 == 0
    pair = pair_ref[...].astype(F32)
    odd = odd_ref[...].astype(F32)
    near = jnp.concatenate(
        [jnp.where(even, odd, pair), back_ref[...].astype(F32), jnp.where(even, pair, odd)], axis=0
    ).astype(BF16)
    last = mid_ref[...] + dot(hot_ref[...], near)
    update = dot_nt(wpos_ref[...], normalize(last).astype(BF16))
    noisy = pos_ref[...] + noise_level * noise_ref[...]
    out_ref[...] = jnp.where(living_ref[...] > 0.0, skip_scale * noisy + output_scale * update, 0.0)


def exchange(pair, odd, groups, count):
    near = [(i, i ^ 1) for i in range(count) if i ^ 1 < count]
    odds = [(i, i + 1) for i in range(1, count - 1, 2)]
    far = [(g * count + a, g * count + b) for g in range(groups) for a, b in odds + [(b, a) for a, b in odds]]
    if groups % 2 == 0 and count % 2 == 0:
        far += [(g * count + i, (g ^ 1) * count + i) for g in range(groups) for i in (0, count - 1)]
    odd = lax.ppermute(odd, ("grp", "row"), far)
    pair = lax.ppermute(pair, "row", near)
    return pair, odd


def kind_of(i):
    return (i ^ (i >> 1) ^ (i >> 2)) & 1


def gather_plan(count):
    bits = [1 << b for b in range(count.bit_length() - 1, 0, -1) if 1 << b < count]
    steps = [[b | 1, b | 1] for b in bits]
    high, low = bits[-2] | 1, bits[-1] | 1
    steps[-2:] = [[high, low], [low, high]]
    lists = [[0], [0]]
    for step in steps[:-1]:
        lists = [lists[p] + [x ^ step[p] for x in lists[p ^ kind_of(step[p])]] for p in range(2)]
    near = [[1 ^ x for x in lists[1 - p]] for p in range(2)]
    last = [[x ^ steps[-1][p] for x in lists[p]] for p in range(2)]
    end = [[1 ^ x for x in last[1 - p]] for p in range(2)]
    return steps, [[lists[p], near[p], last[p], end[p]] for p in range(2)]


def swap(value, count, step):
    return lax.ppermute(value, "row", [(i, i ^ step[kind_of(i)]) for i in range(count)])


def on_device(
    groups,
    count,
    positions,
    noise,
    atom_single,
    atom_token,
    atom_counts,
    window_offsets,
    atom_bias,
    token_single,
    token_bias,
    pair_mask,
    w_coord,
    w_atom_qkv,
    w_atom_out,
    w_agg,
    w_tok_qkv,
    w_tok_gate,
    w_tok_out,
    w_back,
    w_pos,
):
    rows, width = atom_single.shape
    block_rows, model = token_single.shape
    half = block_rows // 2
    info_shape = shape((8,), jnp.int32)
    info, start, normed, pair, odd, offsets, tokens, bias, wout, wagg, wqkv = call(
        embed_body,
        [
            info_shape,
            shape((rows, width), F32),
            shape((rows, width), BF16),
            shape((AHEAD, width), BF16),
            shape((AHEAD, width), BF16),
            shape((1, rows // QWIN), jnp.int32),
            shape((1, rows), jnp.int32),
            shape(atom_bias.shape, F32),
            shape(w_atom_out.shape, BF16),
            shape(w_agg.shape, BF16),
            shape(w_atom_qkv.shape, BF16),
        ],
        [HBM] * 11,
        [
            pltpu.SMEM((1, 1), jnp.int32),
            pltpu.VMEM(positions.shape, F32),
            pltpu.VMEM(noise.shape, F32),
            pltpu.VMEM(atom_single.shape, BF16),
            pltpu.VMEM(w_coord.shape, F32),
            pltpu.VMEM((rows + AHEAD, width), F32),
            pltpu.SemaphoreType.DMA((14,)),
        ],
        out_specs=[SMEM] + [VMEM] * 4 + [SMEM] + [VMEM] * 5,
    )(
        atom_counts[None],
        positions,
        noise,
        atom_single,
        w_coord,
        w_atom_qkv,
        window_offsets[None],
        atom_token,
        atom_bias,
        w_atom_out,
        w_agg,
    )
    pair, odd = exchange(pair, odd, groups, count)
    q, keys, values, att = call(
        local_body,
        [
            shape((rows, width), BF16),
            shape((rows + AHEAD, width), F32),
            shape((rows + AHEAD, width), F32),
            shape((rows, width), BF16),
        ],
        [SMEM] + [VMEM] * 3,
        flops=10**9,
    )(offsets, normed, wqkv, bias)
    packed = model + 128
    mid, own, pair, odd, hot, living = call(
        functools.partial(atoms_body, half),
        [
            shape((rows, width), F32),
            shape((block_rows, packed), F32),
            shape((half, packed), BF16),
            shape((half, packed), BF16),
            shape((rows, block_rows + 2 * half), BF16),
            shape((1, rows), F32),
        ],
        [SMEM, SMEM] + [VMEM] * 12,
        [pltpu.VMEM((BEHIND + rows + AHEAD, width), F32)] * 2 + [pltpu.VMEM((rows, width), BF16)],
    )(info, offsets, tokens, start, q, keys, values, pair, odd, att, bias, wout, wagg, wqkv)
    pair, odd = exchange(pair, odd, groups, count)
    raw, mask = call(
        bias_body,
        [shape(token_bias.shape, F32), shape(pair_mask.shape, jnp.int32)],
        [VMEM, HBM, HBM],
        [pltpu.SemaphoreType.DMA((5,))],
        flops=10**9,
    )(own, token_bias, pair_mask)
    odd, raw, mask = lax.optimization_barrier((odd, raw, mask))
    token_in, norm = call(
        token_body, [shape((block_rows, model), F32), shape((block_rows, model), BF16)], [VMEM] * 4
    )(own, pair, odd, token_single)

    doubling = count & (count - 1) == 0 and count >= 16 and 128 % block_rows == 0
    steps, lists = gather_plan(count) if doubling else ([], None)
    chunks = 4 if doubling else 1
    span = count * block_rows // chunks

    def query(seen):
        return call(
            query_body, [shape((TH * block_rows, model), BF16)], [VMEM] * 2, flops=10**9
        )(seen, w_tok_qkv)[0]

    def stage(seen):
        return call(
            functools.partial(stage_body, lists),
            [shape((chunks, TH * block_rows, span), F32), shape((block_rows, model), F32)],
            [VMEM] * 4 + [HBM],
            [pltpu.VMEM(w_tok_gate.shape, BF16), pltpu.SemaphoreType.DMA((4,))],
            flops=10**9,
        )(seen, norm, raw, mask, w_tok_gate)

    made = [shape(w_tok_out.shape, BF16), shape(w_back.shape, BF16), shape((block_rows, width), F32)]
    kept = [pltpu.VMEM(w_back.shape, BF16), pltpu.SemaphoreType.DMA((5,))]

    def second(chunk, seen):
        return call(
            functools.partial(second_body, chunk),
            [shape((3, block_rows, model), F32)] + made,
            [VMEM] * 5 + [HBM] * 2,
            kept,
            flops=10**9,
        )(query_rows, seen, score_bias, w_tok_qkv, token_in, w_tok_out, w_back)

    def part(chunk, seen):
        return call(
            functools.partial(part_body, chunk),
            [shape((3, block_rows, model), F32)],
            [VMEM] * 4,
            flops=10**9,
        )(query_rows, seen, score_bias, w_tok_qkv)[0]

    if doubling:
        held = norm
        for n, step in enumerate(steps[:-1]):
            arrived = swap(held, count, step)
            if n == 0:
                arrived, query_rows = lax.optimization_barrier((arrived, query(norm)))
            if n == 1:
                arrived, (score_bias, gate) = lax.optimization_barrier((arrived, stage(held)))
            held = jnp.concatenate([held, arrived], axis=0)
        last = swap(held, count, steps[-1])
        near = swap(held, count, [1, 1])
        after, wout, both, base = second(1, near)
        parts = [part(0, held), after]
        last, parts, wout, both, base = lax.optimization_barrier((last, parts, wout, both, base))
        end = swap(last, count, [1, 1])
        parts = parts + [part(2, last)]
    else:
        end = lax.all_gather(norm, "row", axis=0, tiled=True)
        query_rows = query(norm)
        score_bias, gate = stage(norm)
        wout, both, base = call(weights_body, made, [VMEM] + [HBM] * 2, kept)(token_in, w_tok_out, w_back)
        parts = []
    gated, back, pair, odd = call(
        functools.partial(attend_body, half, chunks - 1),
        [
            shape((block_rows, model), BF16),
            shape((block_rows, width), BF16),
            shape((half, width), BF16),
            shape((half, width), BF16),
        ],
        [VMEM] * (7 + len(parts)),
    )(base, query_rows, gate, end, score_bias, w_tok_qkv, both, *parts)
    pair, odd = exchange(pair, odd, groups, count)
    (token_out,) = call(
        out_body, [shape((block_rows, model), BF16)], [VMEM] * 3, flops=10**9
    )(token_in, gated, wout)
    odd, token_out = lax.optimization_barrier((odd, token_out))
    (denoised,) = call(
        final_body, [shape(positions.shape, F32)], [VMEM] * 9
    )(living, hot, mid, back, pair, odd, w_pos, positions, noise)
    return (denoised, token_out)


def solution(mesh):
    placed = (
        P(None, ("grp", "row")),
        P(None, ("grp", "row")),
        P(("grp", "row"), None),
        P(("grp", "row")),
        P(("grp", "row")),
        P(("grp", "row")),
        P(None, ("grp", "row"), None),
        P(("grp", "row"), None),
        P(None, ("grp", "row"), None),
        P(("grp", "row"), None),
    ) + (P(),) * 9
    return jax.shard_map(
        functools.partial(on_device, mesh.shape["grp"], mesh.shape["row"]),
        mesh=mesh,
        in_specs=placed,
        out_specs=(P(None, ("grp", "row")), P(("grp", "row"), None)),
        check_vma=False,
    )
```

```python
import functools

import jax
import jax.numpy as jnp
from jax import lax
from jax.experimental import pallas as pl
from jax.experimental.pallas import tpu as pltpu
from jax.sharding import PartitionSpec as P

AH = 4
TH = 16
QWIN = 32
KWIN = 128
BEHIND = KWIN // 2
AHEAD = KWIN - QWIN

noise_level = 2.0
input_scale = 1.0 / 5.0**0.5
skip_scale = 1.0 / 5.0
output_scale = 2.0 / 5.0**0.5
masked_score = -1e30

F32 = jnp.float32
BF16 = jnp.bfloat16
NT = (((1,), (1,)), ((), ()))


def dot(a, b):
    return jnp.dot(a, b, preferred_element_type=F32)


def dot_nt(a, b):
    return lax.dot_general(a, b, NT, preferred_element_type=F32)


def normalize(values):
    center = values - jnp.mean(values, axis=-1, keepdims=True)
    spread = jnp.mean(center * center, axis=-1, keepdims=True)
    return center * lax.rsqrt(spread + 1e-05)


def iota(shape, dim):
    return lax.broadcasted_iota(jnp.int32, shape, dim)


VMEM = pl.BlockSpec(memory_space=pltpu.VMEM)
SMEM = pl.BlockSpec(memory_space=pltpu.SMEM)
HBM = pl.BlockSpec(memory_space=pltpu.HBM)


def call(body, outs, specs, scratch=(), flops=10**7, limit=8, out_specs=None):
    moved = sum(o.size * o.dtype.itemsize for o in outs)
    held = [spec is HBM for spec in specs]
    run = pl.pallas_call(
        body,
        out_shape=tuple(outs),
        in_specs=specs,
        out_specs=tuple(out_specs or [VMEM] * len(outs)),
        scratch_shapes=list(scratch),
        cost_estimate=pl.CostEstimate(flops=flops, bytes_accessed=moved, transcendentals=0),
        compiler_params=pltpu.CompilerParams(vmem_limit_bytes=limit * 2**20),
    )
    return lambda *args: run(*[pltpu.with_memory_space_constraint(x, pltpu.HBM) if h and x.size > 1 else x for x, h in zip(args, held)])


def shape(dims, dtype):
    return jax.ShapeDtypeStruct(dims, dtype)


def fetch(sems, *moves):
    copies = [pltpu.make_async_copy(src, dst, sems.at[n]) for n, (src, dst) in enumerate(moves)]
    for copy in copies:
        copy.start()
    return copies


def quarters(src, dst):
    step = src.shape[0] // 4
    return [(src.at[pl.ds(n * step, step)], dst.at[pl.ds(n * step, step)]) for n in range(4)]


def embed_body(
    counts_hbm,
    pos_hbm,
    noise_hbm,
    single_hbm,
    wc_hbm,
    wqkv_hbm,
    offsets_hbm,
    token_hbm,
    bias_hbm,
    wout_hbm,
    wagg_hbm,
    info_ref,
    start_ref,
    normed_ref,
    pair_ref,
    odd_ref,
    offsets_ref,
    token_ref,
    bias_ref,
    wout_ref,
    wagg_ref,
    wqkv_ref,
    counts_ref,
    pos_ref,
    noise_ref,
    single_ref,
    wc_ref,
    wide_ref,
    sems,
):
    copies = fetch(
        sems,
        (pos_hbm, pos_ref),
        (noise_hbm, noise_ref),
        (wc_hbm, wc_ref),
        (single_hbm, single_ref),
        (counts_hbm, counts_ref),
        (wqkv_hbm, wqkv_ref),
        (offsets_hbm, offsets_ref),
        (token_hbm, token_ref.at[0]),
        *quarters(bias_hbm, bias_ref),
        (wout_hbm, wout_ref),
        (wagg_hbm, wagg_ref),
    )
    rows, width = single_ref.shape
    wide_ref[rows:, :] = jnp.zeros((AHEAD, width), F32)
    for copy in copies[:3]:
        copy.wait()
    scaled = input_scale * (pos_ref[...] + noise_level * noise_ref[...])
    padded = jnp.concatenate([scaled, jnp.zeros((5, rows), F32)], axis=0)
    across = jnp.transpose(padded)
    copies[3].wait()
    start = single_ref[...].astype(F32)
    for c in range(3):
        start = start + across[:, c : c + 1] * wc_ref[c : c + 1, :]
    start_ref[...] = start
    normed = normalize(start)
    normed_ref[...] = normed.astype(BF16)
    wide_ref[:rows, :] = normed
    copies[4].wait()
    live = counts_ref[0, 0]
    me = lax.axis_index("row")
    info_ref[0] = live
    info_ref[1] = me
    info_ref[2] = lax.axis_size("row") - 1
    tail = live - BEHIND
    even = me % 2 == 0
    pair_ref[...] = wide_ref[pl.ds(jnp.where(even, tail, 0), AHEAD), :].astype(BF16)
    odd_ref[...] = wide_ref[pl.ds(jnp.where(even, 0, tail), AHEAD), :].astype(BF16)
    for copy in copies[5:]:
        copy.wait()


def windows_of(queries, keys, values, biases, masks):
    width = queries[0].shape[1]
    depth = width // AH
    rows = AH * QWIN
    own_head = iota((rows, width), 0) // QWIN == iota((rows, width), 1) // depth
    lane_head = iota((QWIN, width), 1) // depth
    stacked = [jnp.where(own_head, jnp.concatenate([q] * AH, axis=0), 0.0).astype(BF16) for q in queries]
    scores = [dot_nt(q, k) * (1.0 / depth**0.5) + b for q, k, b in zip(stacked, keys, biases)]
    if masks is not None:
        scores = [jnp.where(m, s, masked_score) for m, s in zip(masks, scores)]
    tops = [jnp.max(s, axis=-1, keepdims=True) for s in scores]
    scores = [jnp.exp(s - t) for s, t in zip(scores, tops)]
    shares = [1.0 / jnp.sum(s, axis=-1, keepdims=True) for s in scores]
    weights = [(s * r).astype(BF16) for s, r in zip(scores, shares)]
    mixed = [dot(w, v) for w, v in zip(weights, values)]
    outs = []
    for mix in mixed:
        out = mix[:QWIN]
        for h in range(1, AH):
            out = jnp.where(lane_head == h, mix[h * QWIN : (h + 1) * QWIN], out)
        outs.append(out.astype(BF16))
    return outs


def local_body(offsets, normed_ref, wqkv_ref, bias_ref, q_ref, k_ref, v_ref, att_ref):
    rows, width = normed_ref.shape
    qkv = dot(normed_ref[...], wqkv_ref[...]).astype(BF16)
    q_ref[...] = qkv[:, :width]
    for n, ref in enumerate((k_ref, v_ref)):
        ref[:rows, :] = qkv[:, (n + 1) * width : (n + 2) * width].astype(F32)
        ref[rows:, :] = jnp.zeros((AHEAD, width), F32)
    windows = rows // QWIN
    skip = BEHIND // QWIN
    stop = windows - (AHEAD - QWIN) // QWIN
    for part in (slice(0, skip * QWIN), slice(stop * QWIN, rows)):
        att_ref[part, :] = jnp.zeros((part.stop - part.start, width), BF16)
    at = [slice(m * QWIN, (m + 1) * QWIN) for m in range(skip, stop)]
    base = [m * QWIN + offsets[0, m] for m in range(skip, stop)]
    outs = windows_of(
        [q_ref[a, :].astype(F32) for a in at],
        [k_ref[pl.ds(b, KWIN), :].astype(BF16) for b in base],
        [v_ref[pl.ds(b, KWIN), :].astype(BF16) for b in base],
        [bias_ref[:, a, :].reshape(AH * QWIN, KWIN) for a in at],
        None,
    )
    for a, out in zip(at, outs):
        att_ref[a, :] = out


def atoms_body(
    half,
    info,
    offsets,
    token_ref,
    start_ref,
    q_ref,
    k_ref,
    v_ref,
    pair_ref,
    odd_ref,
    att_ref,
    bias_ref,
    wout_ref,
    wagg_ref,
    wqkv_ref,
    mid_ref,
    own_ref,
    pair_out,
    odd_out,
    hot_ref,
    living_ref,
    k_ext,
    v_ext,
    att,
):
    rows, width = start_ref.shape
    live, me, last = info[0], info[1], info[2]
    even = me % 2 == 0
    pair = dot(pair_ref[...], wqkv_ref[:, width:]).astype(BF16).astype(F32)
    odd = dot(odd_ref[...], wqkv_ref[:, width:]).astype(BF16).astype(F32)
    for n, (ref, ext) in enumerate(((k_ref, k_ext), (v_ref, v_ext))):
        at = slice(n * width, (n + 1) * width)
        ext[:BEHIND, :] = jnp.where(even, odd[:BEHIND, at], pair[:BEHIND, at])
        ext[BEHIND : BEHIND + rows + AHEAD, :] = ref[...]
        ext[pl.ds(BEHIND + live, AHEAD), :] = jnp.where(even, pair[:, at], odd[:, at])
    low = jnp.where(me > 0, 0, BEHIND)
    high = BEHIND + live + jnp.where(me < last, AHEAD, 0)
    att[...] = att_ref[...]
    windows = rows // QWIN
    tails = AHEAD // QWIN
    first = jnp.minimum((live - BEHIND) // QWIN, windows - tails)
    chosen = list(range(BEHIND // QWIN)) + [first + n for n in range(tails)]
    at = [pl.ds(pl.multiple_of(m * QWIN, QWIN), QWIN) for m in chosen]
    base = [BEHIND + QWIN * m + offsets[0, m] for m in chosen]
    slots = [b + iota((1, KWIN), 1) for b in base]
    outs = windows_of(
        [q_ref[a, :].astype(F32) for a in at],
        [k_ext[pl.ds(b, KWIN), :].astype(BF16) for b in base],
        [v_ext[pl.ds(b, KWIN), :].astype(BF16) for b in base],
        [bias_ref[:, a, :].reshape(AH * QWIN, KWIN) for a in at],
        [(s >= low) & (s < high) for s in slots],
    )
    for a, out in zip(at, outs):
        att[a, :] = out
    mid = start_ref[...] + dot(att[...], wout_ref[...])
    mid_ref[...] = mid
    spread = jnp.maximum(dot(mid.astype(BF16), wagg_ref[...]), 0.0).astype(BF16)
    block_rows = own_ref.shape[0]
    living = iota((1, rows), 1) < live
    living_ref[...] = living.astype(F32)
    relative = token_ref[...] - (me * block_rows - half)
    hot = ((iota((block_rows + 2 * half, rows), 0) == relative) & living).astype(F32)
    hot_ref[...] = jnp.transpose(hot).astype(BF16)
    sums = dot(hot.astype(BF16), spread)
    counts = jnp.sum(hot, axis=1, keepdims=True)
    first = jnp.minimum(counts, 256.0)
    lane = iota((counts.shape[0], 128), 1)
    packed = jnp.where(lane == 0, first, jnp.where(lane == 1, counts - first, 0.0))
    model = wagg_ref.shape[1]
    own_ref[:, :model] = sums[half : half + block_rows]
    own_ref[:, model:] = packed[half : half + block_rows]
    lower = jnp.concatenate([sums[:half], packed[:half]], axis=1)
    upper = jnp.concatenate([sums[half + block_rows :], packed[half + block_rows :]], axis=1)
    pair_out[...] = jnp.where(even, upper, lower).astype(BF16)
    odd_out[...] = jnp.where(even, lower, upper).astype(BF16)


def token_body(own_ref, pair_ref, odd_ref, single_ref, in_ref, norm_ref):
    me = lax.axis_index("row")
    even = me % 2 == 0
    model = single_ref.shape[1]
    pair = pair_ref[...].astype(F32)
    odd = odd_ref[...].astype(F32)
    lower = jnp.where(me > 0, jnp.where(even, odd, pair), 0.0)
    upper = jnp.where(me < lax.axis_size("row") - 1, jnp.where(even, pair, odd), 0.0)
    both = own_ref[...] + jnp.concatenate([lower, upper], axis=0)
    count = both[:, model : model + 1] + both[:, model + 1 : model + 2]
    token_in = single_ref[...].astype(F32) + both[:, :model] / jnp.maximum(count, 1.0)
    in_ref[...] = token_in
    norm_ref[...] = normalize(token_in).astype(BF16)


def bias_body(after, bias_hbm, mask_hbm, bias_ref, mask_ref, sems):
    for copy in fetch(sems, (mask_hbm, mask_ref), *quarters(bias_hbm, bias_ref)):
        copy.wait()


def query_body(
    norm_ref,
    in_ref,
    wqkv_ref,
    wout_hbm,
    wback_hbm,
    query_ref,
    wout_ref,
    both_ref,
    base_ref,
    wback_ref,
    sems,
):
    copies = fetch(sems, (wback_hbm, wback_ref), *quarters(wout_hbm, wout_ref))

    @pl.when(lax.axis_index("row") >= 0)
    def _():
        rows, model = norm_ref.shape
        width = model // TH
        group = TH // 2
        span = group * width
        own = iota((group * rows, span), 0) // rows == iota((group * rows, span), 1) // width
        tq = dot(norm_ref[...], wqkv_ref[:, :model])
        for g in range(2):
            part = tq[:, g * span : (g + 1) * span]
            stacked = jnp.where(own, jnp.concatenate([part] * group, axis=0), 0.0).astype(BF16)
            wk = wqkv_ref[:, model + g * span : model + (g + 1) * span]
            query_ref[g * group * rows : (g + 1) * group * rows, :] = dot_nt(stacked, wk).astype(BF16)

    for copy in copies:
        copy.wait()
    both_ref[...] = dot(wout_ref[...], wback_ref[...]).astype(BF16)
    base_ref[...] = dot(in_ref[...].astype(BF16), wback_ref[...])


def stage_body(lists, after, norm_ref, bias_ref, mask_ref, wgate_hbm, out_ref, gate_ref, wgate_ref, sems):
    copies = fetch(sems, *quarters(wgate_hbm, wgate_ref))

    @pl.when(lax.axis_index("row") >= 0)
    def _():
        heads, rows, _ = bias_ref.shape
        if lists is None:
            allowed = mask_ref[...] == 1
            for h in range(heads):
                out_ref[0, h * rows : (h + 1) * rows, :] = jnp.where(allowed, bias_ref[h], masked_score)
        else:
            me = lax.axis_index("row")
            kind = kind_of(me)
            per = 128 // rows
            lane_block = iota((heads * rows, 128), 1) // rows
            for c in range(len(lists[0])):
                for tile in range(len(lists[0][c]) // per):
                    for j in range(per):
                        n = tile * per + j
                        block = me ^ jnp.where(kind == 0, lists[0][c][n], lists[1][c][n])
                        source = pl.ds(pl.multiple_of((block // per) * 128, 128), 128)
                        piece = jnp.where((mask_ref[:, source] == 1)[None], bias_ref[:, :, source], masked_score)
                        piece = piece.reshape(heads * rows, 128)
                        piece = pltpu.roll(piece, ((j + per - block % per) % per) * rows, 1)
                        merged = piece if j == 0 else jnp.where(lane_block == j, piece, merged)
                    out_ref[c, :, tile * 128 : (tile + 1) * 128] = merged

    for copy in copies:
        copy.wait()
    gate_ref[...] = jax.nn.sigmoid(dot(norm_ref[...], wgate_ref[...]))


def part_of(rows, query_ref, keys_ref, bias, wqkv_ref):
    model = query_ref.shape[1]
    width = model // TH
    group = TH // 2
    span = group * width
    keys = keys_ref[...]
    values = dot(keys, wqkv_ref[:, 2 * model :]).astype(BF16)
    lane_head = iota((rows, span), 1) // width

    def by_head(stacked):
        out = jnp.broadcast_to(stacked[:rows], (rows, span))
        for h in range(1, group):
            out = jnp.where(lane_head == h, stacked[h * rows : (h + 1) * rows], out)
        return out

    found = []
    for g in range(2):
        at = slice(g * group * rows, (g + 1) * group * rows)
        scores = dot_nt(query_ref[at, :], keys) * (1.0 / width**0.5) + bias(at)
        top = jnp.max(scores, axis=-1, keepdims=True)
        scores = jnp.exp(scores - top)
        total = jnp.sum(scores, axis=-1, keepdims=True)
        mixed = dot(scores.astype(BF16), values[:, g * span : (g + 1) * span])
        found.append((by_head(top), by_head(total), by_head(mixed)))
    return [jnp.concatenate([found[0][n], found[1][n]], axis=1) for n in range(3)]


def part_body(chunk, query_ref, keys_ref, bias_ref, wqkv_ref, part_ref):
    found = part_of(part_ref.shape[1], query_ref, keys_ref, lambda at: bias_ref[chunk, at, :], wqkv_ref)
    for n in range(3):
        part_ref[n] = found[n]


def attend_body(
    half,
    chunk,
    base_ref,
    query_ref,
    gate_ref,
    keys_ref,
    bias_ref,
    wqkv_ref,
    both_ref,
    *rest,
):
    parts, (gated_ref, back_ref, pair_out, odd_out) = rest[:-4], rest[-4:]
    rows, _ = gate_ref.shape
    even = lax.axis_index("row") % 2 == 0
    found = part_of(rows, query_ref, keys_ref, lambda at: bias_ref[chunk, at, :], wqkv_ref)
    found = [[part[n] for n in range(3)] for part in parts] + [found]
    top = functools.reduce(jnp.maximum, [f[0] for f in found])
    shares = [jnp.exp(f[0] - top) for f in found]
    total = sum(f[1] * w for f, w in zip(found, shares))
    mixed = sum(f[2] * w for f, w in zip(found, shares))
    gated = (gate_ref[...] * (mixed / total)).astype(BF16)
    gated_ref[...] = gated
    back = base_ref[...] + dot(gated, both_ref[...])
    back_ref[...] = back.astype(BF16)
    lower, upper = back[:half], back[rows - half :]
    pair_out[...] = jnp.where(even, upper, lower).astype(BF16)
    odd_out[...] = jnp.where(even, lower, upper).astype(BF16)


def out_body(in_ref, gated_ref, wout_ref, out_ref):
    out_ref[...] = (in_ref[...] + dot(gated_ref[...], wout_ref[...])).astype(BF16)


def final_body(living_ref, hot_ref, mid_ref, back_ref, pair_ref, odd_ref, wpos_ref, pos_ref, noise_ref, out_ref):
    even = lax.axis_index("row") % 2 == 0
    pair = pair_ref[...].astype(F32)
    odd = odd_ref[...].astype(F32)
    near = jnp.concatenate(
        [jnp.where(even, odd, pair), back_ref[...].astype(F32), jnp.where(even, pair, odd)], axis=0
    ).astype(BF16)
    last = mid_ref[...] + dot(hot_ref[...], near)
    update = dot_nt(wpos_ref[...], normalize(last).astype(BF16))
    noisy = pos_ref[...] + noise_level * noise_ref[...]
    out_ref[...] = jnp.where(living_ref[...] > 0.0, skip_scale * noisy + output_scale * update, 0.0)


def exchange(pair, odd, groups, count):
    near = [(i, i ^ 1) for i in range(count) if i ^ 1 < count]
    odds = [(i, i + 1) for i in range(1, count - 1, 2)]
    far = [(g * count + a, g * count + b) for g in range(groups) for a, b in odds + [(b, a) for a, b in odds]]
    if groups % 2 == 0 and count % 2 == 0:
        far += [(g * count + i, (g ^ 1) * count + i) for g in range(groups) for i in (0, count - 1)]
    odd = lax.ppermute(odd, ("grp", "row"), far)
    pair = lax.ppermute(pair, "row", near)
    return pair, odd


def kind_of(i):
    return (i ^ (i >> 1) ^ (i >> 2)) & 1


def gather_plan(count):
    bits = [1 << b for b in range(count.bit_length() - 1, 0, -1) if 1 << b < count]
    steps = [[b | 1, b | 1] for b in bits]
    high, low = bits[-2] | 1, bits[-1] | 1
    steps[-2:] = [[high, low], [low, high]]
    lists = [[0], [0]]
    for step in steps[:-1]:
        lists = [lists[p] + [x ^ step[p] for x in lists[p ^ kind_of(step[p])]] for p in range(2)]
    near = [[1 ^ x for x in lists[1 - p]] for p in range(2)]
    last = [[x ^ steps[-1][p] for x in lists[p]] for p in range(2)]
    end = [[1 ^ x for x in last[1 - p]] for p in range(2)]
    return steps, [[lists[p], near[p], last[p], end[p]] for p in range(2)]


def swap(value, count, step):
    return lax.ppermute(value, "row", [(i, i ^ step[kind_of(i)]) for i in range(count)])


def on_device(
    groups,
    count,
    positions,
    noise,
    atom_single,
    atom_token,
    atom_counts,
    window_offsets,
    atom_bias,
    token_single,
    token_bias,
    pair_mask,
    w_coord,
    w_atom_qkv,
    w_atom_out,
    w_agg,
    w_tok_qkv,
    w_tok_gate,
    w_tok_out,
    w_back,
    w_pos,
):
    rows, width = atom_single.shape
    block_rows, model = token_single.shape
    half = block_rows // 2
    info_shape = shape((8,), jnp.int32)
    info, start, normed, pair, odd, offsets, tokens, bias, wout, wagg, wqkv = call(
        embed_body,
        [
            info_shape,
            shape((rows, width), F32),
            shape((rows, width), BF16),
            shape((AHEAD, width), BF16),
            shape((AHEAD, width), BF16),
            shape((1, rows // QWIN), jnp.int32),
            shape((1, rows), jnp.int32),
            shape(atom_bias.shape, F32),
            shape(w_atom_out.shape, BF16),
            shape(w_agg.shape, BF16),
            shape(w_atom_qkv.shape, BF16),
        ],
        [HBM] * 11,
        [
            pltpu.SMEM((1, 1), jnp.int32),
            pltpu.VMEM(positions.shape, F32),
            pltpu.VMEM(noise.shape, F32),
            pltpu.VMEM(atom_single.shape, BF16),
            pltpu.VMEM(w_coord.shape, F32),
            pltpu.VMEM((rows + AHEAD, width), F32),
            pltpu.SemaphoreType.DMA((14,)),
        ],
        out_specs=[SMEM] + [VMEM] * 4 + [SMEM] + [VMEM] * 5,
    )(
        atom_counts[None],
        positions,
        noise,
        atom_single,
        w_coord,
        w_atom_qkv,
        window_offsets[None],
        atom_token,
        atom_bias,
        w_atom_out,
        w_agg,
    )
    pair, odd = exchange(pair, odd, groups, count)
    q, keys, values, att = call(
        local_body,
        [
            shape((rows, width), BF16),
            shape((rows + AHEAD, width), F32),
            shape((rows + AHEAD, width), F32),
            shape((rows, width), BF16),
        ],
        [SMEM] + [VMEM] * 3,
        flops=10**9,
    )(offsets, normed, wqkv, bias)
    packed = model + 128
    mid, own, pair, odd, hot, living = call(
        functools.partial(atoms_body, half),
        [
            shape((rows, width), F32),
            shape((block_rows, packed), F32),
            shape((half, packed), BF16),
            shape((half, packed), BF16),
            shape((rows, block_rows + 2 * half), BF16),
            shape((1, rows), F32),
        ],
        [SMEM, SMEM] + [VMEM] * 12,
        [pltpu.VMEM((BEHIND + rows + AHEAD, width), F32)] * 2 + [pltpu.VMEM((rows, width), BF16)],
    )(info, offsets, tokens, start, q, keys, values, pair, odd, att, bias, wout, wagg, wqkv)
    pair, odd = exchange(pair, odd, groups, count)
    raw, mask = call(
        bias_body,
        [shape(token_bias.shape, F32), shape(pair_mask.shape, jnp.int32)],
        [VMEM, HBM, HBM],
        [pltpu.SemaphoreType.DMA((5,))],
        flops=10**9,
    )(own, token_bias, pair_mask)
    odd, raw, mask = lax.optimization_barrier((odd, raw, mask))
    token_in, norm = call(
        token_body, [shape((block_rows, model), F32), shape((block_rows, model), BF16)], [VMEM] * 4
    )(own, pair, odd, token_single)

    doubling = count & (count - 1) == 0 and count >= 16 and 128 % block_rows == 0
    steps, lists = gather_plan(count) if doubling else ([], None)
    chunks = 4 if doubling else 1
    span = count * block_rows // chunks

    def query(seen):
        return call(
            query_body,
            [
                shape((TH * block_rows, model), BF16),
                shape(w_tok_out.shape, BF16),
                shape(w_back.shape, BF16),
                shape((block_rows, width), F32),
            ],
            [VMEM] * 3 + [HBM] * 2,
            [pltpu.VMEM(w_back.shape, BF16), pltpu.SemaphoreType.DMA((5,))],
            flops=10**9,
        )(seen, token_in, w_tok_qkv, w_tok_out, w_back)

    def stage(seen):
        return call(
            functools.partial(stage_body, lists),
            [shape((chunks, TH * block_rows, span), F32), shape((block_rows, model), F32)],
            [VMEM] * 4 + [HBM],
            [pltpu.VMEM(w_tok_gate.shape, BF16), pltpu.SemaphoreType.DMA((4,))],
            flops=10**9,
        )(seen, norm, raw, mask, w_tok_gate)

    def part(chunk, seen):
        return call(
            functools.partial(part_body, chunk),
            [shape((3, block_rows, model), F32)],
            [VMEM] * 4,
            flops=10**9,
        )(query_rows, seen, score_bias, w_tok_qkv)[0]

    if doubling:
        held = norm
        for n, step in enumerate(steps[:-1]):
            arrived = swap(held, count, step)
            if n == 0:
                arrived, (query_rows, wout, both, base) = lax.optimization_barrier((arrived, query(norm)))
            if n == 1:
                arrived, (score_bias, gate) = lax.optimization_barrier((arrived, stage(held)))
            held = jnp.concatenate([held, arrived], axis=0)
        last = swap(held, count, steps[-1])
        near = swap(held, count, [1, 1])
        parts = [part(0, held), part(1, near)]
        last, parts = lax.optimization_barrier((last, parts))
        end = swap(last, count, [1, 1])
        parts = parts + [part(2, last)]
    else:
        end = lax.all_gather(norm, "row", axis=0, tiled=True)
        query_rows, wout, both, base = query(norm)
        score_bias, gate = stage(norm)
        parts = []
    gated, back, pair, odd = call(
        functools.partial(attend_body, half, chunks - 1),
        [
            shape((block_rows, model), BF16),
            shape((block_rows, width), BF16),
            shape((half, width), BF16),
            shape((half, width), BF16),
        ],
        [VMEM] * (7 + len(parts)),
    )(base, query_rows, gate, end, score_bias, w_tok_qkv, both, *parts)
    pair, odd = exchange(pair, odd, groups, count)
    (token_out,) = call(
        out_body, [shape((block_rows, model), BF16)], [VMEM] * 3, flops=10**9
    )(token_in, gated, wout)
    odd, token_out = lax.optimization_barrier((odd, token_out))
    (denoised,) = call(
        final_body, [shape(positions.shape, F32)], [VMEM] * 9
    )(living, hot, mid, back, pair, odd, w_pos, positions, noise)
    return (denoised, token_out)


def solution(mesh):
    placed = (
        P(None, ("grp", "row")),
        P(None, ("grp", "row")),
        P(("grp", "row"), None),
        P(("grp", "row")),
        P(("grp", "row")),
        P(("grp", "row")),
        P(None, ("grp", "row"), None),
        P(("grp", "row"), None),
        P(None, ("grp", "row"), None),
        P(("grp", "row"), None),
    ) + (P(),) * 9
    return jax.shard_map(
        functools.partial(on_device, mesh.shape["grp"], mesh.shape["row"]),
        mesh=mesh,
        in_specs=placed,
        out_specs=(P(None, ("grp", "row")), P(("grp", "row"), None)),
        check_vma=False,
    )
```

```python
import functools

import jax
import jax.numpy as jnp
from jax import lax
from jax.experimental import pallas as pl
from jax.experimental.pallas import tpu as pltpu
from jax.sharding import PartitionSpec as P

AH = 4
TH = 16
QWIN = 32
KWIN = 128
BEHIND = KWIN // 2
AHEAD = KWIN - QWIN

noise_level = 2.0
input_scale = 1.0 / 5.0**0.5
skip_scale = 1.0 / 5.0
output_scale = 2.0 / 5.0**0.5
masked_score = -1e30

F32 = jnp.float32
BF16 = jnp.bfloat16
NT = (((1,), (1,)), ((), ()))


def dot(a, b):
    return jnp.dot(a, b, preferred_element_type=F32)


def dot_nt(a, b):
    return lax.dot_general(a, b, NT, preferred_element_type=F32)


def normalize(values):
    center = values - jnp.mean(values, axis=-1, keepdims=True)
    spread = jnp.mean(center * center, axis=-1, keepdims=True)
    return center * lax.rsqrt(spread + 1e-05)


def iota(shape, dim):
    return lax.broadcasted_iota(jnp.int32, shape, dim)


VMEM = pl.BlockSpec(memory_space=pltpu.VMEM)
SMEM = pl.BlockSpec(memory_space=pltpu.SMEM)
HBM = pl.BlockSpec(memory_space=pltpu.HBM)


def call(body, outs, specs, scratch=(), flops=10**7, limit=8, out_specs=None):
    moved = sum(o.size * o.dtype.itemsize for o in outs)
    held = [spec is HBM for spec in specs]
    run = pl.pallas_call(
        body,
        out_shape=tuple(outs),
        in_specs=specs,
        out_specs=tuple(out_specs or [VMEM] * len(outs)),
        scratch_shapes=list(scratch),
        cost_estimate=pl.CostEstimate(flops=flops, bytes_accessed=moved, transcendentals=0),
        compiler_params=pltpu.CompilerParams(vmem_limit_bytes=limit * 2**20),
    )
    return lambda *args: run(*[pltpu.with_memory_space_constraint(x, pltpu.HBM) if h and x.size > 1 else x for x, h in zip(args, held)])


def shape(dims, dtype):
    return jax.ShapeDtypeStruct(dims, dtype)


def fetch(sems, *moves):
    copies = [pltpu.make_async_copy(src, dst, sems.at[n]) for n, (src, dst) in enumerate(moves)]
    for copy in copies:
        copy.start()
    return copies


def quarters(src, dst):
    step = src.shape[0] // 4
    return [(src.at[pl.ds(n * step, step)], dst.at[pl.ds(n * step, step)]) for n in range(4)]


def embed_body(
    counts_hbm,
    pos_hbm,
    noise_hbm,
    single_hbm,
    wc_hbm,
    wqkv_hbm,
    offsets_hbm,
    token_hbm,
    bias_hbm,
    wout_hbm,
    wagg_hbm,
    info_ref,
    start_ref,
    normed_ref,
    pair_ref,
    odd_ref,
    offsets_ref,
    token_ref,
    bias_ref,
    wout_ref,
    wagg_ref,
    wqkv_ref,
    counts_ref,
    pos_ref,
    noise_ref,
    single_ref,
    wc_ref,
    wide_ref,
    sems,
):
    copies = fetch(
        sems,
        (pos_hbm, pos_ref),
        (noise_hbm, noise_ref),
        (wc_hbm, wc_ref),
        (single_hbm, single_ref),
        (counts_hbm, counts_ref),
        (wqkv_hbm, wqkv_ref),
        (offsets_hbm, offsets_ref),
        (token_hbm, token_ref.at[0]),
        *quarters(bias_hbm, bias_ref),
        (wout_hbm, wout_ref),
        (wagg_hbm, wagg_ref),
    )
    rows, width = single_ref.shape
    wide_ref[rows:, :] = jnp.zeros((AHEAD, width), F32)
    for copy in copies[:3]:
        copy.wait()
    scaled = input_scale * (pos_ref[...] + noise_level * noise_ref[...])
    padded = jnp.concatenate([scaled, jnp.zeros((5, rows), F32)], axis=0)
    across = jnp.transpose(padded)
    copies[3].wait()
    start = single_ref[...].astype(F32)
    for c in range(3):
        start = start + across[:, c : c + 1] * wc_ref[c : c + 1, :]
    start_ref[...] = start
    normed = normalize(start)
    normed_ref[...] = normed.astype(BF16)
    wide_ref[:rows, :] = normed
    copies[4].wait()
    live = counts_ref[0, 0]
    me = lax.axis_index("row")
    info_ref[0] = live
    info_ref[1] = me
    info_ref[2] = lax.axis_size("row") - 1
    tail = live - BEHIND
    even = me % 2 == 0
    pair_ref[...] = wide_ref[pl.ds(jnp.where(even, tail, 0), AHEAD), :].astype(BF16)
    odd_ref[...] = wide_ref[pl.ds(jnp.where(even, 0, tail), AHEAD), :].astype(BF16)
    for copy in copies[5:]:
        copy.wait()


def windows_of(queries, keys, values, biases, masks):
    width = queries[0].shape[1]
    depth = width // AH
    rows = AH * QWIN
    own_head = iota((rows, width), 0) // QWIN == iota((rows, width), 1) // depth
    lane_head = iota((QWIN, width), 1) // depth
    stacked = [jnp.where(own_head, jnp.concatenate([q] * AH, axis=0), 0.0).astype(BF16) for q in queries]
    scores = [dot_nt(q, k) * (1.0 / depth**0.5) + b for q, k, b in zip(stacked, keys, biases)]
    if masks is not None:
        scores = [jnp.where(m, s, masked_score) for m, s in zip(masks, scores)]
    tops = [jnp.max(s, axis=-1, keepdims=True) for s in scores]
    scores = [jnp.exp(s - t) for s, t in zip(scores, tops)]
    shares = [1.0 / jnp.sum(s, axis=-1, keepdims=True) for s in scores]
    weights = [(s * r).astype(BF16) for s, r in zip(scores, shares)]
    mixed = [dot(w, v) for w, v in zip(weights, values)]
    outs = []
    for mix in mixed:
        out = mix[:QWIN]
        for h in range(1, AH):
            out = jnp.where(lane_head == h, mix[h * QWIN : (h + 1) * QWIN], out)
        outs.append(out.astype(BF16))
    return outs


def local_body(offsets, normed_ref, wqkv_ref, bias_ref, q_ref, k_ref, v_ref, att_ref):
    rows, width = normed_ref.shape
    qkv = dot(normed_ref[...], wqkv_ref[...]).astype(BF16)
    q_ref[...] = qkv[:, :width]
    for n, ref in enumerate((k_ref, v_ref)):
        ref[:rows, :] = qkv[:, (n + 1) * width : (n + 2) * width].astype(F32)
        ref[rows:, :] = jnp.zeros((AHEAD, width), F32)
    windows = rows // QWIN
    skip = BEHIND // QWIN
    stop = windows - (AHEAD - QWIN) // QWIN
    for part in (slice(0, skip * QWIN), slice(stop * QWIN, rows)):
        att_ref[part, :] = jnp.zeros((part.stop - part.start, width), BF16)
    at = [slice(m * QWIN, (m + 1) * QWIN) for m in range(skip, stop)]
    base = [m * QWIN + offsets[0, m] for m in range(skip, stop)]
    outs = windows_of(
        [q_ref[a, :].astype(F32) for a in at],
        [k_ref[pl.ds(b, KWIN), :].astype(BF16) for b in base],
        [v_ref[pl.ds(b, KWIN), :].astype(BF16) for b in base],
        [bias_ref[:, a, :].reshape(AH * QWIN, KWIN) for a in at],
        None,
    )
    for a, out in zip(at, outs):
        att_ref[a, :] = out


def atoms_body(
    half,
    info,
    offsets,
    token_ref,
    start_ref,
    q_ref,
    k_ref,
    v_ref,
    pair_ref,
    odd_ref,
    att_ref,
    bias_ref,
    wout_ref,
    wagg_ref,
    wqkv_ref,
    mid_ref,
    own_ref,
    pair_out,
    odd_out,
    hot_ref,
    living_ref,
    k_ext,
    v_ext,
    att,
):
    rows, width = start_ref.shape
    live, me, last = info[0], info[1], info[2]
    even = me % 2 == 0
    pair = dot(pair_ref[...], wqkv_ref[:, width:]).astype(BF16).astype(F32)
    odd = dot(odd_ref[...], wqkv_ref[:, width:]).astype(BF16).astype(F32)
    for n, (ref, ext) in enumerate(((k_ref, k_ext), (v_ref, v_ext))):
        at = slice(n * width, (n + 1) * width)
        ext[:BEHIND, :] = jnp.where(even, odd[:BEHIND, at], pair[:BEHIND, at])
        ext[BEHIND : BEHIND + rows + AHEAD, :] = ref[...]
        ext[pl.ds(BEHIND + live, AHEAD), :] = jnp.where(even, pair[:, at], odd[:, at])
    low = jnp.where(me > 0, 0, BEHIND)
    high = BEHIND + live + jnp.where(me < last, AHEAD, 0)
    att[...] = att_ref[...]
    windows = rows // QWIN
    tails = AHEAD // QWIN
    first = jnp.minimum((live - BEHIND) // QWIN, windows - tails)
    chosen = list(range(BEHIND // QWIN)) + [first + n for n in range(tails)]
    at = [pl.ds(pl.multiple_of(m * QWIN, QWIN), QWIN) for m in chosen]
    base = [BEHIND + QWIN * m + offsets[0, m] for m in chosen]
    slots = [b + iota((1, KWIN), 1) for b in base]
    outs = windows_of(
        [q_ref[a, :].astype(F32) for a in at],
        [k_ext[pl.ds(b, KWIN), :].astype(BF16) for b in base],
        [v_ext[pl.ds(b, KWIN), :].astype(BF16) for b in base],
        [bias_ref[:, a, :].reshape(AH * QWIN, KWIN) for a in at],
        [(s >= low) & (s < high) for s in slots],
    )
    for a, out in zip(at, outs):
        att[a, :] = out
    mid = start_ref[...] + dot(att[...], wout_ref[...])
    mid_ref[...] = mid
    spread = jnp.maximum(dot(mid.astype(BF16), wagg_ref[...]), 0.0).astype(BF16)
    block_rows = own_ref.shape[0]
    living = iota((1, rows), 1) < live
    living_ref[...] = living.astype(F32)
    relative = token_ref[...] - (me * block_rows - half)
    hot = ((iota((block_rows + 2 * half, rows), 0) == relative) & living).astype(F32)
    hot_ref[...] = jnp.transpose(hot).astype(BF16)
    sums = dot(hot.astype(BF16), spread)
    counts = jnp.sum(hot, axis=1, keepdims=True)
    first = jnp.minimum(counts, 256.0)
    lane = iota((counts.shape[0], 128), 1)
    packed = jnp.where(lane == 0, first, jnp.where(lane == 1, counts - first, 0.0))
    model = wagg_ref.shape[1]
    own_ref[:, :model] = sums[half : half + block_rows]
    own_ref[:, model:] = packed[half : half + block_rows]
    lower = jnp.concatenate([sums[:half], packed[:half]], axis=1)
    upper = jnp.concatenate([sums[half + block_rows :], packed[half + block_rows :]], axis=1)
    pair_out[...] = jnp.where(even, upper, lower).astype(BF16)
    odd_out[...] = jnp.where(even, lower, upper).astype(BF16)


def token_body(own_ref, pair_ref, odd_ref, single_ref, in_ref, norm_ref):
    me = lax.axis_index("row")
    even = me % 2 == 0
    model = single_ref.shape[1]
    pair = pair_ref[...].astype(F32)
    odd = odd_ref[...].astype(F32)
    lower = jnp.where(me > 0, jnp.where(even, odd, pair), 0.0)
    upper = jnp.where(me < lax.axis_size("row") - 1, jnp.where(even, pair, odd), 0.0)
    both = own_ref[...] + jnp.concatenate([lower, upper], axis=0)
    count = both[:, model : model + 1] + both[:, model + 1 : model + 2]
    token_in = single_ref[...].astype(F32) + both[:, :model] / jnp.maximum(count, 1.0)
    in_ref[...] = token_in
    norm_ref[...] = normalize(token_in).astype(BF16)


def bias_body(after, bias_hbm, mask_hbm, bias_ref, mask_ref, sems):
    for copy in fetch(sems, (mask_hbm, mask_ref), *quarters(bias_hbm, bias_ref)):
        copy.wait()


def query_body(
    norm_ref,
    in_ref,
    wqkv_ref,
    wout_hbm,
    wback_hbm,
    query_ref,
    wout_ref,
    both_ref,
    base_ref,
    wback_ref,
    sems,
):
    copies = fetch(sems, (wback_hbm, wback_ref), *quarters(wout_hbm, wout_ref))

    @pl.when(lax.axis_index("row") >= 0)
    def _():
        rows, model = norm_ref.shape
        width = model // TH
        group = TH // 2
        span = group * width
        own = iota((group * rows, span), 0) // rows == iota((group * rows, span), 1) // width
        tq = dot(norm_ref[...], wqkv_ref[:, :model])
        for g in range(2):
            part = tq[:, g * span : (g + 1) * span]
            stacked = jnp.where(own, jnp.concatenate([part] * group, axis=0), 0.0).astype(BF16)
            wk = wqkv_ref[:, model + g * span : model + (g + 1) * span]
            query_ref[g * group * rows : (g + 1) * group * rows, :] = dot_nt(stacked, wk).astype(BF16)

    for copy in copies:
        copy.wait()
    both_ref[...] = dot(wout_ref[...], wback_ref[...]).astype(BF16)
    base_ref[...] = dot(in_ref[...].astype(BF16), wback_ref[...])


def stage_body(lists, after, norm_ref, bias_ref, mask_ref, wgate_hbm, out_ref, gate_ref, wgate_ref, sems):
    copies = fetch(sems, *quarters(wgate_hbm, wgate_ref))

    @pl.when(lax.axis_index("row") >= 0)
    def _():
        heads, rows, _ = bias_ref.shape
        if lists is None:
            allowed = mask_ref[...] == 1
            for h in range(heads):
                out_ref[0, h * rows : (h + 1) * rows, :] = jnp.where(allowed, bias_ref[h], masked_score)
        else:
            me = lax.axis_index("row")
            kind = kind_of(me)
            per = 128 // rows
            lane_block = iota((heads * rows, 128), 1) // rows
            for c in range(len(lists[0])):
                for tile in range(len(lists[0][c]) // per):
                    for j in range(per):
                        n = tile * per + j
                        block = me ^ jnp.where(kind == 0, lists[0][c][n], lists[1][c][n])
                        source = pl.ds(pl.multiple_of((block // per) * 128, 128), 128)
                        piece = jnp.where((mask_ref[:, source] == 1)[None], bias_ref[:, :, source], masked_score)
                        piece = piece.reshape(heads * rows, 128)
                        piece = pltpu.roll(piece, ((j + per - block % per) % per) * rows, 1)
                        merged = piece if j == 0 else jnp.where(lane_block == j, piece, merged)
                    out_ref[c, :, tile * 128 : (tile + 1) * 128] = merged

    for copy in copies:
        copy.wait()
    gate_ref[...] = jax.nn.sigmoid(dot(norm_ref[...], wgate_ref[...]))


def part_of(rows, query_ref, keys_ref, bias, wqkv_ref):
    model = query_ref.shape[1]
    width = model // TH
    group = TH // 2
    span = group * width
    keys = keys_ref[...]
    values = dot(keys, wqkv_ref[:, 2 * model :]).astype(BF16)
    lane_head = iota((rows, span), 1) // width

    def by_head(stacked):
        out = jnp.broadcast_to(stacked[:rows], (rows, span))
        for h in range(1, group):
            out = jnp.where(lane_head == h, stacked[h * rows : (h + 1) * rows], out)
        return out

    found = []
    for g in range(2):
        at = slice(g * group * rows, (g + 1) * group * rows)
        scores = dot_nt(query_ref[at, :], keys) * (1.0 / width**0.5) + bias(at)
        top = jnp.max(scores, axis=-1, keepdims=True)
        scores = jnp.exp(scores - top)
        total = jnp.sum(scores, axis=-1, keepdims=True)
        mixed = dot(scores.astype(BF16), values[:, g * span : (g + 1) * span])
        found.append((by_head(top), by_head(total), by_head(mixed)))
    return [jnp.concatenate([found[0][n], found[1][n]], axis=1) for n in range(3)]


def part_body(chunk, query_ref, keys_ref, bias_ref, wqkv_ref, part_ref):
    found = part_of(part_ref.shape[1], query_ref, keys_ref, lambda at: bias_ref[chunk, at, :], wqkv_ref)
    for n in range(3):
        part_ref[n] = found[n]


def attend_body(
    half,
    chunk,
    base_ref,
    query_ref,
    gate_ref,
    keys_ref,
    bias_ref,
    wqkv_ref,
    both_ref,
    *rest,
):
    parts, (gated_ref, back_ref, pair_out, odd_out) = rest[:-4], rest[-4:]
    rows, _ = gate_ref.shape
    even = lax.axis_index("row") % 2 == 0
    found = part_of(rows, query_ref, keys_ref, lambda at: bias_ref[chunk, at, :], wqkv_ref)
    found = [[part[n] for n in range(3)] for part in parts] + [found]
    top = functools.reduce(jnp.maximum, [f[0] for f in found])
    shares = [jnp.exp(f[0] - top) for f in found]
    total = sum(f[1] * w for f, w in zip(found, shares))
    mixed = sum(f[2] * w for f, w in zip(found, shares))
    gated = (gate_ref[...] * (mixed / total)).astype(BF16)
    gated_ref[...] = gated
    back = base_ref[...] + dot(gated, both_ref[...])
    back_ref[...] = back.astype(BF16)
    lower, upper = back[:half], back[rows - half :]
    pair_out[...] = jnp.where(even, upper, lower).astype(BF16)
    odd_out[...] = jnp.where(even, lower, upper).astype(BF16)


def out_body(in_ref, gated_ref, wout_ref, out_ref):
    out_ref[...] = (in_ref[...] + dot(gated_ref[...], wout_ref[...])).astype(BF16)


def final_body(living_ref, hot_ref, mid_ref, back_ref, pair_ref, odd_ref, wpos_ref, pos_ref, noise_ref, out_ref):
    even = lax.axis_index("row") % 2 == 0
    pair = pair_ref[...].astype(F32)
    odd = odd_ref[...].astype(F32)
    near = jnp.concatenate(
        [jnp.where(even, odd, pair), back_ref[...].astype(F32), jnp.where(even, pair, odd)], axis=0
    ).astype(BF16)
    last = mid_ref[...] + dot(hot_ref[...], near)
    update = dot_nt(wpos_ref[...], normalize(last).astype(BF16))
    noisy = pos_ref[...] + noise_level * noise_ref[...]
    out_ref[...] = jnp.where(living_ref[...] > 0.0, skip_scale * noisy + output_scale * update, 0.0)


def exchange(pair, odd, groups, count):
    near = [(i, i ^ 1) for i in range(count) if i ^ 1 < count]
    odds = [(i, i + 1) for i in range(1, count - 1, 2)]
    far = [(g * count + a, g * count + b) for g in range(groups) for a, b in odds + [(b, a) for a, b in odds]]
    if groups % 2 == 0 and count % 2 == 0:
        far += [(g * count + i, (g ^ 1) * count + i) for g in range(groups) for i in (0, count - 1)]
    odd = lax.ppermute(odd, ("grp", "row"), far)
    pair = lax.ppermute(pair, "row", near)
    return pair, odd


def kind_of(i):
    for shift in (16, 8, 4, 2, 1):
        i = i ^ (i >> shift)
    return i & 1


def gather_plan(count):
    bits = [1 << b for b in range(count.bit_length() - 1, 0, -1) if 1 << b < count]
    steps = [[b | 1, b | 1] for b in bits]
    top, high, low = (b | 1 for b in bits[-3:])
    steps[-3:] = [[high, top], [top, low], [low, high]]
    lists = [[0], [0]]
    for step in steps[:-1]:
        lists = [lists[p] + [x ^ step[p] for x in lists[p ^ kind_of(step[p])]] for p in range(2)]
    near = [[1 ^ x for x in lists[1 - p]] for p in range(2)]
    last = [[x ^ steps[-1][p] for x in lists[p]] for p in range(2)]
    end = [[1 ^ x for x in last[1 - p]] for p in range(2)]
    return steps, [[lists[p], near[p], last[p], end[p]] for p in range(2)]


def swap(value, count, step):
    return lax.ppermute(value, "row", [(i, i ^ step[kind_of(i)]) for i in range(count)])


def on_device(
    groups,
    count,
    positions,
    noise,
    atom_single,
    atom_token,
    atom_counts,
    window_offsets,
    atom_bias,
    token_single,
    token_bias,
    pair_mask,
    w_coord,
    w_atom_qkv,
    w_atom_out,
    w_agg,
    w_tok_qkv,
    w_tok_gate,
    w_tok_out,
    w_back,
    w_pos,
):
    rows, width = atom_single.shape
    block_rows, model = token_single.shape
    half = block_rows // 2
    info_shape = shape((8,), jnp.int32)
    info, start, normed, pair, odd, offsets, tokens, bias, wout, wagg, wqkv = call(
        embed_body,
        [
            info_shape,
            shape((rows, width), F32),
            shape((rows, width), BF16),
            shape((AHEAD, width), BF16),
            shape((AHEAD, width), BF16),
            shape((1, rows // QWIN), jnp.int32),
            shape((1, rows), jnp.int32),
            shape(atom_bias.shape, F32),
            shape(w_atom_out.shape, BF16),
            shape(w_agg.shape, BF16),
            shape(w_atom_qkv.shape, BF16),
        ],
        [HBM] * 11,
        [
            pltpu.SMEM((1, 1), jnp.int32),
            pltpu.VMEM(positions.shape, F32),
            pltpu.VMEM(noise.shape, F32),
            pltpu.VMEM(atom_single.shape, BF16),
            pltpu.VMEM(w_coord.shape, F32),
            pltpu.VMEM((rows + AHEAD, width), F32),
            pltpu.SemaphoreType.DMA((14,)),
        ],
        out_specs=[SMEM] + [VMEM] * 4 + [SMEM] + [VMEM] * 5,
    )(
        atom_counts[None],
        positions,
        noise,
        atom_single,
        w_coord,
        w_atom_qkv,
        window_offsets[None],
        atom_token,
        atom_bias,
        w_atom_out,
        w_agg,
    )
    pair, odd = exchange(pair, odd, groups, count)
    q, keys, values, att = call(
        local_body,
        [
            shape((rows, width), BF16),
            shape((rows + AHEAD, width), F32),
            shape((rows + AHEAD, width), F32),
            shape((rows, width), BF16),
        ],
        [SMEM] + [VMEM] * 3,
        flops=10**9,
    )(offsets, normed, wqkv, bias)
    packed = model + 128
    mid, own, pair, odd, hot, living = call(
        functools.partial(atoms_body, half),
        [
            shape((rows, width), F32),
            shape((block_rows, packed), F32),
            shape((half, packed), BF16),
            shape((half, packed), BF16),
            shape((rows, block_rows + 2 * half), BF16),
            shape((1, rows), F32),
        ],
        [SMEM, SMEM] + [VMEM] * 12,
        [pltpu.VMEM((BEHIND + rows + AHEAD, width), F32)] * 2 + [pltpu.VMEM((rows, width), BF16)],
    )(info, offsets, tokens, start, q, keys, values, pair, odd, att, bias, wout, wagg, wqkv)
    pair, odd = exchange(pair, odd, groups, count)
    raw, mask = call(
        bias_body,
        [shape(token_bias.shape, F32), shape(pair_mask.shape, jnp.int32)],
        [VMEM, HBM, HBM],
        [pltpu.SemaphoreType.DMA((5,))],
        flops=10**9,
    )(own, token_bias, pair_mask)
    odd, raw, mask = lax.optimization_barrier((odd, raw, mask))
    token_in, norm = call(
        token_body, [shape((block_rows, model), F32), shape((block_rows, model), BF16)], [VMEM] * 4
    )(own, pair, odd, token_single)

    doubling = count & (count - 1) == 0 and count >= 16 and 128 % block_rows == 0
    steps, lists = gather_plan(count) if doubling else ([], None)
    chunks = 4 if doubling else 1
    span = count * block_rows // chunks

    def query(seen):
        return call(
            query_body,
            [
                shape((TH * block_rows, model), BF16),
                shape(w_tok_out.shape, BF16),
                shape(w_back.shape, BF16),
                shape((block_rows, width), F32),
            ],
            [VMEM] * 3 + [HBM] * 2,
            [pltpu.VMEM(w_back.shape, BF16), pltpu.SemaphoreType.DMA((5,))],
            flops=10**9,
        )(seen, token_in, w_tok_qkv, w_tok_out, w_back)

    def stage(seen):
        return call(
            functools.partial(stage_body, lists),
            [shape((chunks, TH * block_rows, span), F32), shape((block_rows, model), F32)],
            [VMEM] * 4 + [HBM],
            [pltpu.VMEM(w_tok_gate.shape, BF16), pltpu.SemaphoreType.DMA((4,))],
            flops=10**9,
        )(seen, norm, raw, mask, w_tok_gate)

    def part(chunk, seen):
        return call(
            functools.partial(part_body, chunk),
            [shape((3, block_rows, model), F32)],
            [VMEM] * 4,
            flops=10**9,
        )(query_rows, seen, score_bias, w_tok_qkv)[0]

    if doubling:
        held = norm
        for n, step in enumerate(steps[:-1]):
            arrived = swap(held, count, step)
            if n == 0:
                arrived, (query_rows, wout, both, base) = lax.optimization_barrier((arrived, query(norm)))
            if n == 1:
                arrived, (score_bias, gate) = lax.optimization_barrier((arrived, stage(held)))
            held = jnp.concatenate([held, arrived], axis=0)
        last = swap(held, count, steps[-1])
        near = swap(held, count, [1, 1])
        parts = [part(0, held), part(1, near)]
        last, parts = lax.optimization_barrier((last, parts))
        end = swap(last, count, [1, 1])
        parts = parts + [part(2, last)]
    else:
        end = lax.all_gather(norm, "row", axis=0, tiled=True)
        query_rows, wout, both, base = query(norm)
        score_bias, gate = stage(norm)
        parts = []
    gated, back, pair, odd = call(
        functools.partial(attend_body, half, chunks - 1),
        [
            shape((block_rows, model), BF16),
            shape((block_rows, width), BF16),
            shape((half, width), BF16),
            shape((half, width), BF16),
        ],
        [VMEM] * (7 + len(parts)),
    )(base, query_rows, gate, end, score_bias, w_tok_qkv, both, *parts)
    pair, odd = exchange(pair, odd, groups, count)
    (token_out,) = call(
        out_body, [shape((block_rows, model), BF16)], [VMEM] * 3, flops=10**9
    )(token_in, gated, wout)
    odd, token_out = lax.optimization_barrier((odd, token_out))
    (denoised,) = call(
        final_body, [shape(positions.shape, F32)], [VMEM] * 9
    )(living, hot, mid, back, pair, odd, w_pos, positions, noise)
    return (denoised, token_out)


def solution(mesh):
    placed = (
        P(None, ("grp", "row")),
        P(None, ("grp", "row")),
        P(("grp", "row"), None),
        P(("grp", "row")),
        P(("grp", "row")),
        P(("grp", "row")),
        P(None, ("grp", "row"), None),
        P(("grp", "row"), None),
        P(None, ("grp", "row"), None),
        P(("grp", "row"), None),
    ) + (P(),) * 9
    return jax.shard_map(
        functools.partial(on_device, mesh.shape["grp"], mesh.shape["row"]),
        mesh=mesh,
        in_specs=placed,
        out_specs=(P(None, ("grp", "row")), P(("grp", "row"), None)),
        check_vma=False,
    )
```
